128 devices in a mesh: gy: 16 (over x_lo, z, core), gx: 8 (over x_hi, y).
Axes of the slice: x: 4 (x_hi: 2, x_lo: 2; x = x_hi * 2 + x_lo), y: 4, z: 4, core: 2. Of those that a mesh axis runs over, the one named last changes fastest.
Arguments:
- e_field: float32 [3, 4, 1024, 1024], P(None, None, 'gy', 'gx'), may hold values from -6 to 6
- h_field: float32 [3, 4, 1024, 1024], P(None, None, 'gy', 'gx'), may hold values from -6 to 6
- j_field: float32 [3, 4, 1024, 1024], P(None, None, 'gy', 'gx'), may hold values from -3 to 3
- material: int32 [4, 1024, 1024], P(None, 'gy', 'gx'), may hold values from 0 to 31
- material_table: float32 [4, 32], replicated, may hold values from 0.05 to 1
- dft_e: float32 [3, 2, 3, 4, 1024, 1024], P(None, None, None, None, 'gy', 'gx'), may hold values from -5 to 7
- dft_h: float32 [3, 2, 3, 4, 1024, 1024], P(None, None, None, None, 'gy', 'gx'), may hold values from -5 to 7
- skin_cell: int32 [128, 128, 128], P(('gy', 'gx')), may hold values from 0 to 32767, as said below
- counts: int32 [128, 128], P(('gy', 'gx')), may hold values from 0 to 128, as said below
- patch_slot: int32 [128, 128, 128], P(('gy', 'gx')), may hold values from 0 to 65535
- area: float32 [3, 4096, 2048], P(None, 'gy', 'gx'), may hold values from -0.5 to 1.5
Outputs:
- e_next: float32 [3, 4, 1024, 1024], P(None, None, 'gy', 'gx')
- j_next: float32 [3, 4, 1024, 1024], P(None, None, 'gy', 'gx')
- dft_e_next: float32 [3, 2, 3, 4, 1024, 1024], P(None, None, None, None, 'gy', 'gx')
- dft_h_next: float32 [3, 2, 3, 4, 1024, 1024], P(None, None, None, None, 'gy', 'gx')
- point_density: float32 [3, 4096, 2048], P(None, 'gy', 'gx')
- avg_density: float32 [3, 4096, 2048], P(None, 'gy', 'gx')
The draws below stay inside these ranges and needn't reach their ends.
Inputs may be any that keep to these rules, and one draw needn't show every extreme that they name: Within one source block s the entries skin_cell[s, :, :] are distinct. Some owner block d has counts[s, d] = 128 for every source block s.
All inputs are finite; a program needn't handle non-finite values.
Results may differ from the reference program's by a relative error of at most 0.0003.
Values sent between devices are 32-bit elements; how exact they have to be, the bound alone decides.
No kernel may reach another device: no remote copies, remote signals or barrier semaphores. Data moves between devices by JAX's collectives and lax.ppermute only.
A program may use at most 192 MiB of HBM per device.

```python
import math
import jax
import jax.numpy as jnp
from jax import lax

PLANES = 4
RX = 64
CY = 128
FREQS = 3
MAT = 32
STEP = 1000
CAP = 128
PU = 256
PV = 256
HALF = 100
BLOCKS = 128
NX = 1024
NY = 1024
U = 4096
V = 2048
N_GY = 16
N_GX = 8


def draw_material_table(key, part):
    low_end = jnp.array([0.5, 0.2, 0.5, 0.05], jnp.float32)[:, None]
    high_end = jnp.array([1.0, 0.6, 0.98, 0.5], jnp.float32)[:, None]
    uniform_part = jax.random.uniform(key, (4, MAT), jnp.float32)
    return low_end + (high_end - low_end) * uniform_part


def spectrum_draw(key, component):
    shape = (FREQS, 2, 3, PLANES, NX, NY)
    offset_base = jnp.zeros((2, 3), jnp.float32).at[0, component].set(2.0).reshape(1, 2, 3, 1, 1, 1)
    return jnp.clip(jax.random.normal(key, shape, jnp.float32), -5.0, 5.0) + offset_base


def draw_dft_e(key, part):
    return spectrum_draw(jax.random.fold_in(key, 11), 0)


def draw_dft_h(key, part):
    return spectrum_draw(jax.random.fold_in(key, 23), 1)


def draw_skin_cell(key, part):
    block_keys = jax.random.split(jax.random.fold_in(key, 5), BLOCKS)
    cell_total = PLANES * RX * CY

    def per_block(block_key):
        return jax.random.permutation(block_key, cell_total)[:BLOCKS * CAP]
    return jax.vmap(per_block)(block_keys).reshape(BLOCKS, BLOCKS, CAP).astype(jnp.int32)


def draw_counts(key, part):
    key_level, key_count, key_column = jax.random.split(jax.random.fold_in(key, 7), 3)
    levels = jax.random.randint(key_level, (BLOCKS,), 1, 5)
    top_count = CAP * levels // 4 + 1
    raw_count = jax.random.randint(key_count, (BLOCKS, BLOCKS), 0, jnp.broadcast_to(top_count[None, :], (BLOCKS, BLOCKS)))
    hot_column = jax.random.randint(key_column, (), 0, BLOCKS)
    column_ids = jnp.arange(BLOCKS, dtype=jnp.int32)[None, :]
    return jnp.where(column_ids == hot_column, CAP, raw_count).astype(jnp.int32)


def draw_patch_slot(key, part):
    return jax.random.randint(jax.random.fold_in(key, 13), (BLOCKS, BLOCKS, CAP), 0, PU * PV).astype(jnp.int32)


def plant(entries, key, least, largest):
    longest = entries.shape.index(max(entries.shape))
    spots = []
    for shift in (0, 1):
        where = [jax.random.randint(jax.random.fold_in(key, axis), (), 0, length) for axis, length in enumerate(entries.shape)]
        where[longest] = (where[longest] + shift) % entries.shape[longest]
        spots.append(tuple(where))
    return entries.at[spots[0]].set(least).at[spots[1]].set(largest)


def block_levels(own_key, shape, cuts, smallest, largest):
    def one(dim, shards_of):
        steps = jax.random.uniform(jax.random.fold_in(jax.random.fold_in(own_key, 6), dim), (shards_of,), jnp.float32, smallest / len(cuts), largest / len(cuts))
        return jnp.repeat(jnp.exp(steps), shape[dim] // shards_of).reshape((-1,) + (1,) * (len(shape) - dim - 1))

    loudness = one(*cuts[0])
    for cut in cuts[1:]:
        loudness = loudness * one(*cut)
    return loudness


def gaussian(key, dims, spread, bound, cuts=(), kind=jnp.bfloat16):
    loudness = block_levels(key, dims, cuts, -0.22, 0.18) if cuts else 1.0
    drawn = jax.random.normal(key, dims, jnp.float32) * spread * loudness
    return jnp.minimum(jnp.maximum(drawn, -bound), bound).astype(kind)


def setup_inputs(seed: int = 0) -> dict:
    key_of = jax.random.split(jax.random.key(seed), 12)
    e_field = gaussian(key_of[0], (3, PLANES, NX, NY), 1.0, 6.0, ((2, 16), (3, 8)), jnp.float32)
    h_field = gaussian(key_of[1], (3, PLANES, NX, NY), 1.0, 6.0, ((2, 16), (3, 8)), jnp.float32)
    j_field = gaussian(key_of[2], (3, PLANES, NX, NY), 0.5, 3.0, ((2, 16), (3, 8)), jnp.float32)
    material = plant(jax.random.randint(key_of[3], (PLANES, NX, NY), 0, MAT), jax.random.fold_in(key_of[3], 1), 0, MAT - 1).astype(jnp.int32)
    material_table = draw_material_table(jax.random.fold_in(key_of[11], 71), 0)
    dft_e = draw_dft_e(jax.random.fold_in(key_of[11], 71), 0)
    dft_h = draw_dft_h(jax.random.fold_in(key_of[11], 71), 0)
    skin_cell = draw_skin_cell(jax.random.fold_in(key_of[11], 71), 0)
    counts = draw_counts(jax.random.fold_in(key_of[11], 71), 0)
    patch_slot = draw_patch_slot(jax.random.fold_in(key_of[11], 71), 0)
    area = jnp.clip(-0.5 + 2.0 * jax.random.uniform(key_of[10], (3, U, V), jnp.float32) ** block_levels(key_of[10], (3, U, V), ((1, 16), (2, 8)), -0.2, 0.2), -0.5, 1.5)
    return {"e_field": e_field, "h_field": h_field, "j_field": j_field, "material": material, "material_table": material_table, "dft_e": dft_e, "dft_h": dft_h, "skin_cell": skin_cell, "counts": counts, "patch_slot": patch_slot, "area": area}


FREQ_LIST = (28.0e9, 39.0e9, 60.0e9)
TIME_STEP = 1.9e-13


def phase_list(offset):
    return [2.0 * math.pi * freq_hz * (STEP + offset) * TIME_STEP for freq_hz in FREQ_LIST]


def accumulate(running, field_in, offset):
    pieces = []
    for phase_angle in phase_list(offset):
        pieces.append(jnp.stack([field_in * math.cos(phase_angle), field_in * (-math.sin(phase_angle))]))
    return running + jnp.stack(pieces)


def curl_field(h_field, rows_below, cols_left):
    magnet_x, magnet_y, magnet_z = h_field[0], h_field[1], h_field[2]
    zero_plane = jnp.zeros_like(magnet_x[:1])
    x_below_z = jnp.concatenate([zero_plane, magnet_x[:-1]], 0)
    y_below_z = jnp.concatenate([zero_plane, magnet_y[:-1]], 0)
    y_below_x = jnp.concatenate([rows_below[0][:, None, :], magnet_y[:, :-1, :]], 1)
    z_below_x = jnp.concatenate([rows_below[1][:, None, :], magnet_z[:, :-1, :]], 1)
    x_below_y = jnp.concatenate([cols_left[0][:, :, None], magnet_x[:, :, :-1]], 2)
    z_below_y = jnp.concatenate([cols_left[1][:, :, None], magnet_z[:, :, :-1]], 2)
    curl_x = (magnet_z - z_below_y) - (magnet_y - y_below_z)
    curl_y = (magnet_x - x_below_z) - (magnet_z - z_below_x)
    curl_z = (magnet_y - y_below_x) - (magnet_x - x_below_y)
    return jnp.stack([curl_x, curl_y, curl_z])


def cross_product(left_vec, right_vec):
    return jnp.stack([left_vec[:, 1] * right_vec[:, 2] - left_vec[:, 2] * right_vec[:, 1],
                      left_vec[:, 2] * right_vec[:, 0] - left_vec[:, 0] * right_vec[:, 2],
                      left_vec[:, 0] * right_vec[:, 1] - left_vec[:, 1] * right_vec[:, 0]], 1)


def cross_flux(e_rows, h_rows):
    return 0.5 * (cross_product(e_rows[:, 0], h_rows[:, 0]) + cross_product(e_rows[:, 1], h_rows[:, 1]))


def to_blocks(values):
    leading = values.shape[0]
    grid = values.reshape(leading, PLANES, N_GY, RX, N_GX, CY).transpose(0, 2, 4, 1, 3, 5)
    return grid.reshape(leading, BLOCKS, PLANES * RX * CY)


def take_blocks(blocked, index_rows):
    return jax.vmap(lambda block_rows, block_index: jnp.take(block_rows, block_index, axis=1), in_axes=(1, 0), out_axes=1)(blocked, index_rows)


def gather_rows(spectrum, skin_cell, live_mask):
    blocked = to_blocks(spectrum.reshape(6 * FREQS, PLANES, NX, NY))
    picked = take_blocks(blocked, skin_cell.reshape(BLOCKS, BLOCKS * CAP))
    return picked.reshape(FREQS, 2, 3, BLOCKS, BLOCKS, CAP) * live_mask


def window_sum(values, along, half_width):
    widths = [(0, 0), (0, 0), (0, 0)]
    widths[along] = (half_width + 1, half_width)
    running = jnp.cumsum(jnp.pad(values, widths), axis=along)
    length = values.shape[along]
    upper_sum = lax.slice_in_dim(running, 2 * half_width, 2 * half_width + length, axis=along)
    lower_sum = lax.slice_in_dim(running, 0, length, axis=along)
    return upper_sum - lower_sum


def reference(e_field, h_field, j_field, material, material_table, dft_e, dft_h, skin_cell, counts, patch_slot, area):
    coeffs = jnp.take(material_table, material, axis=1)
    zero_rows = jnp.zeros((2, PLANES, NY), jnp.float32)
    zero_cols = jnp.zeros((2, PLANES, NX), jnp.float32)
    curl_h = curl_field(h_field, zero_rows, zero_cols)
    e_next = coeffs[0] * e_field + coeffs[1] * (curl_h - j_field)
    j_next = coeffs[2] * j_field + coeffs[3] * (e_next - e_field)
    dft_e_next = accumulate(dft_e, e_next, 0.0)
    dft_h_next = accumulate(dft_h, h_field, 0.5)
    live_mask = (jnp.arange(CAP, dtype=jnp.int32)[None, None, :] < counts[:, :, None]).astype(jnp.float32)
    e_rows = gather_rows(dft_e_next, skin_cell, live_mask)
    h_rows = gather_rows(dft_h_next, skin_cell, live_mask)
    flux = cross_flux(e_rows, h_rows)
    flux = flux.transpose(0, 1, 3, 2, 4).reshape(FREQS, 3, BLOCKS, BLOCKS * CAP)
    area_blocks = area.reshape(3, N_GY, PU, N_GX, PV).transpose(0, 1, 3, 2, 4).reshape(3, BLOCKS, PU * PV)
    patch_index = patch_slot.reshape(BLOCKS, BLOCKS * CAP)
    area_rows = take_blocks(area_blocks, patch_index)
    density = area_rows[0] * flux[:, 0] + area_rows[1] * flux[:, 1] + area_rows[2] * flux[:, 2]
    point_blocks = jax.vmap(lambda target, weight: jnp.zeros((FREQS, PU * PV), jnp.float32).at[:, target].add(weight), in_axes=(0, 1), out_axes=1)(patch_index, density)
    point_density = point_blocks.reshape(FREQS, N_GY, N_GX, PU, PV).transpose(0, 1, 3, 2, 4).reshape(FREQS, U, V)
    strip_sum = window_sum(point_density, 1, HALF)
    avg_density = window_sum(strip_sum, 2, HALF) / (4.0 * HALF * HALF)
    return (e_next, j_next, dft_e_next, dft_h_next, point_density, avg_density)
```

```python
import functools
import math

import jax
import jax.numpy as jnp
from jax import lax
from jax.experimental import pallas as pl
from jax.experimental.pallas import tpu as pltpu
from jax.sharding import PartitionSpec as P

STEP = 1000
HALF = 100
FREQ_LIST = (28000000000.0, 39000000000.0, 60000000000.0)
TIME_STEP = 1.9e-13

f32 = jnp.float32
bf16 = jnp.bfloat16
VMEM = pl.BlockSpec(memory_space=pltpu.VMEM)
SMEM = pl.BlockSpec(memory_space=pltpu.SMEM)


def phase_list(offset):
    return [2.0 * math.pi * freq_hz * (STEP + offset) * TIME_STEP for freq_hz in FREQ_LIST]


def iota(shape, dim):
    return lax.broadcasted_iota(jnp.int32, shape, dim)


def shifted(value, axis, steps):
    count = lax.axis_size(axis)
    leading, last = (max(0, -steps), min(count, count - steps))
    return lax.ppermute(value, axis, [(source, source + steps) for source in range(leading, last)])


def with_halo(cells, sides, width):
    for axis, dim in sides:
        count = lax.axis_size(axis)
        ends = count - 1
        head = lax.slice_in_dim(cells, 0, width, axis=dim)
        tail = lax.slice_in_dim(cells, cells.shape[dim] - width, cells.shape[dim], axis=dim)
        cells = jnp.concatenate(
            [
                lax.ppermute(tail, axis, [(i, (i + 1) % count) for i in range(ends)]),
                cells,
                lax.ppermute(head, axis, [((i + 1) % count, i) for i in range(ends)]),
            ],
            axis=dim,
        )
    return cells


def band_matrix(count, half_width):
    row_ids = iota((count, count + 2 * half_width), 0)
    col_ids = iota((count, count + 2 * half_width), 1)
    return ((col_ids >= row_ids) & (col_ids < row_ids + 2 * half_width)).astype(f32)


def field_kernel(
    e_ref, h_ref, j_ref, kind_ref, table_ref, dft_e_ref, dft_h_ref, row_ref, col_ref,
    e_out, j_out, dft_e_out, dft_h_out, flux_out, below_ref, wide_ref,
):
    z = pl.program_id(0)

    @pl.when(z == 0)
    def _():
        below_ref[...] = jnp.zeros_like(below_ref)
        wide_ref[...] = jnp.zeros_like(wide_ref)
        wide_ref[0:4, 0:32] = table_ref[...]

    rows, cols = kind_ref.shape[1:]
    hx, hy, hz = h_ref[0, 0], h_ref[1, 0], h_ref[2, 0]
    first_row = iota((rows, cols), 0) == 0
    first_col = iota((rows, cols), 1) == 0
    diagonal = iota((rows, rows), 0) == iota((rows, rows), 1)

    def below_x(field, part):
        halo = row_ref[part, pl.ds(z, 1), :]
        return jnp.where(first_row, halo, pltpu.roll(field, 1, 0))

    def below_y(field, part):
        halo = col_ref[part, pl.ds(z, 1), :]
        halo = jnp.sum(jnp.where(diagonal, halo, 0.0), axis=1, keepdims=True)
        return jnp.where(first_col, halo, pltpu.roll(field, 1, 1))

    curl = (
        (hz - below_y(hz, 1)) - (hy - below_ref[1]),
        (hx - below_ref[0]) - (hz - below_x(hz, 1)),
        (hy - below_x(hy, 0)) - (hx - below_y(hx, 0)),
    )
    kinds = kind_ref[0]
    coeffs = [
        jnp.take_along_axis(
            jnp.broadcast_to(wide_ref[r : r + 1, :], (rows, cols)), kinds, axis=1
        )
        for r in range(4)
    ]
    e_next = []
    for c in range(3):
        old_e, old_j = e_ref[c, 0], j_ref[c, 0]
        new_e = coeffs[0] * old_e + coeffs[1] * (curl[c] - old_j)
        e_out[c, 0] = new_e
        j_out[c, 0] = coeffs[2] * old_j + coeffs[3] * (new_e - old_e)
        e_next.append(new_e)
    field_h = (hx, hy, hz)
    phase_e, phase_h = phase_list(0.0), phase_list(0.5)
    half_plane = pl.ds(pl.multiple_of((z // 2) * cols, cols), cols)
    rest_plane = pl.ds(pl.multiple_of((z // 2) * cols + 2 * cols, cols), cols)
    for f in range(3):
        spec_e, spec_h = [], []
        for part in range(2):
            factor_e = math.cos(phase_e[f]) if part == 0 else -math.sin(phase_e[f])
            factor_h = math.cos(phase_h[f]) if part == 0 else -math.sin(phase_h[f])
            now_e = [dft_e_ref[f, part, c, 0] + e_next[c] * factor_e for c in range(3)]
            now_h = [dft_h_ref[f, part, c, 0] + field_h[c] * factor_h for c in range(3)]
            for c in range(3):
                dft_e_out[f, part, c, 0] = now_e[c]
                dft_h_out[f, part, c, 0] = now_h[c]
            spec_e.append(now_e)
            spec_h.append(now_h)
        for c in range(3):
            a, b = (c + 1) % 3, (c + 2) % 3
            flux = 0.5 * (
                (spec_e[0][a] * spec_h[0][b] - spec_e[0][b] * spec_h[0][a])
                + (spec_e[1][a] * spec_h[1][b] - spec_e[1][b] * spec_h[1][a])
            )
            head = flux.astype(bf16)
            flux_out[3 * f + c, z % 2, :, half_plane] = head
            flux_out[3 * f + c, z % 2, :, rest_plane] = (flux - head.astype(f32)).astype(bf16)
    below_ref[0] = hx
    below_ref[1] = hy


def field_step(e, h, j, kinds, table, dft_e, dft_h, rows_below, cols_left):
    planes, rows, cols = kinds.shape
    plane3 = pl.BlockSpec((3, 1, rows, cols), lambda z: (0, z, 0, 0))
    spectra = pl.BlockSpec((3, 2, 3, 1, rows, cols), lambda z: (0, 0, 0, z, 0, 0))

    def whole(shape):
        return pl.BlockSpec(shape, lambda z: (0,) * len(shape))

    flux_shape = (9, 2, rows, 4 * cols)
    return pl.pallas_call(
        field_kernel,
        grid=(planes,),
        out_shape=(
            jax.ShapeDtypeStruct(e.shape, f32),
            jax.ShapeDtypeStruct(e.shape, f32),
            jax.ShapeDtypeStruct(dft_e.shape, f32),
            jax.ShapeDtypeStruct(dft_h.shape, f32),
            jax.ShapeDtypeStruct(flux_shape, bf16),
        ),
        in_specs=[
            plane3, plane3, plane3,
            pl.BlockSpec((1, rows, cols), lambda z: (z, 0, 0)),
            whole(table.shape), spectra, spectra,
            whole(rows_below.shape), whole(cols_left.shape),
        ],
        out_specs=(plane3, plane3, spectra, spectra, whole(flux_shape)),
        scratch_shapes=[pltpu.VMEM((2, rows, cols), f32), pltpu.VMEM((8, cols), f32)],
        name="field_step",
    )(e, h, j, kinds, table, dft_e, dft_h, rows_below, cols_left)


def gather_kernel(count_ref, cell_ref, table_ref, out_ref, packed, found):
    lane = iota((1, 128), 1)

    def pack(d, carry):
        offset, current = carry
        row, start = lax.shift_right_logical(offset, 7), lax.bitwise_and(offset, 127)
        live = count_ref[0, d]
        rolled = pltpu.roll(cell_ref[0, pl.ds(d, 1), :], start, 1)
        merged = jnp.where(lane >= start, rolled, current)
        packed[pl.ds(row, 1), :] = merged
        return offset + live, jnp.where(start + live >= 128, rolled, merged)

    offset, current = lax.fori_loop(
        0, 128, pack, (jnp.int32(0), jnp.zeros((1, 128), jnp.int32)), unroll=8
    )
    packed[pl.ds(lax.shift_right_logical(offset, 7), 1), :] = current

    def chunk(c, _):
        cell = jnp.concatenate([packed[pl.ds(2 * c, 1), :], packed[pl.ds(2 * c + 1, 1), :]], 1)
        high = lax.bitwise_and(lax.shift_right_logical(cell, 14), 1)
        inner = lax.bitwise_or(lax.shift_left(high, 7), lax.bitwise_and(cell, 127))
        outer = lax.bitwise_and(lax.shift_right_logical(cell, 7), 127)
        onehot = jnp.where(iota((256, 256), 0) == inner, 1.0, 0.0).astype(bf16)
        result = jnp.dot(
            table_ref[...].reshape(1152, 512),
            jnp.concatenate([onehot, onehot], 0),
            preferred_element_type=f32,
        ).reshape(9, 128, 256)
        mine = iota((128, 256), 0) == outer
        for q in range(9):
            value = jnp.sum(jnp.where(mine, result[q], 0.0), axis=0, keepdims=True)
            found[2 * c, q : q + 1, :] = value[:, :128]
            found[2 * c + 1, q : q + 1, :] = value[:, 128:]
        return 0

    lax.fori_loop(0, lax.shift_right_logical(offset + 255, 8), chunk, 0)
    lanes = iota((16, 128), 1)

    def unpack(d, offset):
        row, start = lax.shift_right_logical(offset, 7), lax.bitwise_and(offset, 127)
        live = count_ref[0, d]
        back = lax.bitwise_and(128 - start, 127)
        value = jnp.where(
            lanes < 128 - start, pltpu.roll(found[row], back, 1), pltpu.roll(found[row + 1], back, 1)
        )
        value = jnp.where(lanes < live, value, 0.0)
        for q in range(9):
            out_ref[d, q] = value[q : q + 1, :]
        return offset + live

    lax.fori_loop(0, 128, unpack, jnp.int32(0), unroll=4)


def gather_flux(counts, cells, table):
    return pl.pallas_call(
        gather_kernel,
        out_shape=jax.ShapeDtypeStruct((128, 9, 1, 128), f32),
        in_specs=[SMEM, VMEM, VMEM],
        out_specs=VMEM,
        scratch_shapes=[pltpu.VMEM((136, 128), jnp.int32), pltpu.VMEM((136, 16, 128), f32)],
        name="gather_flux",
    )(counts, cells, table)


def slot_row(ref, c):
    return jnp.concatenate([ref[0, pl.ds(2 * c, 1), :], ref[0, pl.ds(2 * c + 1, 1), :]], 1)


def area_kernel(patch_ref, area_ref, out_ref, table):
    area = area_ref[...].reshape(768, 256)
    head = area.astype(bf16)
    table[:, :256] = head
    table[:, 256:] = (area - head.astype(f32)).astype(bf16)

    def chunk(c, _):
        patch = slot_row(patch_ref, c)
        u, v = lax.shift_right_logical(patch, 8), lax.bitwise_and(patch, 255)
        onehot = jnp.where(iota((256, 256), 0) == v, 1.0, 0.0).astype(bf16)
        result = jnp.dot(
            table[...], jnp.concatenate([onehot, onehot], 0), preferred_element_type=f32
        ).reshape(3, 256, 256)
        mine = iota((256, 256), 0) == u
        for q in range(3):
            out_ref[c, q : q + 1, :] = jnp.sum(
                jnp.where(mine, result[q], 0.0), axis=0, keepdims=True
            )
        return 0

    lax.fori_loop(0, 64, chunk, 0)


def gather_area(patch, area):
    return pl.pallas_call(
        area_kernel,
        out_shape=jax.ShapeDtypeStruct((64, 8, 256), f32),
        in_specs=[VMEM, VMEM],
        out_specs=VMEM,
        scratch_shapes=[pltpu.VMEM((768, 512), bf16)],
        cost_estimate=pl.CostEstimate(
            flops=2 * 768 * 512 * 16384, bytes_accessed=2000000, transcendentals=0
        ),
        name="gather_area",
    )(patch, area)


def scatter_kernel(patch_ref, area_ref, flux_ref, out_ref):
    out_ref[...] = jnp.zeros_like(out_ref)

    def chunk(c, _):
        patch = slot_row(patch_ref, c)
        u, v = lax.shift_right_logical(patch, 8), lax.bitwise_and(patch, 255)
        onehot = jnp.where(iota((256, 256), 0) == v, 1.0, 0.0).astype(bf16)
        mine = iota((256, 256), 0) == u
        area = area_ref[c]
        heads, rests = [], []
        for f in range(3):
            density = jnp.zeros((1, 256), f32)
            for q in range(3):
                flux = jnp.concatenate(
                    [flux_ref[2 * c, 3 * f + q], flux_ref[2 * c + 1, 3 * f + q]], 1
                )
                density = density + area[q : q + 1, :] * flux
            head = density.astype(bf16).astype(f32)
            heads.append(jnp.where(mine, head, 0.0).astype(bf16))
            rests.append(jnp.where(mine, density - head, 0.0).astype(bf16))
        left = jnp.concatenate([jnp.concatenate(heads, 0), jnp.concatenate(rests, 0)], 1)
        right = jnp.concatenate([onehot, onehot], 1)
        out_ref[...] += lax.dot_general(
            left, right, (((1,), (1,)), ((), ())), preferred_element_type=f32
        ).reshape(3, 256, 256)
        return 0

    lax.fori_loop(0, 64, chunk, 0)


def scatter_density(patch, area_rows, flux):
    return pl.pallas_call(
        scatter_kernel,
        out_shape=jax.ShapeDtypeStruct((3, 256, 256), f32),
        in_specs=[VMEM, VMEM, VMEM],
        out_specs=VMEM,
        name="scatter_density",
    )(patch, area_rows, flux)


def shards(
    e_field, h_field, j_field, material, material_table, dft_e, dft_h, skin_cell, counts,
    patch_slot, area,
):
    magnet_x, magnet_y, magnet_z = (h_field[0], h_field[1], h_field[2])
    rows_below = shifted(jnp.stack([magnet_y[:, -1, :], magnet_z[:, -1, :]]), "gy", 1)
    cols_left = shifted(jnp.stack([magnet_x[:, :, -1], magnet_z[:, :, -1]]), "gx", 1)
    e_next, j_next, dft_e_next, dft_h_next, table = field_step(
        e_field, h_field, j_field, material, material_table, dft_e, dft_h, rows_below, cols_left
    )
    rows = gather_flux(counts, skin_cell, table.reshape(9, 128, 512))
    arrived = lax.all_to_all(rows, ("gy", "gx"), split_axis=0, concat_axis=0, tiled=True)
    area_rows = gather_area(patch_slot, area)
    point_density = scatter_density(patch_slot, area_rows, arrived)
    padded = with_halo(point_density, (("gy", 1),), HALF)
    strip_sum = jnp.einsum(
        "ij,fjv->fiv",
        band_matrix(256, HALF),
        padded,
        precision=lax.Precision.HIGHEST,
        preferred_element_type=f32,
    )
    padded_cols = with_halo(strip_sum, (("gx", 2),), HALF)
    square_sum = jnp.einsum(
        "fuj,ij->fui",
        padded_cols,
        band_matrix(256, HALF),
        precision=lax.Precision.HIGHEST,
        preferred_element_type=f32,
    )
    avg_density = square_sum / (4.0 * HALF * HALF)
    return (e_next, j_next, dft_e_next, dft_h_next, point_density, avg_density)


def solution(mesh):
    placed = (
        P(None, None, "gy", "gx"),
        P(None, None, "gy", "gx"),
        P(None, None, "gy", "gx"),
        P(None, "gy", "gx"),
        P(),
        P(None, None, None, None, "gy", "gx"),
        P(None, None, None, None, "gy", "gx"),
        P(("gy", "gx"), None, None),
        P(("gy", "gx"), None),
        P(("gy", "gx"), None, None),
        P(None, "gy", "gx"),
    )
    return jax.shard_map(
        shards,
        mesh=mesh,
        in_specs=placed,
        out_specs=(
            P(None, None, "gy", "gx"),
            P(None, None, "gy", "gx"),
            P(None, None, None, None, "gy", "gx"),
            P(None, None, None, None, "gy", "gx"),
            P(None, "gy", "gx"),
            P(None, "gy", "gx"),
        ),
        check_vma=False,
    )
```

```python
import functools
import math

import jax
import jax.numpy as jnp
from jax import lax
from jax.experimental import pallas as pl
from jax.experimental.pallas import tpu as pltpu
from jax.sharding import PartitionSpec as P

STEP = 1000
HALF = 100
FREQ_LIST = (28000000000.0, 39000000000.0, 60000000000.0)
TIME_STEP = 1.9e-13

f32 = jnp.float32
bf16 = jnp.bfloat16
VMEM = pl.BlockSpec(memory_space=pltpu.VMEM)
SMEM = pl.BlockSpec(memory_space=pltpu.SMEM)


def phase_list(offset):
    return [2.0 * math.pi * freq_hz * (STEP + offset) * TIME_STEP for freq_hz in FREQ_LIST]


def iota(shape, dim):
    return lax.broadcasted_iota(jnp.int32, shape, dim)


def shifted(value, axis, steps):
    count = lax.axis_size(axis)
    leading, last = (max(0, -steps), min(count, count - steps))
    return lax.ppermute(value, axis, [(source, source + steps) for source in range(leading, last)])


def onehot(count, index):
    places = iota((count, index.shape[1]), 0).astype(bf16)
    return jnp.where(places == index.astype(bf16), jnp.ones((), bf16), jnp.zeros((), bf16))


def field_kernel(
    e_ref, h_ref, j_ref, kind_ref, table_ref, dft_e_ref, dft_h_ref, row_ref, col_ref,
    e_out, j_out, dft_e_out, dft_h_out, flux_out, below_ref, wide_ref,
):
    z = pl.program_id(0)

    @pl.when(z == 0)
    def _():
        below_ref[...] = jnp.zeros_like(below_ref)
        wide_ref[...] = jnp.zeros_like(wide_ref)
        wide_ref[0:4, 0:32] = table_ref[...]

    rows, cols = kind_ref.shape[1:]
    hx, hy, hz = h_ref[0, 0], h_ref[1, 0], h_ref[2, 0]
    first_row = iota((rows, cols), 0) == 0
    first_col = iota((rows, cols), 1) == 0
    diagonal = iota((rows, rows), 0) == iota((rows, rows), 1)

    def below_x(field, part):
        halo = row_ref[part, pl.ds(z, 1), :]
        return jnp.where(first_row, halo, pltpu.roll(field, 1, 0))

    def below_y(field, part):
        halo = col_ref[part, pl.ds(z, 1), :]
        halo = jnp.sum(jnp.where(diagonal, halo, 0.0), axis=1, keepdims=True)
        return jnp.where(first_col, halo, pltpu.roll(field, 1, 1))

    curl = (
        (hz - below_y(hz, 1)) - (hy - below_ref[1]),
        (hx - below_ref[0]) - (hz - below_x(hz, 1)),
        (hy - below_x(hy, 0)) - (hx - below_y(hx, 0)),
    )
    kinds = kind_ref[0]
    coeffs = [
        jnp.take_along_axis(
            jnp.broadcast_to(wide_ref[r : r + 1, :], (rows, cols)), kinds, axis=1
        )
        for r in range(4)
    ]
    e_next = []
    for c in range(3):
        old_e, old_j = e_ref[c, 0], j_ref[c, 0]
        new_e = coeffs[0] * old_e + coeffs[1] * (curl[c] - old_j)
        e_out[c, 0] = new_e
        j_out[c, 0] = coeffs[2] * old_j + coeffs[3] * (new_e - old_e)
        e_next.append(new_e)
    field_h = (hx, hy, hz)
    phase_e, phase_h = phase_list(0.0), phase_list(0.5)
    half_plane = pl.ds(pl.multiple_of((z // 2) * cols, cols), cols)
    rest_plane = pl.ds(pl.multiple_of((z // 2) * cols + 2 * cols, cols), cols)
    for f in range(3):
        spec_e, spec_h = [], []
        for part in range(2):
            factor_e = math.cos(phase_e[f]) if part == 0 else -math.sin(phase_e[f])
            factor_h = math.cos(phase_h[f]) if part == 0 else -math.sin(phase_h[f])
            now_e = [dft_e_ref[f, part, c, 0] + e_next[c] * factor_e for c in range(3)]
            now_h = [dft_h_ref[f, part, c, 0] + field_h[c] * factor_h for c in range(3)]
            for c in range(3):
                dft_e_out[f, part, c, 0] = now_e[c]
                dft_h_out[f, part, c, 0] = now_h[c]
            spec_e.append(now_e)
            spec_h.append(now_h)
        for c in range(3):
            a, b = (c + 1) % 3, (c + 2) % 3
            flux = 0.5 * (
                (spec_e[0][a] * spec_h[0][b] - spec_e[0][b] * spec_h[0][a])
                + (spec_e[1][a] * spec_h[1][b] - spec_e[1][b] * spec_h[1][a])
            )
            head = flux.astype(bf16)
            flux_out[3 * f + c, z % 2, :, half_plane] = head
            flux_out[3 * f + c, z % 2, :, rest_plane] = (flux - head.astype(f32)).astype(bf16)
    below_ref[0] = hx
    below_ref[1] = hy


def field_step(e, h, j, kinds, table, dft_e, dft_h, rows_below, cols_left):
    planes, rows, cols = kinds.shape
    plane3 = pl.BlockSpec((3, 1, rows, cols), lambda z: (0, z, 0, 0))
    spectra = pl.BlockSpec((3, 2, 3, 1, rows, cols), lambda z: (0, 0, 0, z, 0, 0))

    def whole(shape):
        return pl.BlockSpec(shape, lambda z: (0,) * len(shape))

    flux_shape = (9, 2, rows, 4 * cols)
    return pl.pallas_call(
        field_kernel,
        grid=(planes,),
        out_shape=(
            jax.ShapeDtypeStruct(e.shape, f32),
            jax.ShapeDtypeStruct(e.shape, f32),
            jax.ShapeDtypeStruct(dft_e.shape, f32),
            jax.ShapeDtypeStruct(dft_h.shape, f32),
            jax.ShapeDtypeStruct(flux_shape, bf16),
        ),
        in_specs=[
            plane3, plane3, plane3,
            pl.BlockSpec((1, rows, cols), lambda z: (z, 0, 0)),
            whole(table.shape), spectra, spectra,
            whole(rows_below.shape), whole(cols_left.shape),
        ],
        out_specs=(plane3, plane3, spectra, spectra, whole(flux_shape)),
        scratch_shapes=[pltpu.VMEM((2, rows, cols), f32), pltpu.VMEM((8, cols), f32)],
        name="field_step",
    )(e, h, j, kinds, table, dft_e, dft_h, rows_below, cols_left)


def gather_kernel(count_ref, cell_ref, table_ref, out_ref, packed, found):
    lane = iota((1, 128), 1)

    def pack(d, carry):
        offset, current = carry
        row, start = lax.shift_right_logical(offset, 7), lax.bitwise_and(offset, 127)
        live = count_ref[0, d]
        rolled = pltpu.roll(cell_ref[0, pl.ds(d, 1), :], start, 1)
        merged = jnp.where(lane >= start, rolled, current)
        packed[pl.ds(row, 1), :] = merged
        return offset + live, jnp.where(start + live >= 128, rolled, merged)

    offset, current = lax.fori_loop(
        0, 128, pack, (jnp.int32(0), jnp.zeros((1, 128), jnp.int32)), unroll=32
    )
    packed[pl.ds(lax.shift_right_logical(offset, 7), 1), :] = current

    def lookup(c):
        cell = jnp.concatenate([packed[pl.ds(2 * c, 1), :], packed[pl.ds(2 * c + 1, 1), :]], 1)
        high = lax.bitwise_and(lax.shift_right_logical(cell, 14), 1)
        inner = lax.bitwise_or(lax.shift_left(high, 7), lax.bitwise_and(cell, 127))
        outer = lax.bitwise_and(lax.shift_right_logical(cell, 7), 127)
        hot = onehot(256, inner)
        result = jnp.dot(
            table_ref[...].reshape(1152, 512),
            jnp.concatenate([hot, hot], 0),
            preferred_element_type=f32,
        ).reshape(9, 128, 256)
        mine = iota((128, 256), 0) == outer
        for q in range(9):
            value = jnp.sum(jnp.where(mine, result[q], 0.0), axis=0, keepdims=True)
            found[2 * c, q : q + 1, :] = value[:, :128]
            found[2 * c + 1, q : q + 1, :] = value[:, 128:]

    def chunk(c, _):
        for part in range(4):
            lookup(4 * c + part)
        return 0

    lax.fori_loop(0, lax.shift_right_logical(offset + 1023, 10), chunk, 0)
    lanes = iota((16, 128), 1)

    def unpack(d, offset):
        row, start = lax.shift_right_logical(offset, 7), lax.bitwise_and(offset, 127)
        live = count_ref[0, d]
        back = lax.bitwise_and(128 - start, 127)
        value = jnp.where(
            lanes < 128 - start, pltpu.roll(found[row], back, 1), pltpu.roll(found[row + 1], back, 1)
        )
        value = jnp.where(lanes < live, value, 0.0)
        for q in range(9):
            out_ref[d, q] = value[q : q + 1, :]
        return offset + live

    lax.fori_loop(0, 128, unpack, jnp.int32(0), unroll=16)


def gather_flux(counts, cells, table):
    return pl.pallas_call(
        gather_kernel,
        out_shape=jax.ShapeDtypeStruct((128, 9, 1, 128), f32),
        in_specs=[SMEM, VMEM, VMEM],
        out_specs=VMEM,
        scratch_shapes=[pltpu.VMEM((136, 128), jnp.int32), pltpu.VMEM((136, 16, 128), f32)],
        name="gather_flux",
    )(counts, cells, table)


GROUP = 8


def slot_row(ref, c):
    return jnp.concatenate([ref[0, pl.ds(GROUP * c + i, 1), :] for i in range(GROUP)], 1)


def area_kernel(patch_ref, area_ref, out_ref, table, *, first):
    area = area_ref[...].reshape(768, 256)
    head = area.astype(bf16)
    table[:, :256] = head
    table[:, 256:] = (area - head.astype(f32)).astype(bf16)

    def chunk(c, _):
        patch = slot_row(patch_ref, c + first)
        u, v = lax.shift_right_logical(patch, 8), lax.bitwise_and(patch, 255)
        hot = onehot(256, v)
        result = jnp.dot(
            table[...], jnp.concatenate([hot, hot], 0), preferred_element_type=f32
        ).reshape(3, 256, GROUP * 128)
        mine = iota((256, GROUP * 128), 0) == u
        for q in range(3):
            out_ref[c, q : q + 1, :] = jnp.sum(
                jnp.where(mine, result[q], 0.0), axis=0, keepdims=True
            )
        return 0

    lax.fori_loop(0, out_ref.shape[0], chunk, 0, unroll=4)


def gather_area(patch, area, first, groups):
    return pl.pallas_call(
        functools.partial(area_kernel, first=first),
        out_shape=jax.ShapeDtypeStruct((groups, 8, GROUP * 128), f32),
        in_specs=[VMEM, VMEM],
        out_specs=VMEM,
        scratch_shapes=[pltpu.VMEM((768, 512), bf16)],
        cost_estimate=pl.CostEstimate(
            flops=2 * 768 * 512 * GROUP * 128 * groups, bytes_accessed=2000000, transcendentals=0
        ),
        name="gather_area",
    )(patch, area)


EDGE = 104


def scatter_kernel(patch_ref, area_a_ref, area_b_ref, flux_ref, out_ref, head_ref, tail_ref):
    out_ref[...] = jnp.zeros_like(out_ref)

    def add_group(c, area):
        patch = slot_row(patch_ref, c)
        u, v = lax.shift_right_logical(patch, 8), lax.bitwise_and(patch, 255)
        hot = onehot(256, v)
        mine = iota((256, GROUP * 128), 0).astype(bf16) == u.astype(bf16)
        heads, rests = [], []
        for f in range(3):
            density = jnp.zeros((1, GROUP * 128), f32)
            for q in range(3):
                flux = jnp.concatenate(
                    [flux_ref[GROUP * c + i, 3 * f + q] for i in range(GROUP)], 1
                )
                density = density + area[q : q + 1, :] * flux
            head = density.astype(bf16)
            rest = (density - head.astype(f32)).astype(bf16)
            heads.append(jnp.where(mine, head, jnp.zeros((), bf16)))
            rests.append(jnp.where(mine, rest, jnp.zeros((), bf16)))
        left = jnp.concatenate([jnp.concatenate(heads, 0), jnp.concatenate(rests, 0)], 1)
        right = jnp.concatenate([hot, hot], 1)
        out_ref[...] += lax.dot_general(
            left, right, (((1,), (1,)), ((), ())), preferred_element_type=f32
        ).reshape(3, 256, 256)

    half = area_a_ref.shape[0]

    def first_half(c, _):
        add_group(c, area_a_ref[c])
        return 0

    def second_half(c, _):
        add_group(c + half, area_b_ref[c])
        return 0

    lax.fori_loop(0, half, first_half, 0, unroll=4)
    lax.fori_loop(0, area_b_ref.shape[0], second_half, 0, unroll=4)
    head_ref[...] = out_ref[:, :EDGE, :]
    tail_ref[...] = out_ref[:, 256 - EDGE :, :]


BLOCK_AND_EDGES = (
    jax.ShapeDtypeStruct((3, 256, 256), f32),
    jax.ShapeDtypeStruct((3, EDGE, 256), f32),
    jax.ShapeDtypeStruct((3, EDGE, 256), f32),
)


def scatter_density(patch, area_a, area_b, flux):
    return pl.pallas_call(
        scatter_kernel,
        out_shape=BLOCK_AND_EDGES,
        in_specs=[VMEM] * 4,
        out_specs=(VMEM,) * 3,
        name="scatter_density",
    )(patch, area_a, area_b, flux)


def window_kernel(block_ref, before_ref, after_ref, out_ref, *edges, scale):
    cells = jnp.concatenate([before_ref[0], block_ref[0], after_ref[0]], 0)
    length = cells.shape[0]
    place = iota((length, 256), 0) - EDGE - iota((length, 256), 1)
    band = jnp.where((place >= -HALF) & (place < HALF), 1.0, 0.0).astype(bf16)
    head = cells.astype(bf16)
    rest = (cells - head.astype(f32)).astype(bf16)
    total = lax.dot_general(
        jnp.concatenate([head, rest], 0),
        jnp.concatenate([band, band], 0),
        (((0,), (0,)), ((), ())),
        preferred_element_type=f32,
    )
    if scale != 1.0:
        total = total * scale
    out_ref[0] = total
    if edges:
        edges[0][0] = total[:EDGE]
        edges[1][0] = total[256 - EDGE :]


def window_sum(block, before, after, scale, with_edges):
    whole = pl.BlockSpec((1, 256, 256), lambda f: (f, 0, 0))
    edge = pl.BlockSpec((1, EDGE, 256), lambda f: (f, 0, 0))
    return pl.pallas_call(
        functools.partial(window_kernel, scale=scale),
        grid=(3,),
        out_shape=BLOCK_AND_EDGES if with_edges else BLOCK_AND_EDGES[:1],
        in_specs=[whole, edge, edge],
        out_specs=(whole, edge, edge) if with_edges else (whole,),
        name="window_sum",
    )(block, before, after)


def shards(
    e_field, h_field, j_field, material, material_table, dft_e, dft_h, skin_cell, counts,
    patch_slot, area,
):
    magnet_x, magnet_y, magnet_z = (h_field[0], h_field[1], h_field[2])
    rows_below = shifted(jnp.stack([magnet_y[:, -1, :], magnet_z[:, -1, :]]), "gy", 1)
    cols_left = shifted(jnp.stack([magnet_x[:, :, -1], magnet_z[:, :, -1]]), "gx", 1)
    area_a = gather_area(patch_slot, area, 0, 8)
    rows_below, cols_left, area_a = lax.optimization_barrier((rows_below, cols_left, area_a))
    e_next, j_next, dft_e_next, dft_h_next, table = field_step(
        e_field, h_field, j_field, material, material_table, dft_e, dft_h, rows_below, cols_left
    )
    rows = gather_flux(counts, skin_cell, table.reshape(9, 128, 512))
    arrived = lax.all_to_all(rows, ("gy", "gx"), split_axis=0, concat_axis=0, tiled=True)
    area_b = gather_area(patch_slot, area, 8, 8)
    point_density, head, tail = scatter_density(patch_slot, area_a, area_b, arrived)
    before, after = shifted(tail, "gy", 1), shifted(head, "gy", -1)
    strip_sum, head, tail = window_sum(point_density, before, after, 1.0, True)
    before, after = shifted(tail, "gx", 1), shifted(head, "gx", -1)
    (avg_density,) = window_sum(strip_sum, before, after, 1.0 / (4.0 * HALF * HALF), False)
    return (e_next, j_next, dft_e_next, dft_h_next, point_density, avg_density)


def solution(mesh):
    placed = (
        P(None, None, "gy", "gx"),
        P(None, None, "gy", "gx"),
        P(None, None, "gy", "gx"),
        P(None, "gy", "gx"),
        P(),
        P(None, None, None, None, "gy", "gx"),
        P(None, None, None, None, "gy", "gx"),
        P(("gy", "gx"), None, None),
        P(("gy", "gx"), None),
        P(("gy", "gx"), None, None),
        P(None, "gy", "gx"),
    )
    return jax.shard_map(
        shards,
        mesh=mesh,
        in_specs=placed,
        out_specs=(
            P(None, None, "gy", "gx"),
            P(None, None, "gy", "gx"),
            P(None, None, None, None, "gy", "gx"),
            P(None, None, None, None, "gy", "gx"),
            P(None, "gy", "gx"),
            P(None, "gy", "gx"),
        ),
        check_vma=False,
    )
```

```python
import functools
import math

import jax
import jax.numpy as jnp
from jax import lax
from jax.experimental import pallas as pl
from jax.experimental.pallas import tpu as pltpu
from jax.sharding import PartitionSpec as P

STEP = 1000
HALF = 100
FREQ_LIST = (28000000000.0, 39000000000.0, 60000000000.0)
TIME_STEP = 1.9e-13

f32 = jnp.float32
bf16 = jnp.bfloat16
VMEM = pl.BlockSpec(memory_space=pltpu.VMEM)
SMEM = pl.BlockSpec(memory_space=pltpu.SMEM)


def phase_list(offset):
    return [2.0 * math.pi * freq_hz * (STEP + offset) * TIME_STEP for freq_hz in FREQ_LIST]


def iota(shape, dim):
    return lax.broadcasted_iota(jnp.int32, shape, dim)


def shifted(value, axis, steps):
    count = lax.axis_size(axis)
    leading, last = (max(0, -steps), min(count, count - steps))
    return lax.ppermute(value, axis, [(source, source + steps) for source in range(leading, last)])


def onehot(count, index):
    places = iota((count, index.shape[1]), 0).astype(bf16)
    return jnp.where(places == index.astype(bf16), jnp.ones((), bf16), jnp.zeros((), bf16))


def field_kernel(
    e_ref, h_ref, j_ref, kind_ref, table_ref, dft_e_ref, dft_h_ref, row_ref, col_ref,
    e_out, j_out, dft_e_out, dft_h_out, flux_out, below_ref, wide_ref,
):
    z = pl.program_id(0)

    @pl.when(z == 0)
    def _():
        below_ref[...] = jnp.zeros_like(below_ref)
        wide_ref[...] = jnp.zeros_like(wide_ref)
        wide_ref[0:4, 0:32] = table_ref[...]

    rows, cols = kind_ref.shape[1:]
    hx, hy, hz = h_ref[0, 0], h_ref[1, 0], h_ref[2, 0]
    first_row = iota((rows, cols), 0) == 0
    first_col = iota((rows, cols), 1) == 0
    diagonal = iota((rows, rows), 0) == iota((rows, rows), 1)

    def below_x(field, part):
        halo = row_ref[part, pl.ds(z, 1), :]
        return jnp.where(first_row, halo, pltpu.roll(field, 1, 0))

    def below_y(field, part):
        halo = col_ref[part, pl.ds(z, 1), :]
        halo = jnp.sum(jnp.where(diagonal, halo, 0.0), axis=1, keepdims=True)
        return jnp.where(first_col, halo, pltpu.roll(field, 1, 1))

    curl = (
        (hz - below_y(hz, 1)) - (hy - below_ref[1]),
        (hx - below_ref[0]) - (hz - below_x(hz, 1)),
        (hy - below_x(hy, 0)) - (hx - below_y(hx, 0)),
    )
    kinds = kind_ref[0]
    coeffs = [
        jnp.take_along_axis(
            jnp.broadcast_to(wide_ref[r : r + 1, :], (rows, cols)), kinds, axis=1
        )
        for r in range(4)
    ]
    e_next = []
    for c in range(3):
        old_e, old_j = e_ref[c, 0], j_ref[c, 0]
        new_e = coeffs[0] * old_e + coeffs[1] * (curl[c] - old_j)
        e_out[c, 0] = new_e
        j_out[c, 0] = coeffs[2] * old_j + coeffs[3] * (new_e - old_e)
        e_next.append(new_e)
    field_h = (hx, hy, hz)
    phase_e, phase_h = phase_list(0.0), phase_list(0.5)
    half_plane = pl.ds(pl.multiple_of((z // 2) * cols, cols), cols)
    rest_plane = pl.ds(pl.multiple_of((z // 2) * cols + 2 * cols, cols), cols)
    for f in range(3):
        spec_e, spec_h = [], []
        for part in range(2):
            factor_e = math.cos(phase_e[f]) if part == 0 else -math.sin(phase_e[f])
            factor_h = math.cos(phase_h[f]) if part == 0 else -math.sin(phase_h[f])
            now_e = [dft_e_ref[f, part, c, 0] + e_next[c] * factor_e for c in range(3)]
            now_h = [dft_h_ref[f, part, c, 0] + field_h[c] * factor_h for c in range(3)]
            for c in range(3):
                dft_e_out[f, part, c, 0] = now_e[c]
                dft_h_out[f, part, c, 0] = now_h[c]
            spec_e.append(now_e)
            spec_h.append(now_h)
        for c in range(3):
            a, b = (c + 1) % 3, (c + 2) % 3
            flux = 0.5 * (
                (spec_e[0][a] * spec_h[0][b] - spec_e[0][b] * spec_h[0][a])
                + (spec_e[1][a] * spec_h[1][b] - spec_e[1][b] * spec_h[1][a])
            )
            head = flux.astype(bf16)
            flux_out[3 * f + c, z % 2, :, half_plane] = head
            flux_out[3 * f + c, z % 2, :, rest_plane] = (flux - head.astype(f32)).astype(bf16)
    below_ref[0] = hx
    below_ref[1] = hy


def field_step(e, h, j, kinds, table, dft_e, dft_h, rows_below, cols_left):
    planes, rows, cols = kinds.shape
    plane3 = pl.BlockSpec((3, 1, rows, cols), lambda z: (0, z, 0, 0))
    spectra = pl.BlockSpec((3, 2, 3, 1, rows, cols), lambda z: (0, 0, 0, z, 0, 0))

    def whole(shape):
        return pl.BlockSpec(shape, lambda z: (0,) * len(shape))

    flux_shape = (9, 2, rows, 4 * cols)
    return pl.pallas_call(
        field_kernel,
        grid=(planes,),
        out_shape=(
            jax.ShapeDtypeStruct(e.shape, f32),
            jax.ShapeDtypeStruct(e.shape, f32),
            jax.ShapeDtypeStruct(dft_e.shape, f32),
            jax.ShapeDtypeStruct(dft_h.shape, f32),
            jax.ShapeDtypeStruct(flux_shape, bf16),
        ),
        in_specs=[
            plane3, plane3, plane3,
            pl.BlockSpec((1, rows, cols), lambda z: (z, 0, 0)),
            whole(table.shape), spectra, spectra,
            whole(rows_below.shape), whole(cols_left.shape),
        ],
        out_specs=(plane3, plane3, spectra, spectra, whole(flux_shape)),
        scratch_shapes=[pltpu.VMEM((2, rows, cols), f32), pltpu.VMEM((8, cols), f32)],
        compiler_params=pltpu.CompilerParams(vmem_limit_bytes=20 << 20),
        name="field_step",
    )(e, h, j, kinds, table, dft_e, dft_h, rows_below, cols_left)


def gather_kernel(count_ref, cell_ref, table_ref, out_ref, packed, found):
    lane = iota((1, 128), 1)

    def pack(d, carry):
        offset, current = carry
        row, start = lax.shift_right_logical(offset, 7), lax.bitwise_and(offset, 127)
        live = count_ref[0, d]
        rolled = pltpu.roll(cell_ref[0, pl.ds(d, 1), :], start, 1)
        merged = jnp.where(lane >= start, rolled, current)
        packed[pl.ds(row, 1), :] = merged
        return offset + live, jnp.where(start + live >= 128, rolled, merged)

    offset, current = lax.fori_loop(
        0, 128, pack, (jnp.int32(0), jnp.zeros((1, 128), jnp.int32)), unroll=32
    )
    packed[pl.ds(lax.shift_right_logical(offset, 7), 1), :] = current

    def lookup(c):
        cell = jnp.concatenate([packed[pl.ds(2 * c, 1), :], packed[pl.ds(2 * c + 1, 1), :]], 1)
        high = lax.bitwise_and(lax.shift_right_logical(cell, 14), 1)
        inner = lax.bitwise_or(lax.shift_left(high, 7), lax.bitwise_and(cell, 127))
        outer = lax.bitwise_and(lax.shift_right_logical(cell, 7), 127)
        hot = onehot(256, inner)
        result = jnp.dot(
            table_ref[...].reshape(1152, 512),
            jnp.concatenate([hot, hot], 0),
            preferred_element_type=f32,
        ).reshape(9, 128, 256)
        mine = iota((128, 256), 0) == outer
        for q in range(9):
            value = jnp.sum(jnp.where(mine, result[q], 0.0), axis=0, keepdims=True)
            found[2 * c, q : q + 1, :] = value[:, :128]
            found[2 * c + 1, q : q + 1, :] = value[:, 128:]

    def chunk(c, _):
        for part in range(4):
            lookup(4 * c + part)
        return 0

    lax.fori_loop(0, lax.shift_right_logical(offset + 1023, 10), chunk, 0)
    lanes = iota((16, 128), 1)

    def unpack(d, offset):
        row, start = lax.shift_right_logical(offset, 7), lax.bitwise_and(offset, 127)
        live = count_ref[0, d]
        back = lax.bitwise_and(128 - start, 127)
        value = jnp.where(
            lanes < 128 - start, pltpu.roll(found[row], back, 1), pltpu.roll(found[row + 1], back, 1)
        )
        value = jnp.where(lanes < live, value, 0.0)
        for q in range(9):
            out_ref[d, q] = value[q : q + 1, :]
        return offset + live

    lax.fori_loop(0, 128, unpack, jnp.int32(0), unroll=16)


def gather_flux(counts, cells, table):
    return pl.pallas_call(
        gather_kernel,
        out_shape=jax.ShapeDtypeStruct((128, 9, 1, 128), f32),
        in_specs=[SMEM, VMEM, VMEM],
        out_specs=VMEM,
        scratch_shapes=[pltpu.VMEM((136, 128), jnp.int32), pltpu.VMEM((136, 16, 128), f32)],
        compiler_params=pltpu.CompilerParams(vmem_limit_bytes=24 << 20),
        name="gather_flux",
    )(counts, cells, table)


GROUP = 8


def slot_row(ref, c):
    return jnp.concatenate([ref[0, pl.ds(GROUP * c + i, 1), :] for i in range(GROUP)], 1)


def area_kernel(patch_ref, area_ref, out_ref, table, *, first):
    area = area_ref[...].reshape(768, 256)
    head = area.astype(bf16)
    table[:, :256] = head
    table[:, 256:] = (area - head.astype(f32)).astype(bf16)

    def chunk(c, _):
        patch = slot_row(patch_ref, c + first)
        u, v = lax.shift_right_logical(patch, 8), lax.bitwise_and(patch, 255)
        hot = onehot(256, v)
        result = jnp.dot(
            table[...], jnp.concatenate([hot, hot], 0), preferred_element_type=f32
        ).reshape(3, 256, GROUP * 128)
        mine = iota((256, GROUP * 128), 0) == u
        for q in range(3):
            out_ref[c, q : q + 1, :] = jnp.sum(
                jnp.where(mine, result[q], 0.0), axis=0, keepdims=True
            )
        return 0

    lax.fori_loop(0, out_ref.shape[0], chunk, 0, unroll=4)


def gather_area(patch, area, first, groups):
    return pl.pallas_call(
        functools.partial(area_kernel, first=first),
        out_shape=jax.ShapeDtypeStruct((groups, 8, GROUP * 128), f32),
        in_specs=[VMEM, VMEM],
        out_specs=VMEM,
        scratch_shapes=[pltpu.VMEM((768, 512), bf16)],
        compiler_params=pltpu.CompilerParams(vmem_limit_bytes=32 << 20),
        cost_estimate=pl.CostEstimate(
            flops=2 * 768 * 512 * GROUP * 128 * groups, bytes_accessed=2000000, transcendentals=0
        ),
        name="gather_area",
    )(patch, area)


EDGE = 104


def scatter_kernel(
    patch_ref, area_a_ref, area_b_ref, flux_ref, out_ref, copy_ref, head_ref, tail_ref
):
    out_ref[...] = jnp.zeros_like(out_ref)

    def add_group(c, area):
        patch = slot_row(patch_ref, c)
        u, v = lax.shift_right_logical(patch, 8), lax.bitwise_and(patch, 255)
        hot = onehot(256, v)
        mine = iota((256, GROUP * 128), 0).astype(bf16) == u.astype(bf16)
        heads, rests = [], []
        for f in range(3):
            density = jnp.zeros((1, GROUP * 128), f32)
            for q in range(3):
                flux = jnp.concatenate(
                    [flux_ref[GROUP * c + i, 3 * f + q] for i in range(GROUP)], 1
                )
                density = density + area[q : q + 1, :] * flux
            head = density.astype(bf16)
            rest = (density - head.astype(f32)).astype(bf16)
            heads.append(jnp.where(mine, head, jnp.zeros((), bf16)))
            rests.append(jnp.where(mine, rest, jnp.zeros((), bf16)))
        left = jnp.concatenate([jnp.concatenate(heads, 0), jnp.concatenate(rests, 0)], 1)
        right = jnp.concatenate([hot, hot], 1)
        out_ref[...] += lax.dot_general(
            left, right, (((1,), (1,)), ((), ())), preferred_element_type=f32
        ).reshape(3, 256, 256)

    half = area_a_ref.shape[0]

    def first_half(c, _):
        add_group(c, area_a_ref[c])
        return 0

    def second_half(c, _):
        add_group(c + half, area_b_ref[c])
        return 0

    lax.fori_loop(0, half, first_half, 0, unroll=4)
    lax.fori_loop(0, area_b_ref.shape[0], second_half, 0, unroll=4)
    copy_ref[...] = out_ref[...]
    head_ref[...] = out_ref[:, :EDGE, :]
    tail_ref[...] = out_ref[:, 256 - EDGE :, :]


BLOCK_AND_EDGES = (
    jax.ShapeDtypeStruct((3, 256, 256), f32),
    jax.ShapeDtypeStruct((3, EDGE, 256), f32),
    jax.ShapeDtypeStruct((3, EDGE, 256), f32),
)


def scatter_density(patch, area_a, area_b, flux):
    return pl.pallas_call(
        scatter_kernel,
        out_shape=BLOCK_AND_EDGES[:1] + BLOCK_AND_EDGES,
        in_specs=[VMEM] * 4,
        out_specs=(VMEM,) * 4,
        compiler_params=pltpu.CompilerParams(vmem_limit_bytes=40 << 20),
        name="scatter_density",
    )(patch, area_a, area_b, flux)


def window_kernel(block_ref, before_ref, after_ref, out_ref, *edges, scale):
    length = 256 + 2 * EDGE
    place = iota((length, 256), 0) - EDGE - iota((length, 256), 1)
    band = jnp.where((place >= -HALF) & (place < HALF), 1.0, 0.0).astype(bf16)
    for f in range(3):
        cells = jnp.concatenate([before_ref[f], block_ref[f], after_ref[f]], 0)
        head = cells.astype(bf16)
        rest = (cells - head.astype(f32)).astype(bf16)
        total = lax.dot_general(
            jnp.concatenate([head, rest], 0),
            jnp.concatenate([band, band], 0),
            (((0,), (0,)), ((), ())),
            preferred_element_type=f32,
        )
        if scale != 1.0:
            total = total * scale
        out_ref[f] = total
        if edges:
            edges[0][f] = total[:EDGE]
            edges[1][f] = total[256 - EDGE :]


def window_sum(block, before, after, scale, with_edges):
    count = 3 if with_edges else 1
    return pl.pallas_call(
        functools.partial(window_kernel, scale=scale),
        out_shape=BLOCK_AND_EDGES[:count],
        in_specs=[VMEM] * 3,
        out_specs=(VMEM,) * count,
        compiler_params=pltpu.CompilerParams(vmem_limit_bytes=16 << 20),
        name="window_sum",
    )(block, before, after)


def shards(
    e_field, h_field, j_field, material, material_table, dft_e, dft_h, skin_cell, counts,
    patch_slot, area,
):
    magnet_x, magnet_y, magnet_z = (h_field[0], h_field[1], h_field[2])
    rows_below = shifted(jnp.stack([magnet_y[:, -1, :], magnet_z[:, -1, :]]), "gy", 1)
    cols_left = shifted(jnp.stack([magnet_x[:, :, -1], magnet_z[:, :, -1]]), "gx", 1)
    area_a = gather_area(patch_slot, area, 0, 6)
    rows_below, cols_left, area_a = lax.optimization_barrier((rows_below, cols_left, area_a))
    e_next, j_next, dft_e_next, dft_h_next, table = field_step(
        e_field, h_field, j_field, material, material_table, dft_e, dft_h, rows_below, cols_left
    )
    rows = gather_flux(counts, skin_cell, table.reshape(9, 128, 512))
    arrived = lax.all_to_all(rows, ("gy", "gx"), split_axis=0, concat_axis=0, tiled=True)
    area_b = gather_area(patch_slot, area, 6, 10)
    point_density, block, head, tail = scatter_density(patch_slot, area_a, area_b, arrived)
    before, after = shifted(tail, "gy", 1), shifted(head, "gy", -1)
    strip_sum, head, tail = window_sum(block, before, after, 1.0, True)
    before, after = shifted(tail, "gx", 1), shifted(head, "gx", -1)
    (avg_density,) = window_sum(strip_sum, before, after, 1.0 / (4.0 * HALF * HALF), False)
    return (e_next, j_next, dft_e_next, dft_h_next, point_density, avg_density)


def solution(mesh):
    placed = (
        P(None, None, "gy", "gx"),
        P(None, None, "gy", "gx"),
        P(None, None, "gy", "gx"),
        P(None, "gy", "gx"),
        P(),
        P(None, None, None, None, "gy", "gx"),
        P(None, None, None, None, "gy", "gx"),
        P(("gy", "gx"), None, None),
        P(("gy", "gx"), None),
        P(("gy", "gx"), None, None),
        P(None, "gy", "gx"),
    )
    return jax.shard_map(
        shards,
        mesh=mesh,
        in_specs=placed,
        out_specs=(
            P(None, None, "gy", "gx"),
            P(None, None, "gy", "gx"),
            P(None, None, None, None, "gy", "gx"),
            P(None, None, None, None, "gy", "gx"),
            P(None, "gy", "gx"),
            P(None, "gy", "gx"),
        ),
        check_vma=False,
    )
```

```python
import functools
import math

import jax
import jax.numpy as jnp
from jax import lax
from jax.experimental import pallas as pl
from jax.experimental.pallas import tpu as pltpu
from jax.sharding import PartitionSpec as P

STEP = 1000
HALF = 100
FREQ_LIST = (28000000000.0, 39000000000.0, 60000000000.0)
TIME_STEP = 1.9e-13

f32 = jnp.float32
bf16 = jnp.bfloat16
VMEM = pl.BlockSpec(memory_space=pltpu.VMEM)
SMEM = pl.BlockSpec(memory_space=pltpu.SMEM)


def phase_list(offset):
    return [2.0 * math.pi * freq_hz * (STEP + offset) * TIME_STEP for freq_hz in FREQ_LIST]


def iota(shape, dim):
    return lax.broadcasted_iota(jnp.int32, shape, dim)


def shifted(value, axis, steps):
    count = lax.axis_size(axis)
    leading, last = (max(0, -steps), min(count, count - steps))
    return lax.ppermute(value, axis, [(source, source + steps) for source in range(leading, last)])


def onehot(count, index):
    places = iota((count, index.shape[1]), 0).astype(bf16)
    return jnp.where(places == index.astype(bf16), jnp.ones((), bf16), jnp.zeros((), bf16))


def field_kernel(
    e_ref, h_ref, j_ref, kind_ref, table_ref, dft_e_ref, dft_h_ref, row_ref, col_ref,
    e_out, j_out, dft_e_out, dft_h_out, flux_out, below_ref, wide_ref,
):
    z = pl.program_id(0)

    @pl.when(z == 0)
    def _():
        below_ref[...] = jnp.zeros_like(below_ref)
        wide_ref[...] = jnp.zeros_like(wide_ref)
        wide_ref[0:4, 0:32] = table_ref[...]

    rows, cols = kind_ref.shape[1:]
    hx, hy, hz = h_ref[0, 0], h_ref[1, 0], h_ref[2, 0]
    first_row = iota((rows, cols), 0) == 0
    first_col = iota((rows, cols), 1) == 0
    diagonal = iota((rows, rows), 0) == iota((rows, rows), 1)

    def below_x(field, part):
        halo = row_ref[part, pl.ds(z, 1), :]
        return jnp.where(first_row, halo, pltpu.roll(field, 1, 0))

    def below_y(field, part):
        halo = col_ref[part, pl.ds(z, 1), :]
        halo = jnp.sum(jnp.where(diagonal, halo, 0.0), axis=1, keepdims=True)
        return jnp.where(first_col, halo, pltpu.roll(field, 1, 1))

    curl = (
        (hz - below_y(hz, 1)) - (hy - below_ref[1]),
        (hx - below_ref[0]) - (hz - below_x(hz, 1)),
        (hy - below_x(hy, 0)) - (hx - below_y(hx, 0)),
    )
    kinds = kind_ref[0]
    coeffs = [
        jnp.take_along_axis(
            jnp.broadcast_to(wide_ref[r : r + 1, :], (rows, cols)), kinds, axis=1
        )
        for r in range(4)
    ]
    e_next = []
    for c in range(3):
        old_e, old_j = e_ref[c, 0], j_ref[c, 0]
        new_e = coeffs[0] * old_e + coeffs[1] * (curl[c] - old_j)
        e_out[c, 0] = new_e
        j_out[c, 0] = coeffs[2] * old_j + coeffs[3] * (new_e - old_e)
        e_next.append(new_e)
    field_h = (hx, hy, hz)
    phase_e, phase_h = phase_list(0.0), phase_list(0.5)
    half_plane = pl.ds(pl.multiple_of((z // 2) * cols, cols), cols)
    rest_plane = pl.ds(pl.multiple_of((z // 2) * cols + 2 * cols, cols), cols)
    for f in range(3):
        spec_e, spec_h = [], []
        for part in range(2):
            factor_e = math.cos(phase_e[f]) if part == 0 else -math.sin(phase_e[f])
            factor_h = math.cos(phase_h[f]) if part == 0 else -math.sin(phase_h[f])
            now_e = [dft_e_ref[f, part, c, 0] + e_next[c] * factor_e for c in range(3)]
            now_h = [dft_h_ref[f, part, c, 0] + field_h[c] * factor_h for c in range(3)]
            for c in range(3):
                dft_e_out[f, part, c, 0] = now_e[c]
                dft_h_out[f, part, c, 0] = now_h[c]
            spec_e.append(now_e)
            spec_h.append(now_h)
        for c in range(3):
            a, b = (c + 1) % 3, (c + 2) % 3
            flux = 0.5 * (
                (spec_e[0][a] * spec_h[0][b] - spec_e[0][b] * spec_h[0][a])
                + (spec_e[1][a] * spec_h[1][b] - spec_e[1][b] * spec_h[1][a])
            )
            head = flux.astype(bf16)
            flux_out[3 * f + c, z % 2, :, half_plane] = head
            flux_out[3 * f + c, z % 2, :, rest_plane] = (flux - head.astype(f32)).astype(bf16)
    below_ref[0] = hx
    below_ref[1] = hy


def field_step(e, h, j, kinds, table, dft_e, dft_h, rows_below, cols_left):
    planes, rows, cols = kinds.shape
    plane3 = pl.BlockSpec((3, 1, rows, cols), lambda z: (0, z, 0, 0))
    spectra = pl.BlockSpec((3, 2, 3, 1, rows, cols), lambda z: (0, 0, 0, z, 0, 0))

    def whole(shape):
        return pl.BlockSpec(shape, lambda z: (0,) * len(shape))

    flux_shape = (9, 2, rows, 4 * cols)
    return pl.pallas_call(
        field_kernel,
        grid=(planes,),
        out_shape=(
            jax.ShapeDtypeStruct(e.shape, f32),
            jax.ShapeDtypeStruct(e.shape, f32),
            jax.ShapeDtypeStruct(dft_e.shape, f32),
            jax.ShapeDtypeStruct(dft_h.shape, f32),
            jax.ShapeDtypeStruct(flux_shape, bf16),
        ),
        in_specs=[
            plane3, plane3, plane3,
            pl.BlockSpec((1, rows, cols), lambda z: (z, 0, 0)),
            whole(table.shape), spectra, spectra,
            whole(rows_below.shape), whole(cols_left.shape),
        ],
        out_specs=(plane3, plane3, spectra, spectra, whole(flux_shape)),
        scratch_shapes=[pltpu.VMEM((2, rows, cols), f32), pltpu.VMEM((8, cols), f32)],
        compiler_params=pltpu.CompilerParams(vmem_limit_bytes=20 << 20),
        name="field_step",
    )(e, h, j, kinds, table, dft_e, dft_h, rows_below, cols_left)


def gather_kernel(count_ref, offset_ref, packed, table_ref, out_ref, found):
    def lookup(c):
        cell = jnp.concatenate([packed[pl.ds(2 * c, 1), :], packed[pl.ds(2 * c + 1, 1), :]], 1)
        high = lax.bitwise_and(lax.shift_right_logical(cell, 14), 1)
        inner = lax.bitwise_or(lax.shift_left(high, 7), lax.bitwise_and(cell, 127))
        outer = lax.bitwise_and(lax.shift_right_logical(cell, 7), 127)
        hot = onehot(256, inner)
        result = jnp.dot(
            table_ref[...].reshape(1152, 512),
            jnp.concatenate([hot, hot], 0),
            preferred_element_type=f32,
        ).reshape(9, 128, 256)
        mine = iota((128, 256), 0) == outer
        for q in range(9):
            value = jnp.sum(jnp.where(mine, result[q], 0.0), axis=0, keepdims=True)
            found[2 * c, q : q + 1, :] = value[:, :128]
            found[2 * c + 1, q : q + 1, :] = value[:, 128:]

    def chunk(c, _):
        for part in range(4):
            lookup(4 * c + part)
        return 0

    lax.fori_loop(0, lax.shift_right_logical(offset_ref[0, 128] + 1023, 10), chunk, 0)
    lanes = iota((16, 128), 1)

    def unpack(d, _):
        offset = offset_ref[0, d]
        row, start = lax.shift_right_logical(offset, 7), lax.bitwise_and(offset, 127)
        live = count_ref[0, d]
        back = lax.bitwise_and(128 - start, 127)
        value = jnp.where(
            lanes < 128 - start, pltpu.roll(found[row], back, 1), pltpu.roll(found[row + 1], back, 1)
        )
        value = jnp.where(lanes < live, value, 0.0)
        for q in range(9):
            out_ref[d, q] = value[q : q + 1, :]
        return 0

    lax.fori_loop(0, 128, unpack, 0, unroll=16)


def gather_flux(counts, offsets, packed, table):
    return pl.pallas_call(
        gather_kernel,
        out_shape=jax.ShapeDtypeStruct((128, 9, 1, 128), f32),
        in_specs=[SMEM, SMEM, VMEM, VMEM],
        out_specs=VMEM,
        scratch_shapes=[pltpu.VMEM((136, 16, 128), f32)],
        compiler_params=pltpu.CompilerParams(vmem_limit_bytes=24 << 20),
        name="gather_flux",
    )(counts, offsets, packed, table)


GROUP = 8


def slot_row(ref, c):
    return jnp.concatenate([ref[0, pl.ds(GROUP * c + i, 1), :] for i in range(GROUP)], 1)


def split_area(area_ref, table):
    area = area_ref[...].reshape(768, 256)
    head = area.astype(bf16)
    table[:, :256] = head
    table[:, 256:] = (area - head.astype(f32)).astype(bf16)


def area_group(patch_ref, table, out_ref, c, first):
    patch = slot_row(patch_ref, c + first)
    u, v = lax.shift_right_logical(patch, 8), lax.bitwise_and(patch, 255)
    hot = onehot(256, v)
    result = jnp.dot(
        table[...], jnp.concatenate([hot, hot], 0), preferred_element_type=f32
    ).reshape(3, 256, GROUP * 128)
    mine = iota((256, GROUP * 128), 0) == u
    for q in range(3):
        out_ref[c, q : q + 1, :] = jnp.sum(jnp.where(mine, result[q], 0.0), axis=0, keepdims=True)


def first_area_kernel(
    count_ref, cell_ref, patch_ref, area_ref, out_ref, packed, offset_ref, table, *, groups
):
    split_area(area_ref, table)
    lane = iota((1, 128), 1)
    share = 128 // groups

    def chunk(c, carry):
        offset, current = carry
        for i in range(share):
            d = c * share + i
            row, start = lax.shift_right_logical(offset, 7), lax.bitwise_and(offset, 127)
            live = count_ref[0, d]
            offset_ref[0, d] = offset
            rolled = pltpu.roll(cell_ref[0, pl.ds(d, 1), :], start, 1)
            merged = jnp.where(lane >= start, rolled, current)
            packed[pl.ds(row, 1), :] = merged
            current = jnp.where(start + live >= 128, rolled, merged)
            offset = offset + live
        area_group(patch_ref, table, out_ref, c, 0)
        return offset, current

    offset, current = lax.fori_loop(
        0, groups, chunk, (jnp.int32(0), jnp.zeros((1, 128), jnp.int32)), unroll=2
    )
    packed[pl.ds(lax.shift_right_logical(offset, 7), 1), :] = current
    offset_ref[0, 128] = offset


def area_kernel(patch_ref, area_ref, out_ref, table, *, first):
    split_area(area_ref, table)

    def chunk(c, _):
        area_group(patch_ref, table, out_ref, c, first)
        return 0

    lax.fori_loop(0, out_ref.shape[0], chunk, 0, unroll=4)


def area_cost(groups):
    return pl.CostEstimate(
        flops=2 * 768 * 512 * GROUP * 128 * groups, bytes_accessed=2000000, transcendentals=0
    )


def gather_area_and_pack(counts, cells, patch, area, groups):
    return pl.pallas_call(
        functools.partial(first_area_kernel, groups=groups),
        out_shape=(
            jax.ShapeDtypeStruct((groups, 8, GROUP * 128), f32),
            jax.ShapeDtypeStruct((136, 128), jnp.int32),
            jax.ShapeDtypeStruct((1, 136), jnp.int32),
        ),
        in_specs=[SMEM, VMEM, VMEM, VMEM],
        out_specs=(VMEM, VMEM, SMEM),
        scratch_shapes=[pltpu.VMEM((768, 512), bf16)],
        compiler_params=pltpu.CompilerParams(vmem_limit_bytes=32 << 20),
        cost_estimate=area_cost(groups),
        name="area_and_pack",
    )(counts, cells, patch, area)


def gather_area(patch, area, first, groups):
    return pl.pallas_call(
        functools.partial(area_kernel, first=first),
        out_shape=jax.ShapeDtypeStruct((groups, 8, GROUP * 128), f32),
        in_specs=[VMEM, VMEM],
        out_specs=VMEM,
        scratch_shapes=[pltpu.VMEM((768, 512), bf16)],
        compiler_params=pltpu.CompilerParams(vmem_limit_bytes=32 << 20),
        cost_estimate=area_cost(groups),
        name="gather_area",
    )(patch, area)


EDGE = 104


def scatter_kernel(
    patch_ref, area_a_ref, area_b_ref, flux_ref, out_ref, head_ref, tail_ref, *, first
):
    freqs = out_ref.shape[0]
    out_ref[...] = jnp.zeros_like(out_ref)

    def add_group(c, area):
        patch = slot_row(patch_ref, c)
        u, v = lax.shift_right_logical(patch, 8), lax.bitwise_and(patch, 255)
        hot = onehot(256, v)
        mine = iota((256, GROUP * 128), 0).astype(bf16) == u.astype(bf16)
        heads, rests = [], []
        for f in range(first, first + freqs):
            density = jnp.zeros((1, GROUP * 128), f32)
            for q in range(3):
                flux = jnp.concatenate(
                    [flux_ref[GROUP * c + i, 3 * f + q] for i in range(GROUP)], 1
                )
                density = density + area[q : q + 1, :] * flux
            head = density.astype(bf16)
            rest = (density - head.astype(f32)).astype(bf16)
            heads.append(jnp.where(mine, head, jnp.zeros((), bf16)))
            rests.append(jnp.where(mine, rest, jnp.zeros((), bf16)))
        left = jnp.concatenate([jnp.concatenate(heads, 0), jnp.concatenate(rests, 0)], 1)
        right = jnp.concatenate([hot, hot], 1)
        out_ref[...] += lax.dot_general(
            left, right, (((1,), (1,)), ((), ())), preferred_element_type=f32
        ).reshape(freqs, 256, 256)

    half = area_a_ref.shape[0]

    def first_part(c, _):
        add_group(c, area_a_ref[c])
        return 0

    def second_part(c, _):
        add_group(c + half, area_b_ref[c])
        return 0

    lax.fori_loop(0, half, first_part, 0, unroll=4)
    lax.fori_loop(0, area_b_ref.shape[0], second_part, 0, unroll=4)
    for f in range(freqs):
        head_ref[f] = jnp.transpose(out_ref[f, :, :128])[:EDGE]
        tail_ref[f] = jnp.transpose(out_ref[f, :, 128:])[128 - EDGE :]


def block_and_edges(freqs):
    return (
        jax.ShapeDtypeStruct((freqs, 256, 256), f32),
        jax.ShapeDtypeStruct((freqs, EDGE, 256), f32),
        jax.ShapeDtypeStruct((freqs, EDGE, 256), f32),
    )


def scatter_density(patch, area_a, area_b, flux, first, freqs):
    return pl.pallas_call(
        functools.partial(scatter_kernel, first=first),
        out_shape=block_and_edges(freqs),
        in_specs=[VMEM] * 4,
        out_specs=(VMEM,) * 3,
        compiler_params=pltpu.CompilerParams(vmem_limit_bytes=36 << 20),
        cost_estimate=pl.CostEstimate(
            flops=2 * freqs * 65536 * 2 * 16384, bytes_accessed=2000000, transcendentals=0
        ),
        name="scatter_density",
    )(patch, area_a, area_b, flux)


def in_window(place):
    return jnp.where((place >= -HALF) & (place < HALF), 1.0, 0.0).astype(bf16)


def two_parts(cells):
    head = cells.astype(bf16)
    return head, (cells - head.astype(f32)).astype(bf16)


def column_kernel(block_ref, before_ref, after_ref, out_ref, head_ref, tail_ref):
    inner = in_window(iota((256, 256), 0) - iota((256, 256), 1))
    place, column = iota((EDGE, 256), 0), iota((EDGE, 256), 1)
    outer = jnp.concatenate(
        [in_window(place - EDGE - column), in_window(place + 256 - column)], 0
    )
    inner = jnp.concatenate([inner, inner], 0)
    outer = jnp.concatenate([outer, outer], 0)
    for f in range(out_ref.shape[0]):
        total = jnp.dot(
            jnp.concatenate(two_parts(block_ref[f]), 1), inner, preferred_element_type=f32
        )
        edges = jnp.concatenate([before_ref[f], after_ref[f]], 0)
        total = total + lax.dot_general(
            jnp.concatenate(two_parts(edges), 0),
            outer,
            (((0,), (0,)), ((), ())),
            preferred_element_type=f32,
        )
        out_ref[f] = total
        head_ref[f] = total[:EDGE]
        tail_ref[f] = total[256 - EDGE :]


def column_sum(block, before, after):
    freqs = block.shape[0]
    return pl.pallas_call(
        column_kernel,
        out_shape=block_and_edges(freqs),
        in_specs=[VMEM] * 3,
        out_specs=(VMEM,) * 3,
        compiler_params=pltpu.CompilerParams(vmem_limit_bytes=16 << 20),
        name="column_sum",
    )(block, before, after)


def row_kernel(*refs):
    out_ref = refs[-1]
    length = 256 + 2 * EDGE
    band = in_window(iota((256, length), 1) - EDGE - iota((256, length), 0))
    band = jnp.concatenate([band, band], 1)
    done = 0
    for block_ref, before_ref, after_ref in zip(refs[0:-1:3], refs[1:-1:3], refs[2:-1:3]):
        for f in range(block_ref.shape[0]):
            cells = jnp.concatenate([before_ref[f], block_ref[f], after_ref[f]], 0)
            total = jnp.dot(
                band, jnp.concatenate(two_parts(cells), 0), preferred_element_type=f32
            )
            out_ref[done] = total * (1.0 / (4.0 * HALF * HALF))
            done += 1


def row_sum(*pieces):
    return pl.pallas_call(
        row_kernel,
        out_shape=jax.ShapeDtypeStruct((3, 256, 256), f32),
        in_specs=[VMEM] * len(pieces),
        out_specs=VMEM,
        compiler_params=pltpu.CompilerParams(vmem_limit_bytes=16 << 20),
        name="row_sum",
    )(*pieces)


def shards(
    e_field, h_field, j_field, material, material_table, dft_e, dft_h, skin_cell, counts,
    patch_slot, area,
):
    magnet_x, magnet_y, magnet_z = (h_field[0], h_field[1], h_field[2])
    rows_below = shifted(jnp.stack([magnet_y[:, -1, :], magnet_z[:, -1, :]]), "gy", 1)
    cols_left = shifted(jnp.stack([magnet_x[:, :, -1], magnet_z[:, :, -1]]), "gx", 1)
    area_a, packed, offsets = gather_area_and_pack(counts, skin_cell, patch_slot, area, 4)
    rows_below, cols_left, area_a = lax.optimization_barrier((rows_below, cols_left, area_a))
    e_next, j_next, dft_e_next, dft_h_next, table = field_step(
        e_field, h_field, j_field, material, material_table, dft_e, dft_h, rows_below, cols_left
    )
    rows = gather_flux(counts, offsets, packed, table.reshape(9, 128, 512))
    arrived = lax.all_to_all(rows, ("gy", "gx"), split_axis=0, concat_axis=0, tiled=True)
    area_b = gather_area(patch_slot, area, 4, 12)

    blocks, pieces = [], []
    edges = []
    for first, freqs in ((0, 2), (2, 1)):
        block, head, tail = scatter_density(patch_slot, area_a, area_b, arrived, first, freqs)
        blocks.append(block)
        edges.append((shifted(tail, "gx", 1), shifted(head, "gx", -1)))
    for block, (before, after) in zip(blocks, edges):
        strip, head, tail = column_sum(block, before, after)
        pieces += [strip, shifted(tail, "gy", 1), shifted(head, "gy", -1)]
    point_density = jnp.concatenate(blocks, 0)
    avg_density = row_sum(*pieces)
    return (e_next, j_next, dft_e_next, dft_h_next, point_density, avg_density)


def solution(mesh):
    placed = (
        P(None, None, "gy", "gx"),
        P(None, None, "gy", "gx"),
        P(None, None, "gy", "gx"),
        P(None, "gy", "gx"),
        P(),
        P(None, None, None, None, "gy", "gx"),
        P(None, None, None, None, "gy", "gx"),
        P(("gy", "gx"), None, None),
        P(("gy", "gx"), None),
        P(("gy", "gx"), None, None),
        P(None, "gy", "gx"),
    )
    return jax.shard_map(
        shards,
        mesh=mesh,
        in_specs=placed,
        out_specs=(
            P(None, None, "gy", "gx"),
            P(None, None, "gy", "gx"),
            P(None, None, None, None, "gy", "gx"),
            P(None, None, None, None, "gy", "gx"),
            P(None, "gy", "gx"),
            P(None, "gy", "gx"),
        ),
        check_vma=False,
    )
```

```python
import functools
import math

import jax
import jax.numpy as jnp
from jax import lax
from jax.experimental import pallas as pl
from jax.experimental.pallas import tpu as pltpu
from jax.sharding import PartitionSpec as P

STEP = 1000
HALF = 100
FREQ_LIST = (28000000000.0, 39000000000.0, 60000000000.0)
TIME_STEP = 1.9e-13

f32 = jnp.float32
bf16 = jnp.bfloat16
VMEM = pl.BlockSpec(memory_space=pltpu.VMEM)
SMEM = pl.BlockSpec(memory_space=pltpu.SMEM)


def phase_list(offset):
    return [2.0 * math.pi * freq_hz * (STEP + offset) * TIME_STEP for freq_hz in FREQ_LIST]


def iota(shape, dim):
    return lax.broadcasted_iota(jnp.int32, shape, dim)


def shifted(value, axis, steps):
    count = lax.axis_size(axis)
    leading, last = (max(0, -steps), min(count, count - steps))
    return lax.ppermute(value, axis, [(source, source + steps) for source in range(leading, last)])


def exchange(first, second, axis):
    count = lax.axis_size(axis)
    swaps = []
    for start, value in ((0, first), (1, second)):
        lower = range(start, count - 1, 2)
        pairs = [(i, i + 1) for i in lower] + [(i + 1, i) for i in lower]
        swaps.append(lax.ppermute(value, axis, pairs))
    return swaps


def put_edges(odd, head, tail, first_ref, second_ref, f):
    @pl.when(odd == 0)
    def _():
        first_ref[f] = tail
        second_ref[f] = head

    @pl.when(odd != 0)
    def _():
        first_ref[f] = head
        second_ref[f] = tail


def got_edges(odd, first_ref, second_ref, f):
    first, second = first_ref[f], second_ref[f]
    return jnp.where(odd == 0, second, first), jnp.where(odd == 0, first, second)


def onehot(count, index):
    places = iota((count, index.shape[1]), 0).astype(bf16)
    return jnp.where(places == index.astype(bf16), jnp.ones((), bf16), jnp.zeros((), bf16))


def field_kernel(
    e_ref, h_ref, j_ref, kind_ref, table_ref, dft_e_ref, dft_h_ref, row_ref, col_ref,
    e_out, j_out, dft_e_out, dft_h_out, flux_out, below_ref, wide_ref,
):
    z = pl.program_id(0)

    @pl.when(z == 0)
    def _():
        below_ref[...] = jnp.zeros_like(below_ref)
        wide_ref[...] = jnp.zeros_like(wide_ref)
        wide_ref[0:4, 0:32] = table_ref[...]

    rows, cols = kind_ref.shape[1:]
    hx, hy, hz = h_ref[0, 0], h_ref[1, 0], h_ref[2, 0]
    first_row = iota((rows, cols), 0) == 0
    first_col = iota((rows, cols), 1) == 0
    diagonal = iota((rows, rows), 0) == iota((rows, rows), 1)

    def below_x(field, part):
        halo = row_ref[part, pl.ds(z, 1), :]
        return jnp.where(first_row, halo, pltpu.roll(field, 1, 0))

    def below_y(field, part):
        halo = col_ref[part, pl.ds(z, 1), :]
        halo = jnp.sum(jnp.where(diagonal, halo, 0.0), axis=1, keepdims=True)
        return jnp.where(first_col, halo, pltpu.roll(field, 1, 1))

    curl = (
        (hz - below_y(hz, 1)) - (hy - below_ref[1]),
        (hx - below_ref[0]) - (hz - below_x(hz, 1)),
        (hy - below_x(hy, 0)) - (hx - below_y(hx, 0)),
    )
    kinds = kind_ref[0]
    coeffs = [
        jnp.take_along_axis(
            jnp.broadcast_to(wide_ref[r : r + 1, :], (rows, cols)), kinds, axis=1
        )
        for r in range(4)
    ]
    e_next = []
    for c in range(3):
        old_e, old_j = e_ref[c, 0], j_ref[c, 0]
        new_e = coeffs[0] * old_e + coeffs[1] * (curl[c] - old_j)
        e_out[c, 0] = new_e
        j_out[c, 0] = coeffs[2] * old_j + coeffs[3] * (new_e - old_e)
        e_next.append(new_e)
    field_h = (hx, hy, hz)
    phase_e, phase_h = phase_list(0.0), phase_list(0.5)
    half_plane = pl.ds(pl.multiple_of((z // 2) * cols, cols), cols)
    rest_plane = pl.ds(pl.multiple_of((z // 2) * cols + 2 * cols, cols), cols)
    for f in range(3):
        spec_e, spec_h = [], []
        for part in range(2):
            factor_e = math.cos(phase_e[f]) if part == 0 else -math.sin(phase_e[f])
            factor_h = math.cos(phase_h[f]) if part == 0 else -math.sin(phase_h[f])
            now_e = [dft_e_ref[f, part, c, 0] + e_next[c] * factor_e for c in range(3)]
            now_h = [dft_h_ref[f, part, c, 0] + field_h[c] * factor_h for c in range(3)]
            for c in range(3):
                dft_e_out[f, part, c, 0] = now_e[c]
                dft_h_out[f, part, c, 0] = now_h[c]
            spec_e.append(now_e)
            spec_h.append(now_h)
        for c in range(3):
            a, b = (c + 1) % 3, (c + 2) % 3
            flux = 0.5 * (
                (spec_e[0][a] * spec_h[0][b] - spec_e[0][b] * spec_h[0][a])
                + (spec_e[1][a] * spec_h[1][b] - spec_e[1][b] * spec_h[1][a])
            )
            head = flux.astype(bf16)
            flux_out[3 * f + c, z % 2, :, half_plane] = head
            flux_out[3 * f + c, z % 2, :, rest_plane] = (flux - head.astype(f32)).astype(bf16)
    below_ref[0] = hx
    below_ref[1] = hy


def field_step(e, h, j, kinds, table, dft_e, dft_h, rows_below, cols_left):
    planes, rows, cols = kinds.shape
    plane3 = pl.BlockSpec((3, 1, rows, cols), lambda z: (0, z, 0, 0))
    spectra = pl.BlockSpec((3, 2, 3, 1, rows, cols), lambda z: (0, 0, 0, z, 0, 0))

    def whole(shape):
        return pl.BlockSpec(shape, lambda z: (0,) * len(shape))

    flux_shape = (9, 2, rows, 4 * cols)
    return pl.pallas_call(
        field_kernel,
        grid=(planes,),
        out_shape=(
            jax.ShapeDtypeStruct(e.shape, f32),
            jax.ShapeDtypeStruct(e.shape, f32),
            jax.ShapeDtypeStruct(dft_e.shape, f32),
            jax.ShapeDtypeStruct(dft_h.shape, f32),
            jax.ShapeDtypeStruct(flux_shape, bf16),
        ),
        in_specs=[
            plane3, plane3, plane3,
            pl.BlockSpec((1, rows, cols), lambda z: (z, 0, 0)),
            whole(table.shape), spectra, spectra,
            whole(rows_below.shape), whole(cols_left.shape),
        ],
        out_specs=(plane3, plane3, spectra, spectra, whole(flux_shape)),
        scratch_shapes=[pltpu.VMEM((2, rows, cols), f32), pltpu.VMEM((8, cols), f32)],
        compiler_params=pltpu.CompilerParams(vmem_limit_bytes=20 << 20),
        name="field_step",
    )(e, h, j, kinds, table, dft_e, dft_h, rows_below, cols_left)


def gather_kernel(count_ref, offset_ref, packed, table_ref, out_ref, found):
    def lookup(c):
        cell = jnp.concatenate([packed[pl.ds(2 * c, 1), :], packed[pl.ds(2 * c + 1, 1), :]], 1)
        high = lax.bitwise_and(lax.shift_right_logical(cell, 14), 1)
        inner = lax.bitwise_or(lax.shift_left(high, 7), lax.bitwise_and(cell, 127))
        outer = lax.bitwise_and(lax.shift_right_logical(cell, 7), 127)
        hot = onehot(256, inner)
        result = jnp.dot(
            table_ref[...].reshape(1152, 512),
            jnp.concatenate([hot, hot], 0),
            preferred_element_type=f32,
        ).reshape(9, 128, 256)
        mine = iota((128, 256), 0) == outer
        for q in range(9):
            value = jnp.sum(jnp.where(mine, result[q], 0.0), axis=0, keepdims=True)
            found[2 * c, q : q + 1, :] = value[:, :128]
            found[2 * c + 1, q : q + 1, :] = value[:, 128:]

    def chunk(c, _):
        for part in range(4):
            lookup(4 * c + part)
        return 0

    lax.fori_loop(0, lax.shift_right_logical(offset_ref[0, 128] + 1023, 10), chunk, 0)
    lanes = iota((16, 128), 1)

    def unpack(d, _):
        offset = offset_ref[0, d]
        row, start = lax.shift_right_logical(offset, 7), lax.bitwise_and(offset, 127)
        live = count_ref[0, d]
        back = lax.bitwise_and(128 - start, 127)
        value = jnp.where(
            lanes < 128 - start, pltpu.roll(found[row], back, 1), pltpu.roll(found[row + 1], back, 1)
        )
        value = jnp.where(lanes < live, value, 0.0)
        for q in range(9):
            out_ref[d, q] = value[q : q + 1, :]
        return 0

    lax.fori_loop(0, 128, unpack, 0, unroll=16)


def gather_flux(counts, offsets, packed, table):
    return pl.pallas_call(
        gather_kernel,
        out_shape=jax.ShapeDtypeStruct((128, 9, 1, 128), f32),
        in_specs=[SMEM, SMEM, VMEM, VMEM],
        out_specs=VMEM,
        scratch_shapes=[pltpu.VMEM((136, 16, 128), f32)],
        compiler_params=pltpu.CompilerParams(vmem_limit_bytes=24 << 20),
        name="gather_flux",
    )(counts, offsets, packed, table)


GROUP = 8


def slot_row(ref, c):
    return jnp.concatenate([ref[0, pl.ds(GROUP * c + i, 1), :] for i in range(GROUP)], 1)


def split_area(area_ref, table):
    area = area_ref[...].reshape(768, 256)
    head = area.astype(bf16)
    table[:, :256] = head
    table[:, 256:] = (area - head.astype(f32)).astype(bf16)


def area_group(patch_ref, table, out_ref, c, first):
    patch = slot_row(patch_ref, c + first)
    u, v = lax.shift_right_logical(patch, 8), lax.bitwise_and(patch, 255)
    hot = onehot(256, v)
    result = jnp.dot(
        table[...], jnp.concatenate([hot, hot], 0), preferred_element_type=f32
    ).reshape(3, 256, GROUP * 128)
    mine = iota((256, GROUP * 128), 0) == u
    for q in range(3):
        out_ref[c, q : q + 1, :] = jnp.sum(jnp.where(mine, result[q], 0.0), axis=0, keepdims=True)


def first_area_kernel(
    count_ref, cell_ref, patch_ref, area_ref, out_ref, packed, offset_ref, table, *, groups
):
    split_area(area_ref, table)
    lane = iota((1, 128), 1)
    share = 128 // groups

    def chunk(c, carry):
        offset, current = carry
        for i in range(share):
            d = c * share + i
            row, start = lax.shift_right_logical(offset, 7), lax.bitwise_and(offset, 127)
            live = count_ref[0, d]
            offset_ref[0, d] = offset
            rolled = pltpu.roll(cell_ref[0, pl.ds(d, 1), :], start, 1)
            merged = jnp.where(lane >= start, rolled, current)
            packed[pl.ds(row, 1), :] = merged
            current = jnp.where(start + live >= 128, rolled, merged)
            offset = offset + live
        area_group(patch_ref, table, out_ref, c, 0)
        return offset, current

    offset, current = lax.fori_loop(
        0, groups, chunk, (jnp.int32(0), jnp.zeros((1, 128), jnp.int32)), unroll=2
    )
    packed[pl.ds(lax.shift_right_logical(offset, 7), 1), :] = current
    offset_ref[0, 128] = offset


def area_kernel(patch_ref, area_ref, out_ref, table, *, first):
    split_area(area_ref, table)

    def chunk(c, _):
        area_group(patch_ref, table, out_ref, c, first)
        return 0

    lax.fori_loop(0, out_ref.shape[0], chunk, 0, unroll=4)


def area_cost(groups):
    return pl.CostEstimate(
        flops=2 * 768 * 512 * GROUP * 128 * groups, bytes_accessed=2000000, transcendentals=0
    )


def gather_area_and_pack(counts, cells, patch, area, groups):
    return pl.pallas_call(
        functools.partial(first_area_kernel, groups=groups),
        out_shape=(
            jax.ShapeDtypeStruct((groups, 8, GROUP * 128), f32),
            jax.ShapeDtypeStruct((136, 128), jnp.int32),
            jax.ShapeDtypeStruct((1, 136), jnp.int32),
        ),
        in_specs=[SMEM, VMEM, VMEM, VMEM],
        out_specs=(VMEM, VMEM, SMEM),
        scratch_shapes=[pltpu.VMEM((768, 512), bf16)],
        compiler_params=pltpu.CompilerParams(vmem_limit_bytes=32 << 20),
        cost_estimate=area_cost(groups),
        name="area_and_pack",
    )(counts, cells, patch, area)


def gather_area(patch, area, first, groups):
    return pl.pallas_call(
        functools.partial(area_kernel, first=first),
        out_shape=jax.ShapeDtypeStruct((groups, 8, GROUP * 128), f32),
        in_specs=[VMEM, VMEM],
        out_specs=VMEM,
        scratch_shapes=[pltpu.VMEM((768, 512), bf16)],
        compiler_params=pltpu.CompilerParams(vmem_limit_bytes=32 << 20),
        cost_estimate=area_cost(groups),
        name="gather_area",
    )(patch, area)


EDGE = 104
PIECES = ((0, 2), (2, 1))


def scatter_kernel(
    odd_ref, patch_ref, area_a_ref, area_b_ref, flux_ref, out_ref, first_ref, second_ref, *, first
):
    freqs = out_ref.shape[0]
    out_ref[...] = jnp.zeros_like(out_ref)

    def add_group(c, area):
        patch = slot_row(patch_ref, c)
        u, v = lax.shift_right_logical(patch, 8), lax.bitwise_and(patch, 255)
        hot = onehot(256, v)
        mine = iota((256, GROUP * 128), 0).astype(bf16) == u.astype(bf16)
        heads, rests = [], []
        for f in range(first, first + freqs):
            density = jnp.zeros((1, GROUP * 128), f32)
            for q in range(3):
                flux = jnp.concatenate(
                    [flux_ref[GROUP * c + i, 3 * f + q] for i in range(GROUP)], 1
                )
                density = density + area[q : q + 1, :] * flux
            head = density.astype(bf16)
            rest = (density - head.astype(f32)).astype(bf16)
            heads.append(jnp.where(mine, head, jnp.zeros((), bf16)))
            rests.append(jnp.where(mine, rest, jnp.zeros((), bf16)))
        left = jnp.concatenate([jnp.concatenate(heads, 0), jnp.concatenate(rests, 0)], 1)
        right = jnp.concatenate([hot, hot], 1)
        out_ref[...] += lax.dot_general(
            left, right, (((1,), (1,)), ((), ())), preferred_element_type=f32
        ).reshape(freqs, 256, 256)

    half = area_a_ref.shape[0]

    def first_part(c, _):
        add_group(c, area_a_ref[c])
        return 0

    def second_part(c, _):
        add_group(c + half, area_b_ref[c])
        return 0

    lax.fori_loop(0, half, first_part, 0, unroll=4)
    lax.fori_loop(0, area_b_ref.shape[0], second_part, 0, unroll=4)
    for f in range(freqs):
        head = jnp.transpose(out_ref[f, :, :128])[:EDGE]
        tail = jnp.transpose(out_ref[f, :, 128:])[128 - EDGE :]
        put_edges(odd_ref[0, 0], head, tail, first_ref, second_ref, f)


def block_and_edges(freqs):
    return (
        jax.ShapeDtypeStruct((freqs, 256, 256), f32),
        jax.ShapeDtypeStruct((freqs, EDGE, 256), f32),
        jax.ShapeDtypeStruct((freqs, EDGE, 256), f32),
    )


def scatter_density(odd, patch, area_a, area_b, flux, first, freqs):
    return pl.pallas_call(
        functools.partial(scatter_kernel, first=first),
        out_shape=block_and_edges(freqs),
        in_specs=[SMEM] + [VMEM] * 4,
        out_specs=(VMEM,) * 3,
        compiler_params=pltpu.CompilerParams(vmem_limit_bytes=36 << 20),
        cost_estimate=pl.CostEstimate(
            flops=2 * freqs * 65536 * 2 * 16384, bytes_accessed=2000000, transcendentals=0
        ),
        name="scatter_density",
    )(odd, patch, area_a, area_b, flux)


def in_window(place):
    return jnp.where((place >= -HALF) & (place < HALF), 1.0, 0.0).astype(bf16)


def two_parts(cells):
    head = cells.astype(bf16)
    return head, (cells - head.astype(f32)).astype(bf16)


def column_kernel(odd_ref, block_ref, one_ref, two_ref, out_ref, first_ref, second_ref):
    inner = in_window(iota((256, 256), 0) - iota((256, 256), 1))
    place, column = iota((EDGE, 256), 0), iota((EDGE, 256), 1)
    outer = jnp.concatenate(
        [in_window(place - EDGE - column), in_window(place + 256 - column)], 0
    )
    inner = jnp.concatenate([inner, inner], 0)
    outer = jnp.concatenate([outer, outer], 0)
    for f in range(out_ref.shape[0]):
        total = jnp.dot(
            jnp.concatenate(two_parts(block_ref[f]), 1), inner, preferred_element_type=f32
        )
        edges = jnp.concatenate(got_edges(odd_ref[0, 0], one_ref, two_ref, f), 0)
        total = total + lax.dot_general(
            jnp.concatenate(two_parts(edges), 0),
            outer,
            (((0,), (0,)), ((), ())),
            preferred_element_type=f32,
        )
        out_ref[f] = total
        put_edges(odd_ref[0, 1], total[:EDGE], total[256 - EDGE :], first_ref, second_ref, f)


def column_sum(odd, block, first, second):
    freqs = block.shape[0]
    return pl.pallas_call(
        column_kernel,
        out_shape=block_and_edges(freqs),
        in_specs=[SMEM] + [VMEM] * 3,
        out_specs=(VMEM,) * 3,
        compiler_params=pltpu.CompilerParams(vmem_limit_bytes=16 << 20),
        name="column_sum",
    )(odd, block, first, second)


def row_kernel(odd_ref, *refs):
    out_ref = refs[-1]
    length = 256 + 2 * EDGE
    band = in_window(iota((256, length), 1) - EDGE - iota((256, length), 0))
    band = jnp.concatenate([band, band], 1)
    done = 0
    for block_ref, one_ref, two_ref in zip(refs[0:-1:3], refs[1:-1:3], refs[2:-1:3]):
        for f in range(block_ref.shape[0]):
            before, after = got_edges(odd_ref[0, 1], one_ref, two_ref, f)
            cells = jnp.concatenate([before, block_ref[f], after], 0)
            total = jnp.dot(
                band, jnp.concatenate(two_parts(cells), 0), preferred_element_type=f32
            )
            out_ref[done] = total * (1.0 / (4.0 * HALF * HALF))
            done += 1


def row_sum(odd, *pieces):
    return pl.pallas_call(
        row_kernel,
        out_shape=jax.ShapeDtypeStruct((3, 256, 256), f32),
        in_specs=[SMEM] + [VMEM] * len(pieces),
        out_specs=VMEM,
        compiler_params=pltpu.CompilerParams(vmem_limit_bytes=16 << 20),
        name="row_sum",
    )(odd, *pieces)


def shards(
    e_field, h_field, j_field, material, material_table, dft_e, dft_h, skin_cell, counts,
    patch_slot, area,
):
    magnet_x, magnet_y, magnet_z = (h_field[0], h_field[1], h_field[2])
    rows_below = shifted(jnp.stack([magnet_y[:, -1, :], magnet_z[:, -1, :]]), "gy", 1)
    cols_left = shifted(jnp.stack([magnet_x[:, :, -1], magnet_z[:, :, -1]]), "gx", 1)
    odd = jnp.stack([lax.axis_index("gx") % 2, lax.axis_index("gy") % 2]).reshape(1, 2)
    area_a, packed, offsets = gather_area_and_pack(counts, skin_cell, patch_slot, area, 4)
    rows_below, cols_left, area_a = lax.optimization_barrier((rows_below, cols_left, area_a))
    e_next, j_next, dft_e_next, dft_h_next, table = field_step(
        e_field, h_field, j_field, material, material_table, dft_e, dft_h, rows_below, cols_left
    )
    rows = gather_flux(counts, offsets, packed, table.reshape(9, 128, 512))
    arrived = lax.all_to_all(rows, ("gy", "gx"), split_axis=0, concat_axis=0, tiled=True)
    area_b = gather_area(patch_slot, area, 4, 12)

    blocks, pieces, swaps = [], [], []
    for first, freqs in PIECES:
        block, *edges = scatter_density(odd, patch_slot, area_a, area_b, arrived, first, freqs)
        blocks.append(block)
        swaps.append(exchange(*edges, "gx"))
    for block, swap in zip(blocks, swaps):
        strip, *edges = column_sum(odd, block, *swap)
        pieces += [strip, *exchange(*edges, "gy")]
    point_density = jnp.concatenate(blocks, 0)
    avg_density = row_sum(odd, *pieces)
    return (e_next, j_next, dft_e_next, dft_h_next, point_density, avg_density)


def solution(mesh):
    placed = (
        P(None, None, "gy", "gx"),
        P(None, None, "gy", "gx"),
        P(None, None, "gy", "gx"),
        P(None, "gy", "gx"),
        P(),
        P(None, None, None, None, "gy", "gx"),
        P(None, None, None, None, "gy", "gx"),
        P(("gy", "gx"), None, None),
        P(("gy", "gx"), None),
        P(("gy", "gx"), None, None),
        P(None, "gy", "gx"),
    )
    return jax.shard_map(
        shards,
        mesh=mesh,
        in_specs=placed,
        out_specs=(
            P(None, None, "gy", "gx"),
            P(None, None, "gy", "gx"),
            P(None, None, None, None, "gy", "gx"),
            P(None, None, None, None, "gy", "gx"),
            P(None, "gy", "gx"),
            P(None, "gy", "gx"),
        ),
        check_vma=False,
    )
```

```python
import functools
import math

import jax
import jax.numpy as jnp
from jax import lax
from jax.experimental import pallas as pl
from jax.experimental.pallas import tpu as pltpu
from jax.sharding import PartitionSpec as P

STEP = 1000
HALF = 100
FREQ_LIST = (28000000000.0, 39000000000.0, 60000000000.0)
TIME_STEP = 1.9e-13

f32 = jnp.float32
bf16 = jnp.bfloat16
VMEM = pl.BlockSpec(memory_space=pltpu.VMEM)
SMEM = pl.BlockSpec(memory_space=pltpu.SMEM)


def phase_list(offset):
    return [2.0 * math.pi * freq_hz * (STEP + offset) * TIME_STEP for freq_hz in FREQ_LIST]


def iota(shape, dim):
    return lax.broadcasted_iota(jnp.int32, shape, dim)


def shifted(value, axis, steps):
    count = lax.axis_size(axis)
    leading, last = (max(0, -steps), min(count, count - steps))
    return lax.ppermute(value, axis, [(source, source + steps) for source in range(leading, last)])


def exchange(first, second, axis):
    count = lax.axis_size(axis)
    swaps = []
    for start, value in ((1, first), (0, second)):
        lower = range(start, count - 1, 2)
        pairs = [(i, i + 1) for i in lower] + [(i + 1, i) for i in lower]
        swaps.append(lax.ppermute(value, axis, pairs))
    return swaps


def is_odd(odd_ref, axis):
    row = odd_ref[axis : axis + 1, :]
    return jnp.concatenate([row, row], 1) != 0


def put_edges(odd, head, tail, first_ref, second_ref, f):
    first_ref[f] = jnp.where(odd, tail, head)
    second_ref[f] = jnp.where(odd, head, tail)


def got_edges(odd, first_ref, second_ref, f):
    first, second = first_ref[f], second_ref[f]
    return jnp.where(odd, second, first), jnp.where(odd, first, second)


def onehot(count, index):
    places = iota((count, index.shape[1]), 0).astype(bf16)
    return jnp.where(places == index.astype(bf16), jnp.ones((), bf16), jnp.zeros((), bf16))


def field_kernel(
    e_ref, h_ref, j_ref, kind_ref, table_ref, dft_e_ref, dft_h_ref, row_ref, col_ref,
    e_out, j_out, dft_e_out, dft_h_out, flux_out, below_ref, wide_ref,
):
    z = pl.program_id(0)

    @pl.when(z == 0)
    def _():
        below_ref[...] = jnp.zeros_like(below_ref)
        wide_ref[...] = jnp.zeros_like(wide_ref)
        wide_ref[0:4, 0:32] = table_ref[...]

    rows, cols = kind_ref.shape[1:]
    hx, hy, hz = h_ref[0, 0], h_ref[1, 0], h_ref[2, 0]
    first_row = iota((rows, cols), 0) == 0
    first_col = iota((rows, cols), 1) == 0
    diagonal = iota((rows, rows), 0) == iota((rows, rows), 1)

    def below_x(field, part):
        halo = row_ref[part, pl.ds(z, 1), :]
        return jnp.where(first_row, halo, pltpu.roll(field, 1, 0))

    def below_y(field, part):
        halo = col_ref[part, pl.ds(z, 1), :]
        halo = jnp.sum(jnp.where(diagonal, halo, 0.0), axis=1, keepdims=True)
        return jnp.where(first_col, halo, pltpu.roll(field, 1, 1))

    curl = (
        (hz - below_y(hz, 1)) - (hy - below_ref[1]),
        (hx - below_ref[0]) - (hz - below_x(hz, 1)),
        (hy - below_x(hy, 0)) - (hx - below_y(hx, 0)),
    )
    kinds = kind_ref[0]
    coeffs = [
        jnp.take_along_axis(
            jnp.broadcast_to(wide_ref[r : r + 1, :], (rows, cols)), kinds, axis=1
        )
        for r in range(4)
    ]
    e_next = []
    for c in range(3):
        old_e, old_j = e_ref[c, 0], j_ref[c, 0]
        new_e = coeffs[0] * old_e + coeffs[1] * (curl[c] - old_j)
        e_out[c, 0] = new_e
        j_out[c, 0] = coeffs[2] * old_j + coeffs[3] * (new_e - old_e)
        e_next.append(new_e)
    field_h = (hx, hy, hz)
    phase_e, phase_h = phase_list(0.0), phase_list(0.5)
    half_plane = pl.ds(pl.multiple_of((z // 2) * cols, cols), cols)
    rest_plane = pl.ds(pl.multiple_of((z // 2) * cols + 2 * cols, cols), cols)
    for f in range(3):
        spec_e, spec_h = [], []
        for part in range(2):
            factor_e = math.cos(phase_e[f]) if part == 0 else -math.sin(phase_e[f])
            factor_h = math.cos(phase_h[f]) if part == 0 else -math.sin(phase_h[f])
            now_e = [dft_e_ref[f, part, c, 0] + e_next[c] * factor_e for c in range(3)]
            now_h = [dft_h_ref[f, part, c, 0] + field_h[c] * factor_h for c in range(3)]
            for c in range(3):
                dft_e_out[f, part, c, 0] = now_e[c]
                dft_h_out[f, part, c, 0] = now_h[c]
            spec_e.append(now_e)
            spec_h.append(now_h)
        for c in range(3):
            a, b = (c + 1) % 3, (c + 2) % 3
            flux = 0.5 * (
                (spec_e[0][a] * spec_h[0][b] - spec_e[0][b] * spec_h[0][a])
                + (spec_e[1][a] * spec_h[1][b] - spec_e[1][b] * spec_h[1][a])
            )
            head = flux.astype(bf16)
            flux_out[3 * f + c, z % 2, :, half_plane] = head
            flux_out[3 * f + c, z % 2, :, rest_plane] = (flux - head.astype(f32)).astype(bf16)
    below_ref[0] = hx
    below_ref[1] = hy


def field_step(e, h, j, kinds, table, dft_e, dft_h, rows_below, cols_left):
    planes, rows, cols = kinds.shape
    plane3 = pl.BlockSpec((3, 1, rows, cols), lambda z: (0, z, 0, 0))
    spectra = pl.BlockSpec((3, 2, 3, 1, rows, cols), lambda z: (0, 0, 0, z, 0, 0))

    def whole(shape):
        return pl.BlockSpec(shape, lambda z: (0,) * len(shape))

    flux_shape = (9, 2, rows, 4 * cols)
    return pl.pallas_call(
        field_kernel,
        grid=(planes,),
        out_shape=(
            jax.ShapeDtypeStruct(e.shape, f32),
            jax.ShapeDtypeStruct(e.shape, f32),
            jax.ShapeDtypeStruct(dft_e.shape, f32),
            jax.ShapeDtypeStruct(dft_h.shape, f32),
            jax.ShapeDtypeStruct(flux_shape, bf16),
        ),
        in_specs=[
            plane3, plane3, plane3,
            pl.BlockSpec((1, rows, cols), lambda z: (z, 0, 0)),
            whole(table.shape), spectra, spectra,
            whole(rows_below.shape), whole(cols_left.shape),
        ],
        out_specs=(plane3, plane3, spectra, spectra, whole(flux_shape)),
        scratch_shapes=[pltpu.VMEM((2, rows, cols), f32), pltpu.VMEM((8, cols), f32)],
        compiler_params=pltpu.CompilerParams(vmem_limit_bytes=20 << 20),
        name="field_step",
    )(e, h, j, kinds, table, dft_e, dft_h, rows_below, cols_left)


def gather_kernel(count_ref, offset_ref, packed, table_ref, out_ref, found):
    def lookup(c):
        cell = jnp.concatenate([packed[pl.ds(2 * c, 1), :], packed[pl.ds(2 * c + 1, 1), :]], 1)
        high = lax.bitwise_and(lax.shift_right_logical(cell, 14), 1)
        inner = lax.bitwise_or(lax.shift_left(high, 7), lax.bitwise_and(cell, 127))
        outer = lax.bitwise_and(lax.shift_right_logical(cell, 7), 127)
        hot = onehot(256, inner)
        result = jnp.dot(
            table_ref[...].reshape(1152, 512),
            jnp.concatenate([hot, hot], 0),
            preferred_element_type=f32,
        ).reshape(9, 128, 256)
        mine = iota((128, 256), 0) == outer
        for q in range(9):
            value = jnp.sum(jnp.where(mine, result[q], 0.0), axis=0, keepdims=True)
            found[2 * c, q : q + 1, :] = value[:, :128]
            found[2 * c + 1, q : q + 1, :] = value[:, 128:]

    def chunk(c, _):
        for part in range(4):
            lookup(4 * c + part)
        return 0

    lax.fori_loop(0, lax.shift_right_logical(offset_ref[0, 128] + 1023, 10), chunk, 0)
    lanes = iota((16, 128), 1)

    def unpack(d, _):
        offset = offset_ref[0, d]
        row, start = lax.shift_right_logical(offset, 7), lax.bitwise_and(offset, 127)
        live = count_ref[0, d]
        back = lax.bitwise_and(128 - start, 127)
        value = jnp.where(
            lanes < 128 - start, pltpu.roll(found[row], back, 1), pltpu.roll(found[row + 1], back, 1)
        )
        value = jnp.where(lanes < live, value, 0.0)
        for q in range(9):
            out_ref[d, q] = value[q : q + 1, :]
        return 0

    lax.fori_loop(0, 128, unpack, 0, unroll=16)


def gather_flux(counts, offsets, packed, table):
    return pl.pallas_call(
        gather_kernel,
        out_shape=jax.ShapeDtypeStruct((128, 9, 1, 128), f32),
        in_specs=[SMEM, SMEM, VMEM, VMEM],
        out_specs=VMEM,
        scratch_shapes=[pltpu.VMEM((136, 16, 128), f32)],
        compiler_params=pltpu.CompilerParams(vmem_limit_bytes=24 << 20),
        name="gather_flux",
    )(counts, offsets, packed, table)


GROUP = 8


def slot_row(ref, c):
    return jnp.concatenate([ref[0, pl.ds(GROUP * c + i, 1), :] for i in range(GROUP)], 1)


def split_area(area_ref, table):
    area = area_ref[...].reshape(768, 256)
    head = area.astype(bf16)
    table[:, :256] = head
    table[:, 256:] = (area - head.astype(f32)).astype(bf16)


def area_group(patch_ref, table, out_ref, c, first):
    patch = slot_row(patch_ref, c + first)
    u, v = lax.shift_right_logical(patch, 8), lax.bitwise_and(patch, 255)
    hot = onehot(256, v)
    result = jnp.dot(
        table[...], jnp.concatenate([hot, hot], 0), preferred_element_type=f32
    ).reshape(3, 256, GROUP * 128)
    mine = iota((256, GROUP * 128), 0) == u
    for q in range(3):
        out_ref[c, q : q + 1, :] = jnp.sum(jnp.where(mine, result[q], 0.0), axis=0, keepdims=True)


def first_area_kernel(
    count_ref, cell_ref, patch_ref, area_ref, out_ref, packed, offset_ref, table, *, groups
):
    split_area(area_ref, table)
    lane = iota((1, 128), 1)
    share = 128 // groups

    def chunk(c, carry):
        offset, current = carry
        for i in range(share):
            d = c * share + i
            row, start = lax.shift_right_logical(offset, 7), lax.bitwise_and(offset, 127)
            live = count_ref[0, d]
            offset_ref[0, d] = offset
            rolled = pltpu.roll(cell_ref[0, pl.ds(d, 1), :], start, 1)
            merged = jnp.where(lane >= start, rolled, current)
            packed[pl.ds(row, 1), :] = merged
            current = jnp.where(start + live >= 128, rolled, merged)
            offset = offset + live
        area_group(patch_ref, table, out_ref, c, 0)
        return offset, current

    offset, current = lax.fori_loop(
        0, groups, chunk, (jnp.int32(0), jnp.zeros((1, 128), jnp.int32)), unroll=2
    )
    packed[pl.ds(lax.shift_right_logical(offset, 7), 1), :] = current
    offset_ref[0, 128] = offset


def area_kernel(patch_ref, area_ref, out_ref, table, *, first):
    split_area(area_ref, table)

    def chunk(c, _):
        area_group(patch_ref, table, out_ref, c, first)
        return 0

    lax.fori_loop(0, out_ref.shape[0], chunk, 0, unroll=4)


def area_cost(groups):
    return pl.CostEstimate(
        flops=2 * 768 * 512 * GROUP * 128 * groups, bytes_accessed=2000000, transcendentals=0
    )


def gather_area_and_pack(counts, cells, patch, area, groups):
    return pl.pallas_call(
        functools.partial(first_area_kernel, groups=groups),
        out_shape=(
            jax.ShapeDtypeStruct((groups, 8, GROUP * 128), f32),
            jax.ShapeDtypeStruct((136, 128), jnp.int32),
            jax.ShapeDtypeStruct((1, 136), jnp.int32),
        ),
        in_specs=[SMEM, VMEM, VMEM, VMEM],
        out_specs=(VMEM, VMEM, SMEM),
        scratch_shapes=[pltpu.VMEM((768, 512), bf16)],
        compiler_params=pltpu.CompilerParams(vmem_limit_bytes=32 << 20),
        cost_estimate=area_cost(groups),
        name="area_and_pack",
    )(counts, cells, patch, area)


def gather_area(patch, area, first, groups):
    return pl.pallas_call(
        functools.partial(area_kernel, first=first),
        out_shape=jax.ShapeDtypeStruct((groups, 8, GROUP * 128), f32),
        in_specs=[VMEM, VMEM],
        out_specs=VMEM,
        scratch_shapes=[pltpu.VMEM((768, 512), bf16)],
        compiler_params=pltpu.CompilerParams(vmem_limit_bytes=32 << 20),
        cost_estimate=area_cost(groups),
        name="gather_area",
    )(patch, area)


EDGE = 104
PIECES = ((0, 2), (2, 1))


def scatter_kernel(
    odd_ref, patch_ref, area_a_ref, area_b_ref, flux_ref, out_ref, first_ref, second_ref, *, first
):
    freqs = out_ref.shape[0]
    out_ref[...] = jnp.zeros_like(out_ref)

    def add_group(c, area):
        patch = slot_row(patch_ref, c)
        u, v = lax.shift_right_logical(patch, 8), lax.bitwise_and(patch, 255)
        hot = onehot(256, v)
        mine = iota((256, GROUP * 128), 0).astype(bf16) == u.astype(bf16)
        heads, rests = [], []
        for f in range(first, first + freqs):
            density = jnp.zeros((1, GROUP * 128), f32)
            for q in range(3):
                flux = jnp.concatenate(
                    [flux_ref[GROUP * c + i, 3 * f + q] for i in range(GROUP)], 1
                )
                density = density + area[q : q + 1, :] * flux
            head = density.astype(bf16)
            rest = (density - head.astype(f32)).astype(bf16)
            heads.append(jnp.where(mine, head, jnp.zeros((), bf16)))
            rests.append(jnp.where(mine, rest, jnp.zeros((), bf16)))
        left = jnp.concatenate([jnp.concatenate(heads, 0), jnp.concatenate(rests, 0)], 1)
        right = jnp.concatenate([hot, hot], 1)
        out_ref[...] += lax.dot_general(
            left, right, (((1,), (1,)), ((), ())), preferred_element_type=f32
        ).reshape(freqs, 256, 256)

    half = area_a_ref.shape[0]

    def first_part(c, _):
        add_group(c, area_a_ref[c])
        return 0

    def second_part(c, _):
        add_group(c + half, area_b_ref[c])
        return 0

    lax.fori_loop(0, half, first_part, 0, unroll=4)
    lax.fori_loop(0, area_b_ref.shape[0], second_part, 0, unroll=4)
    for f in range(freqs):
        head = jnp.transpose(out_ref[f, :, :128])[:EDGE]
        tail = jnp.transpose(out_ref[f, :, 128:])[128 - EDGE :]
        put_edges(is_odd(odd_ref, 0), head, tail, first_ref, second_ref, f)


def block_and_edges(freqs):
    return (
        jax.ShapeDtypeStruct((freqs, 256, 256), f32),
        jax.ShapeDtypeStruct((freqs, EDGE, 256), f32),
        jax.ShapeDtypeStruct((freqs, EDGE, 256), f32),
    )


def scatter_density(odd, patch, area_a, area_b, flux, first, freqs):
    return pl.pallas_call(
        functools.partial(scatter_kernel, first=first),
        out_shape=block_and_edges(freqs),
        in_specs=[VMEM] * 5,
        out_specs=(VMEM,) * 3,
        compiler_params=pltpu.CompilerParams(vmem_limit_bytes=36 << 20),
        cost_estimate=pl.CostEstimate(
            flops=2 * freqs * 65536 * 2 * 16384, bytes_accessed=2000000, transcendentals=0
        ),
        name="scatter_density",
    )(odd, patch, area_a, area_b, flux)


def in_window(place):
    return jnp.where((place >= -HALF) & (place < HALF), 1.0, 0.0).astype(bf16)


def two_parts(cells):
    head = cells.astype(bf16)
    return head, (cells - head.astype(f32)).astype(bf16)


def column_kernel(odd_ref, *refs):
    refs, (out_ref, first_ref, second_ref) = refs[:-3], refs[-3:]
    inner = in_window(iota((256, 256), 0) - iota((256, 256), 1))
    place, column = iota((EDGE, 256), 0), iota((EDGE, 256), 1)
    outer = jnp.concatenate(
        [in_window(place - EDGE - column), in_window(place + 256 - column)], 0
    )
    inner = jnp.concatenate([inner, inner], 0)
    outer = jnp.concatenate([outer, outer], 0)
    done = 0
    for block_ref, one_ref, two_ref in zip(refs[0::3], refs[1::3], refs[2::3]):
        for f in range(block_ref.shape[0]):
            total = jnp.dot(
                jnp.concatenate(two_parts(block_ref[f]), 1), inner, preferred_element_type=f32
            )
            edges = jnp.concatenate(got_edges(is_odd(odd_ref, 0), one_ref, two_ref, f), 0)
            total = total + lax.dot_general(
                jnp.concatenate(two_parts(edges), 0),
                outer,
                (((0,), (0,)), ((), ())),
                preferred_element_type=f32,
            )
            out_ref[done] = total
            put_edges(
                is_odd(odd_ref, 1), total[:EDGE], total[256 - EDGE :], first_ref, second_ref, done
            )
            done += 1


def column_sum(odd, *pieces):
    return pl.pallas_call(
        column_kernel,
        out_shape=block_and_edges(3),
        in_specs=[VMEM] * (1 + len(pieces)),
        out_specs=(VMEM,) * 3,
        compiler_params=pltpu.CompilerParams(vmem_limit_bytes=16 << 20),
        name="column_sum",
    )(odd, *pieces)


def row_kernel(odd_ref, block_ref, one_ref, two_ref, out_ref):
    length = 256 + 2 * EDGE
    band = in_window(iota((256, length), 1) - EDGE - iota((256, length), 0))
    band = jnp.concatenate([band, band], 1)
    for f in range(3):
        before, after = got_edges(is_odd(odd_ref, 1), one_ref, two_ref, f)
        cells = jnp.concatenate([before, block_ref[f], after], 0)
        total = jnp.dot(band, jnp.concatenate(two_parts(cells), 0), preferred_element_type=f32)
        out_ref[f] = total * (1.0 / (4.0 * HALF * HALF))


def row_sum(odd, block, first, second):
    return pl.pallas_call(
        row_kernel,
        out_shape=jax.ShapeDtypeStruct((3, 256, 256), f32),
        in_specs=[VMEM] * 4,
        out_specs=VMEM,
        compiler_params=pltpu.CompilerParams(vmem_limit_bytes=16 << 20),
        name="row_sum",
    )(odd, block, first, second)


def shards(
    e_field, h_field, j_field, material, material_table, dft_e, dft_h, skin_cell, counts,
    patch_slot, area,
):
    magnet_x, magnet_y, magnet_z = (h_field[0], h_field[1], h_field[2])
    rows_below = shifted(jnp.stack([magnet_y[:, -1, :], magnet_z[:, -1, :]]), "gy", 1)
    cols_left = shifted(jnp.stack([magnet_x[:, :, -1], magnet_z[:, :, -1]]), "gx", 1)
    odd = jnp.stack([lax.axis_index("gx") % 2, lax.axis_index("gy") % 2])
    odd = jnp.broadcast_to(odd[:, None], (2, 128))
    area_a, packed, offsets = gather_area_and_pack(counts, skin_cell, patch_slot, area, 4)
    rows_below, cols_left, area_a = lax.optimization_barrier((rows_below, cols_left, area_a))
    e_next, j_next, dft_e_next, dft_h_next, table = field_step(
        e_field, h_field, j_field, material, material_table, dft_e, dft_h, rows_below, cols_left
    )
    rows = gather_flux(counts, offsets, packed, table.reshape(9, 128, 512))
    arrived = lax.all_to_all(rows, ("gy", "gx"), split_axis=0, concat_axis=0, tiled=True)
    area_b = gather_area(patch_slot, area, 4, 12)

    blocks, pieces = [], []
    for first, freqs in PIECES:
        block, *edges = scatter_density(odd, patch_slot, area_a, area_b, arrived, first, freqs)
        blocks.append(block)
        pieces += [block, *exchange(*edges, "gx")]
    strip, *edges = column_sum(odd, *pieces)
    edges = exchange(*edges, "gy")
    point_density = jnp.concatenate(blocks, 0)
    avg_density = row_sum(odd, strip, *edges)
    return (e_next, j_next, dft_e_next, dft_h_next, point_density, avg_density)


def solution(mesh):
    placed = (
        P(None, None, "gy", "gx"),
        P(None, None, "gy", "gx"),
        P(None, None, "gy", "gx"),
        P(None, "gy", "gx"),
        P(),
        P(None, None, None, None, "gy", "gx"),
        P(None, None, None, None, "gy", "gx"),
        P(("gy", "gx"), None, None),
        P(("gy", "gx"), None),
        P(("gy", "gx"), None, None),
        P(None, "gy", "gx"),
    )
    return jax.shard_map(
        shards,
        mesh=mesh,
        in_specs=placed,
        out_specs=(
            P(None, None, "gy", "gx"),
            P(None, None, "gy", "gx"),
            P(None, None, None, None, "gy", "gx"),
            P(None, None, None, None, "gy", "gx"),
            P(None, "gy", "gx"),
            P(None, "gy", "gx"),
        ),
        check_vma=False,
    )
```

```python
import functools
import math

import jax
import jax.numpy as jnp
from jax import lax
from jax.experimental import pallas as pl
from jax.experimental.pallas import tpu as pltpu
from jax.sharding import PartitionSpec as P

STEP = 1000
HALF = 100
FREQ_LIST = (28000000000.0, 39000000000.0, 60000000000.0)
TIME_STEP = 1.9e-13

f32 = jnp.float32
bf16 = jnp.bfloat16
f8 = jnp.float8_e4m3fn
TOP = 100000.0
VMEM = pl.BlockSpec(memory_space=pltpu.VMEM)
SMEM = pl.BlockSpec(memory_space=pltpu.SMEM)


def phase_list(offset):
    return [2.0 * math.pi * freq_hz * (STEP + offset) * TIME_STEP for freq_hz in FREQ_LIST]


def iota(shape, dim):
    return lax.broadcasted_iota(jnp.int32, shape, dim)


def shifted(value, axis, steps):
    count = lax.axis_size(axis)
    leading, last = (max(0, -steps), min(count, count - steps))
    return lax.ppermute(value, axis, [(source, source + steps) for source in range(leading, last)])


def exchange(first, second, axis):
    count = lax.axis_size(axis)
    swaps = []
    for start, value in ((1, first), (0, second)):
        lower = range(start, count - 1, 2)
        pairs = [(i, i + 1) for i in lower] + [(i + 1, i) for i in lower]
        swaps.append(lax.ppermute(value, axis, pairs))
    return swaps


def is_odd(odd_ref, axis):
    row = odd_ref[axis : axis + 1, :]
    return jnp.concatenate([row, row], 1) != 0


def put_edges(odd, head, tail, first_ref, second_ref, f):
    first_ref[f] = jnp.where(odd, tail, head)
    second_ref[f] = jnp.where(odd, head, tail)


def got_edges(odd, first_ref, second_ref, f):
    first, second = first_ref[f], second_ref[f]
    return jnp.where(odd, second, first), jnp.where(odd, first, second)


def onehot(count, index):
    places = iota((count, index.shape[1]), 0).astype(bf16)
    return jnp.where(places == index.astype(bf16), jnp.ones((), bf16), jnp.zeros((), bf16))


def largest(values):
    top = jnp.max(jnp.max(jnp.abs(values), axis=0, keepdims=True), axis=1, keepdims=True)
    return jnp.maximum(top, 1e-30)


def split_scaled(values, head_ref, rest_ref):
    top = largest(values)
    values = values * (TOP / top)
    head = values.astype(bf16)
    head_ref[...] = head
    rest_ref[...] = (values - head.astype(f32)).astype(f8)
    return top * (1.0 / TOP)


def field_kernel(
    e_ref, h_ref, j_ref, kind_ref, table_ref, dft_e_ref, dft_h_ref, row_ref, col_ref,
    e_out, j_out, dft_e_out, dft_h_out, flux_out, below_ref, wide_ref,
):
    z = pl.program_id(0)

    @pl.when(z == 0)
    def _():
        below_ref[...] = jnp.zeros_like(below_ref)
        wide_ref[...] = jnp.zeros_like(wide_ref)
        wide_ref[0:4, 0:32] = table_ref[...]

    rows, cols = kind_ref.shape[1:]
    hx, hy, hz = h_ref[0, 0], h_ref[1, 0], h_ref[2, 0]
    first_row = iota((rows, cols), 0) == 0
    first_col = iota((rows, cols), 1) == 0
    diagonal = iota((rows, rows), 0) == iota((rows, rows), 1)

    def below_x(field, part):
        halo = row_ref[part, pl.ds(z, 1), :]
        return jnp.where(first_row, halo, pltpu.roll(field, 1, 0))

    def below_y(field, part):
        halo = col_ref[part, pl.ds(z, 1), :]
        halo = jnp.sum(jnp.where(diagonal, halo, 0.0), axis=1, keepdims=True)
        return jnp.where(first_col, halo, pltpu.roll(field, 1, 1))

    curl = (
        (hz - below_y(hz, 1)) - (hy - below_ref[1]),
        (hx - below_ref[0]) - (hz - below_x(hz, 1)),
        (hy - below_x(hy, 0)) - (hx - below_y(hx, 0)),
    )
    kinds = kind_ref[0]
    coeffs = [
        jnp.take_along_axis(
            jnp.broadcast_to(wide_ref[r : r + 1, :], (rows, cols)), kinds, axis=1
        )
        for r in range(4)
    ]
    e_next = []
    for c in range(3):
        old_e, old_j = e_ref[c, 0], j_ref[c, 0]
        new_e = coeffs[0] * old_e + coeffs[1] * (curl[c] - old_j)
        e_out[c, 0] = new_e
        j_out[c, 0] = coeffs[2] * old_j + coeffs[3] * (new_e - old_e)
        e_next.append(new_e)
    field_h = (hx, hy, hz)
    phase_e, phase_h = phase_list(0.0), phase_list(0.5)
    for f in range(3):
        spec_e, spec_h = [], []
        for part in range(2):
            factor_e = math.cos(phase_e[f]) if part == 0 else -math.sin(phase_e[f])
            factor_h = math.cos(phase_h[f]) if part == 0 else -math.sin(phase_h[f])
            now_e = [dft_e_ref[f, part, c, 0] + e_next[c] * factor_e for c in range(3)]
            now_h = [dft_h_ref[f, part, c, 0] + field_h[c] * factor_h for c in range(3)]
            for c in range(3):
                dft_e_out[f, part, c, 0] = now_e[c]
                dft_h_out[f, part, c, 0] = now_h[c]
            spec_e.append(now_e)
            spec_h.append(now_h)
        for c in range(3):
            a, b = (c + 1) % 3, (c + 2) % 3
            flux = 0.5 * (
                (spec_e[0][a] * spec_h[0][b] - spec_e[0][b] * spec_h[0][a])
                + (spec_e[1][a] * spec_h[1][b] - spec_e[1][b] * spec_h[1][a])
            )
            flux_out[3 * f + c, 0] = flux
    below_ref[0] = hx
    below_ref[1] = hy


def field_step(e, h, j, kinds, table, dft_e, dft_h, rows_below, cols_left):
    planes, rows, cols = kinds.shape
    plane3 = pl.BlockSpec((3, 1, rows, cols), lambda z: (0, z, 0, 0))
    spectra = pl.BlockSpec((3, 2, 3, 1, rows, cols), lambda z: (0, 0, 0, z, 0, 0))

    flux = pl.BlockSpec((9, 1, rows, cols), lambda z: (0, z, 0, 0))

    def whole(shape):
        return pl.BlockSpec(shape, lambda z: (0,) * len(shape))

    return pl.pallas_call(
        field_kernel,
        grid=(planes,),
        out_shape=(
            jax.ShapeDtypeStruct(e.shape, f32),
            jax.ShapeDtypeStruct(e.shape, f32),
            jax.ShapeDtypeStruct(dft_e.shape, f32),
            jax.ShapeDtypeStruct(dft_h.shape, f32),
            jax.ShapeDtypeStruct((9, planes, rows, cols), f32),
        ),
        in_specs=[
            plane3, plane3, plane3,
            pl.BlockSpec((1, rows, cols), lambda z: (z, 0, 0)),
            whole(table.shape), spectra, spectra,
            whole(rows_below.shape), whole(cols_left.shape),
        ],
        out_specs=(plane3, plane3, spectra, spectra, flux),
        scratch_shapes=[pltpu.VMEM((2, rows, cols), f32), pltpu.VMEM((8, cols), f32)],
        compiler_params=pltpu.CompilerParams(vmem_limit_bytes=20 << 20),
        name="field_step",
    )(e, h, j, kinds, table, dft_e, dft_h, rows_below, cols_left)


def gather_kernel(offset_ref, packed, flux_ref, out_ref, found, head_ref, rest_ref):
    planes = [flux_ref[:, z].reshape(576, 128) for z in range(4)]
    back = split_scaled(jnp.concatenate(planes, 1), head_ref, rest_ref)

    def lookup(c):
        cell = jnp.concatenate([packed[pl.ds(2 * c, 1), :], packed[pl.ds(2 * c + 1, 1), :]], 1)
        plane = lax.bitwise_and(lax.shift_right_logical(cell, 13), 3)
        row = lax.bitwise_and(lax.shift_right_logical(cell, 7), 63)
        inner = lax.bitwise_or(lax.shift_left(plane, 7), lax.bitwise_and(cell, 127))
        hot = jnp.concatenate(
            [onehot(256, inner), onehot(256, jnp.where(inner >= 256, inner - 256, 512))], 0
        )
        result = jnp.dot(head_ref[...], hot, preferred_element_type=f32)
        result = result + jnp.dot(rest_ref[...], hot.astype(f8), preferred_element_type=f32)
        result = result.reshape(9, 64, 256)
        mine = iota((64, 256), 0) == row
        for q in range(9):
            value = jnp.sum(jnp.where(mine, result[q], 0.0), axis=0, keepdims=True) * back
            found[2 * c, q : q + 1, :] = value[:, :128]
            found[2 * c + 1, q : q + 1, :] = value[:, 128:]

    def chunk(c, _):
        for part in range(4):
            lookup(4 * c + part)
        return 0

    lax.fori_loop(0, lax.shift_right_logical(offset_ref[0, 128] + 1023, 10), chunk, 0)
    lanes = iota((16, 128), 1)

    def unpack(d, _):
        offset = offset_ref[0, d]
        row, start = lax.shift_right_logical(offset, 7), lax.bitwise_and(offset, 127)
        live = offset_ref[0, d + 1] - offset
        back = lax.bitwise_and(128 - start, 127)
        value = jnp.where(
            lanes < 128 - start, pltpu.roll(found[row], back, 1), pltpu.roll(found[row + 1], back, 1)
        )
        value = jnp.where(lanes < live, value, 0.0)
        for q in range(9):
            out_ref[d, q] = value[q : q + 1, :]
        return 0

    lax.fori_loop(0, 128, unpack, 0, unroll=16)


def gather_flux(offsets, packed, flux):
    return pl.pallas_call(
        gather_kernel,
        out_shape=jax.ShapeDtypeStruct((128, 9, 1, 128), f32),
        in_specs=[SMEM, VMEM, VMEM],
        out_specs=VMEM,
        scratch_shapes=[
            pltpu.VMEM((136, 16, 128), f32),
            pltpu.VMEM((576, 512), bf16),
            pltpu.VMEM((576, 512), f8),
        ],
        compiler_params=pltpu.CompilerParams(vmem_limit_bytes=28 << 20),
        name="gather_flux",
    )(offsets, packed, flux)


GROUP = 8


def slot_row(ref, c):
    return jnp.concatenate([ref[0, pl.ds(GROUP * c + i, 1), :] for i in range(GROUP)], 1)


AREA_SCRATCH = [pltpu.VMEM((384, 512), bf16), pltpu.VMEM((384, 512), f8)]


def split_area(area_ref, head_ref, rest_ref):
    halves = [area_ref[:, :128, :].reshape(384, 256), area_ref[:, 128:, :].reshape(384, 256)]
    return split_scaled(jnp.concatenate(halves, 1), head_ref, rest_ref)


def area_group(patch_ref, head_ref, rest_ref, back, out_ref, c, first):
    patch = slot_row(patch_ref, c + first)
    u, v = lax.shift_right_logical(patch, 8), lax.bitwise_and(patch, 255)
    hot = jnp.concatenate(
        [onehot(256, jnp.where(u < 128, v, 512)), onehot(256, jnp.where(u < 128, 512, v))], 0
    )
    result = jnp.dot(head_ref[...], hot, preferred_element_type=f32)
    result = result + jnp.dot(rest_ref[...], hot.astype(f8), preferred_element_type=f32)
    result = result.reshape(3, 128, GROUP * 128)
    mine = iota((128, GROUP * 128), 0) == lax.bitwise_and(u, 127)
    for q in range(3):
        found = jnp.sum(jnp.where(mine, result[q], 0.0), axis=0, keepdims=True)
        out_ref[c, q : q + 1, :] = found * back


def first_area_kernel(
    count_ref, cell_ref, patch_ref, area_ref, out_ref, packed, offset_ref, head_ref, rest_ref,
    *, groups
):
    back = split_area(area_ref, head_ref, rest_ref)
    lane = iota((1, 128), 1)
    share = 128 // groups

    def chunk(c, carry):
        offset, current = carry
        for i in range(share):
            d = c * share + i
            row, start = lax.shift_right_logical(offset, 7), lax.bitwise_and(offset, 127)
            live = count_ref[0, d]
            offset_ref[0, d] = offset
            rolled = pltpu.roll(cell_ref[0, pl.ds(d, 1), :], start, 1)
            merged = jnp.where(lane >= start, rolled, current)
            packed[pl.ds(row, 1), :] = merged
            current = jnp.where(start + live >= 128, rolled, merged)
            offset = offset + live
        area_group(patch_ref, head_ref, rest_ref, back, out_ref, c, 0)
        return offset, current

    offset, current = lax.fori_loop(
        0, groups, chunk, (jnp.int32(0), jnp.zeros((1, 128), jnp.int32)), unroll=2
    )
    packed[pl.ds(lax.shift_right_logical(offset, 7), 1), :] = current
    offset_ref[0, 128] = offset


def area_kernel(patch_ref, area_ref, out_ref, head_ref, rest_ref, *, first):
    back = split_area(area_ref, head_ref, rest_ref)

    def chunk(c, _):
        area_group(patch_ref, head_ref, rest_ref, back, out_ref, c, first)
        return 0

    lax.fori_loop(0, out_ref.shape[0], chunk, 0, unroll=7)


def area_cost(groups):
    return pl.CostEstimate(
        flops=2 * 768 * 512 * GROUP * 128 * groups, bytes_accessed=2000000, transcendentals=0
    )


def gather_area_and_pack(counts, cells, patch, area, groups):
    return pl.pallas_call(
        functools.partial(first_area_kernel, groups=groups),
        out_shape=(
            jax.ShapeDtypeStruct((groups, 8, GROUP * 128), f32),
            jax.ShapeDtypeStruct((136, 128), jnp.int32),
            jax.ShapeDtypeStruct((1, 136), jnp.int32),
        ),
        in_specs=[SMEM, VMEM, VMEM, VMEM],
        out_specs=(VMEM, VMEM, SMEM),
        scratch_shapes=AREA_SCRATCH,
        compiler_params=pltpu.CompilerParams(vmem_limit_bytes=32 << 20),
        cost_estimate=area_cost(groups),
        name="area_and_pack",
    )(counts, cells, patch, area)


def gather_area(patch, area, first, groups):
    return pl.pallas_call(
        functools.partial(area_kernel, first=first),
        out_shape=jax.ShapeDtypeStruct((groups, 8, GROUP * 128), f32),
        in_specs=[VMEM, VMEM],
        out_specs=VMEM,
        scratch_shapes=AREA_SCRATCH,
        compiler_params=pltpu.CompilerParams(vmem_limit_bytes=32 << 20),
        cost_estimate=area_cost(groups),
        name="gather_area",
    )(patch, area)


EDGE = 104
PIECES = ((0, 2), (2, 1))


def scatter_kernel(
    odd_ref, patch_ref, area_a_ref, area_b_ref, flux_ref, out_ref, first_ref, second_ref, dense,
    *, first
):
    freqs = out_ref.shape[0]
    half, groups = area_a_ref.shape[0], dense.shape[0]
    out_ref[...] = jnp.zeros_like(out_ref)
    top = jnp.zeros((1, GROUP * 128), f32)
    for c in range(groups):
        area = area_a_ref[c] if c < half else area_b_ref[c - half]
        for f in range(freqs):
            density = jnp.zeros((1, GROUP * 128), f32)
            for q in range(3):
                flux = jnp.concatenate(
                    [flux_ref[GROUP * c + i, 3 * (first + f) + q] for i in range(GROUP)], 1
                )
                density = density + area[q : q + 1, :] * flux
            dense[c, f : f + 1, :] = density
            top = jnp.maximum(top, jnp.abs(density))
    top = largest(top)
    scale = TOP / top

    def add_group(c, _):
        patch = slot_row(patch_ref, c)
        u, v = lax.shift_right_logical(patch, 8), lax.bitwise_and(patch, 255)
        hot = onehot(256, v)
        mine = iota((256, GROUP * 128), 0).astype(bf16) == u.astype(bf16)
        heads, rests = [], []
        for f in range(freqs):
            density = dense[c, f : f + 1, :] * scale
            head = density.astype(bf16)
            rest = (density - head.astype(f32)).astype(bf16)
            heads.append(jnp.where(mine, head, jnp.zeros((), bf16)))
            rests.append(jnp.where(mine, rest, jnp.zeros((), bf16)).astype(f8))
        dims = (((1,), (1,)), ((), ()))
        total = lax.dot_general(jnp.concatenate(heads, 0), hot, dims, preferred_element_type=f32)
        total = total + lax.dot_general(
            jnp.concatenate(rests, 0), hot.astype(f8), dims, preferred_element_type=f32
        )
        out_ref[...] += total.reshape(freqs, 256, 256)
        return 0

    lax.fori_loop(0, groups, add_group, 0, unroll=8)
    out_ref[...] = out_ref[...] * (top * (1.0 / TOP)).reshape(1, 1, 1)
    for f in range(freqs):
        head = jnp.transpose(out_ref[f, :, :128])[:EDGE]
        tail = jnp.transpose(out_ref[f, :, 128:])[128 - EDGE :]
        put_edges(is_odd(odd_ref, 0), head, tail, first_ref, second_ref, f)


def block_and_edges(freqs):
    return (
        jax.ShapeDtypeStruct((freqs, 256, 256), f32),
        jax.ShapeDtypeStruct((freqs, EDGE, 256), f32),
        jax.ShapeDtypeStruct((freqs, EDGE, 256), f32),
    )


def scatter_density(odd, patch, area_a, area_b, flux, first, freqs):
    return pl.pallas_call(
        functools.partial(scatter_kernel, first=first),
        out_shape=block_and_edges(freqs),
        in_specs=[VMEM] * 5,
        out_specs=(VMEM,) * 3,
        scratch_shapes=[pltpu.VMEM((128 // GROUP, 8, GROUP * 128), f32)],
        compiler_params=pltpu.CompilerParams(vmem_limit_bytes=36 << 20),
        cost_estimate=pl.CostEstimate(
            flops=2 * freqs * 65536 * 2 * 16384, bytes_accessed=2000000, transcendentals=0
        ),
        name="scatter_density",
    )(odd, patch, area_a, area_b, flux)


def in_window(place):
    return jnp.where((place >= -HALF) & (place < HALF), 1.0, 0.0).astype(bf16)


def two_parts(cells):
    head = cells.astype(bf16)
    return head, (cells - head.astype(f32)).astype(bf16)


def column_kernel(odd_ref, *refs):
    refs, (out_ref, first_ref, second_ref) = refs[:-3], refs[-3:]
    inner = in_window(iota((256, 256), 0) - iota((256, 256), 1))
    place, column = iota((EDGE, 256), 0), iota((EDGE, 256), 1)
    outer = jnp.concatenate(
        [in_window(place - EDGE - column), in_window(place + 256 - column)], 0
    )
    inner = jnp.concatenate([inner, inner], 0)
    outer = jnp.concatenate([outer, outer], 0)
    done = 0
    for block_ref, one_ref, two_ref in zip(refs[0::3], refs[1::3], refs[2::3]):
        for f in range(block_ref.shape[0]):
            total = jnp.dot(
                jnp.concatenate(two_parts(block_ref[f]), 1), inner, preferred_element_type=f32
            )
            edges = jnp.concatenate(got_edges(is_odd(odd_ref, 0), one_ref, two_ref, f), 0)
            total = total + lax.dot_general(
                jnp.concatenate(two_parts(edges), 0),
                outer,
                (((0,), (0,)), ((), ())),
                preferred_element_type=f32,
            )
            out_ref[done] = total
            put_edges(
                is_odd(odd_ref, 1), total[:EDGE], total[256 - EDGE :], first_ref, second_ref, done
            )
            done += 1


def column_sum(odd, *pieces):
    return pl.pallas_call(
        column_kernel,
        out_shape=block_and_edges(3),
        in_specs=[VMEM] * (1 + len(pieces)),
        out_specs=(VMEM,) * 3,
        compiler_params=pltpu.CompilerParams(vmem_limit_bytes=16 << 20),
        name="column_sum",
    )(odd, *pieces)


def row_kernel(odd_ref, block_ref, one_ref, two_ref, out_ref):
    length = 256 + 2 * EDGE
    band = in_window(iota((256, length), 1) - EDGE - iota((256, length), 0))
    band = jnp.concatenate([band, band], 1)
    for f in range(3):
        before, after = got_edges(is_odd(odd_ref, 1), one_ref, two_ref, f)
        cells = jnp.concatenate([before, block_ref[f], after], 0)
        total = jnp.dot(band, jnp.concatenate(two_parts(cells), 0), preferred_element_type=f32)
        out_ref[f] = total * (1.0 / (4.0 * HALF * HALF))


def row_sum(odd, block, first, second):
    return pl.pallas_call(
        row_kernel,
        out_shape=jax.ShapeDtypeStruct((3, 256, 256), f32),
        in_specs=[VMEM] * 4,
        out_specs=VMEM,
        compiler_params=pltpu.CompilerParams(vmem_limit_bytes=16 << 20),
        name="row_sum",
    )(odd, block, first, second)


def shards(
    e_field, h_field, j_field, material, material_table, dft_e, dft_h, skin_cell, counts,
    patch_slot, area,
):
    magnet_x, magnet_y, magnet_z = (h_field[0], h_field[1], h_field[2])
    rows_below = shifted(jnp.stack([magnet_y[:, -1, :], magnet_z[:, -1, :]]), "gy", 1)
    cols_left = shifted(jnp.stack([magnet_x[:, :, -1], magnet_z[:, :, -1]]), "gx", 1)
    odd = jnp.stack([lax.axis_index("gx") % 2, lax.axis_index("gy") % 2])
    odd = jnp.broadcast_to(odd[:, None], (2, 128))
    area_a, packed, offsets = gather_area_and_pack(counts, skin_cell, patch_slot, area, 2)
    rows_below, cols_left, area_a = lax.optimization_barrier((rows_below, cols_left, area_a))
    e_next, j_next, dft_e_next, dft_h_next, flux = field_step(
        e_field, h_field, j_field, material, material_table, dft_e, dft_h, rows_below, cols_left
    )
    rows = gather_flux(offsets, packed, flux)
    arrived = lax.all_to_all(rows, ("gy", "gx"), split_axis=0, concat_axis=0, tiled=True)
    area_b = gather_area(patch_slot, area, 2, 14)

    blocks, pieces = [], []
    for first, freqs in PIECES:
        block, *edges = scatter_density(odd, patch_slot, area_a, area_b, arrived, first, freqs)
        blocks.append(block)
        pieces += [block, *exchange(*edges, "gx")]
    strip, *edges = column_sum(odd, *pieces)
    edges = exchange(*edges, "gy")
    point_density = jnp.concatenate(blocks, 0)
    avg_density = row_sum(odd, strip, *edges)
    return (e_next, j_next, dft_e_next, dft_h_next, point_density, avg_density)


def solution(mesh):
    placed = (
        P(None, None, "gy", "gx"),
        P(None, None, "gy", "gx"),
        P(None, None, "gy", "gx"),
        P(None, "gy", "gx"),
        P(),
        P(None, None, None, None, "gy", "gx"),
        P(None, None, None, None, "gy", "gx"),
        P(("gy", "gx"), None, None),
        P(("gy", "gx"), None),
        P(("gy", "gx"), None, None),
        P(None, "gy", "gx"),
    )
    return jax.shard_map(
        shards,
        mesh=mesh,
        in_specs=placed,
        out_specs=(
            P(None, None, "gy", "gx"),
            P(None, None, "gy", "gx"),
            P(None, None, None, None, "gy", "gx"),
            P(None, None, None, None, "gy", "gx"),
            P(None, "gy", "gx"),
            P(None, "gy", "gx"),
        ),
        check_vma=False,
    )
```

```python
import functools
import math

import jax
import jax.numpy as jnp
from jax import lax
from jax.experimental import pallas as pl
from jax.experimental.pallas import tpu as pltpu
from jax.sharding import PartitionSpec as P

STEP = 1000
HALF = 100
FREQ_LIST = (28000000000.0, 39000000000.0, 60000000000.0)
TIME_STEP = 1.9e-13

f32 = jnp.float32
bf16 = jnp.bfloat16
f8 = jnp.float8_e4m3fn
TOP = 100000.0
VMEM = pl.BlockSpec(memory_space=pltpu.VMEM)
SMEM = pl.BlockSpec(memory_space=pltpu.SMEM)


def phase_list(offset):
    return [2.0 * math.pi * freq_hz * (STEP + offset) * TIME_STEP for freq_hz in FREQ_LIST]


def iota(shape, dim):
    return lax.broadcasted_iota(jnp.int32, shape, dim)


def shifted(value, axis, steps):
    count = lax.axis_size(axis)
    leading, last = (max(0, -steps), min(count, count - steps))
    return lax.ppermute(value, axis, [(source, source + steps) for source in range(leading, last)])


def exchange(first, second, axis):
    count = lax.axis_size(axis)
    swaps = []
    for start, value in ((1, first), (0, second)):
        lower = range(start, count - 1, 2)
        pairs = [(i, i + 1) for i in lower] + [(i + 1, i) for i in lower]
        swaps.append(lax.ppermute(value, axis, pairs))
    return swaps


def is_odd(odd_ref, axis):
    row = odd_ref[axis : axis + 1, :]
    return jnp.concatenate([row, row], 1) != 0


def put_edges(odd, head, tail, first_ref, second_ref, f):
    first_ref[f] = jnp.where(odd, tail, head)
    second_ref[f] = jnp.where(odd, head, tail)


def got_edges(odd, first_ref, second_ref, f):
    first, second = first_ref[f], second_ref[f]
    return jnp.where(odd, second, first), jnp.where(odd, first, second)


def onehot(count, index):
    places = iota((count, index.shape[1]), 0).astype(bf16)
    return jnp.where(places == index.astype(bf16), jnp.ones((), bf16), jnp.zeros((), bf16))


def largest(values):
    top = jnp.max(jnp.max(jnp.abs(values), axis=0, keepdims=True), axis=1, keepdims=True)
    return jnp.maximum(top, 1e-30)


def split_scaled(values, head_ref, rest_ref):
    top = largest(values)
    values = values * (TOP / top)
    head = values.astype(bf16)
    head_ref[...] = head
    rest_ref[...] = (values - head.astype(f32)).astype(f8)
    return top * (1.0 / TOP)


def edge_kernel(h_ref, row_out, col_out):
    planes, rows, cols = h_ref.shape[1:]
    diagonal = iota((rows, rows), 0) == iota((rows, rows), 1)
    for z in range(planes):
        for part, c in enumerate((1, 2)):
            row_out[part, z : z + 1, :] = h_ref[c, z, rows - 1 : rows, :]
        for part, c in enumerate((0, 2)):
            last = jnp.broadcast_to(h_ref[c, z, :, cols - 1 : cols], (rows, rows))
            col_out[part, z : z + 1, :] = jnp.sum(
                jnp.where(diagonal, last, 0.0), axis=0, keepdims=True
            )


def field_edges(h):
    planes, rows, cols = h.shape[1:]
    return pl.pallas_call(
        edge_kernel,
        out_shape=(
            jax.ShapeDtypeStruct((2, planes, cols), f32),
            jax.ShapeDtypeStruct((2, planes, rows), f32),
        ),
        in_specs=[VMEM],
        out_specs=(VMEM, VMEM),
        compiler_params=pltpu.CompilerParams(vmem_limit_bytes=8 << 20),
        name="field_edges",
    )(h)


def field_plane(
    z, e_ref, h_ref, j_ref, kind_ref, wide_ref, dft_e_ref, dft_h_ref, row_ref, col_ref,
    e_out, j_out, dft_e_out, dft_h_out, flux_out,
):
    rows, cols = kind_ref.shape[1:]
    hx, hy, hz = h_ref[0, z], h_ref[1, z], h_ref[2, z]
    first_row = iota((rows, cols), 0) == 0
    first_col = iota((rows, cols), 1) == 0
    diagonal = iota((rows, rows), 0) == iota((rows, rows), 1)

    def below_x(field, part):
        halo = row_ref[part, z : z + 1, :]
        return jnp.where(first_row, halo, pltpu.roll(field, 1, 0))

    def below_y(field, part):
        halo = col_ref[part, z : z + 1, :]
        halo = jnp.sum(jnp.where(diagonal, halo, 0.0), axis=1, keepdims=True)
        return jnp.where(first_col, halo, pltpu.roll(field, 1, 1))

    zero = jnp.zeros((rows, cols), f32)
    below_z = (h_ref[0, z - 1], h_ref[1, z - 1]) if z else (zero, zero)
    curl = (
        (hz - below_y(hz, 1)) - (hy - below_z[1]),
        (hx - below_z[0]) - (hz - below_x(hz, 1)),
        (hy - below_x(hy, 0)) - (hx - below_y(hx, 0)),
    )
    kinds = kind_ref[z]
    coeffs = [
        jnp.take_along_axis(
            jnp.broadcast_to(wide_ref[r : r + 1, :], (rows, cols)), kinds, axis=1
        )
        for r in range(4)
    ]
    e_next = []
    for c in range(3):
        old_e, old_j = e_ref[c, z], j_ref[c, z]
        new_e = coeffs[0] * old_e + coeffs[1] * (curl[c] - old_j)
        e_out[c, z] = new_e
        j_out[c, z] = coeffs[2] * old_j + coeffs[3] * (new_e - old_e)
        e_next.append(new_e)
    field_h = (hx, hy, hz)
    phase_e, phase_h = phase_list(0.0), phase_list(0.5)
    for f in range(3):
        spec_e, spec_h = [], []
        for part in range(2):
            factor_e = math.cos(phase_e[f]) if part == 0 else -math.sin(phase_e[f])
            factor_h = math.cos(phase_h[f]) if part == 0 else -math.sin(phase_h[f])
            now_e = [dft_e_ref[f, part, c, z] + e_next[c] * factor_e for c in range(3)]
            now_h = [dft_h_ref[f, part, c, z] + field_h[c] * factor_h for c in range(3)]
            for c in range(3):
                dft_e_out[f, part, c, z] = now_e[c]
                dft_h_out[f, part, c, z] = now_h[c]
            spec_e.append(now_e)
            spec_h.append(now_h)
        for c in range(3):
            a, b = (c + 1) % 3, (c + 2) % 3
            flux_out[3 * f + c, z] = 0.5 * (
                (spec_e[0][a] * spec_h[0][b] - spec_e[0][b] * spec_h[0][a])
                + (spec_e[1][a] * spec_h[1][b] - spec_e[1][b] * spec_h[1][a])
            )


def lookup_flux(offset_ref, packed, flux_ref, out_ref, found, head_ref, rest_ref):
    planes = [flux_ref[:, z].reshape(576, 128) for z in range(4)]
    back = split_scaled(jnp.concatenate(planes, 1), head_ref, rest_ref)

    def lookup(c):
        cell = jnp.concatenate([packed[pl.ds(2 * c, 1), :], packed[pl.ds(2 * c + 1, 1), :]], 1)
        plane = lax.bitwise_and(lax.shift_right_logical(cell, 13), 3)
        row = lax.bitwise_and(lax.shift_right_logical(cell, 7), 63)
        inner = lax.bitwise_or(lax.shift_left(plane, 7), lax.bitwise_and(cell, 127))
        hot = jnp.concatenate(
            [onehot(256, inner), onehot(256, jnp.where(inner >= 256, inner - 256, 512))], 0
        )
        result = jnp.dot(head_ref[...], hot, preferred_element_type=f32)
        result = result + jnp.dot(rest_ref[...], hot.astype(f8), preferred_element_type=f32)
        result = result.reshape(9, 64, 256)
        mine = iota((64, 256), 0) == row
        for q in range(9):
            value = jnp.sum(jnp.where(mine, result[q], 0.0), axis=0, keepdims=True) * back
            found[2 * c, q : q + 1, :] = value[:, :128]
            found[2 * c + 1, q : q + 1, :] = value[:, 128:]

    def chunk(c, _):
        for part in range(4):
            lookup(4 * c + part)
        return 0

    lax.fori_loop(0, lax.shift_right_logical(offset_ref[0, 128] + 1023, 10), chunk, 0)
    lanes = iota((16, 128), 1)

    def unpack(d, _):
        offset = offset_ref[0, d]
        row, start = lax.shift_right_logical(offset, 7), lax.bitwise_and(offset, 127)
        live = offset_ref[0, d + 1] - offset
        back = lax.bitwise_and(128 - start, 127)
        value = jnp.where(
            lanes < 128 - start, pltpu.roll(found[row], back, 1), pltpu.roll(found[row + 1], back, 1)
        )
        value = jnp.where(lanes < live, value, 0.0)
        for q in range(9):
            out_ref[d, q] = value[q : q + 1, :]
        return 0

    lax.fori_loop(0, 128, unpack, 0, unroll=32)


def field_kernel(
    offset_ref, packed, e_ref, h_ref, j_ref, kind_ref, table_ref, dft_e_ref, dft_h_ref, row_ref,
    col_ref, e_hbm, j_hbm, dft_e_hbm, dft_h_hbm, out_ref, e_new, j_new, dft_e_new, dft_h_new,
    flux_ref, wide_ref, found, head_ref, rest_ref, sems,
):
    wide_ref[...] = jnp.zeros_like(wide_ref)
    wide_ref[0:4, 0:32] = table_ref[...]
    planes = kind_ref.shape[0]
    copies = []
    for z in range(planes):
        field_plane(
            z, e_ref, h_ref, j_ref, kind_ref, wide_ref, dft_e_ref, dft_h_ref, row_ref, col_ref,
            e_new, j_new, dft_e_new, dft_h_new, flux_ref,
        )
    for i, (new, hbm) in enumerate(
        ((dft_e_new, dft_e_hbm), (dft_h_new, dft_h_hbm), (e_new, e_hbm), (j_new, j_hbm))
    ):
        copy = pltpu.make_async_copy(new, hbm, sems.at[i])
        copy.start()
        copies.append(copy)
    lookup_flux(offset_ref, packed, flux_ref, out_ref, found, head_ref, rest_ref)
    for copy in copies:
        copy.wait()


def field_and_flux(offsets, packed, e, h, j, kinds, table, dft_e, dft_h, rows_below, cols_left):
    planes, rows, cols = kinds.shape
    fields = [e.shape, e.shape, dft_e.shape, dft_h.shape]
    return pl.pallas_call(
        field_kernel,
        out_shape=tuple(jax.ShapeDtypeStruct(shape, f32) for shape in fields)
        + (jax.ShapeDtypeStruct((128, 9, 1, 128), f32),),
        in_specs=[SMEM] + [VMEM] * 10,
        out_specs=(pl.BlockSpec(memory_space=pl.ANY),) * 4 + (VMEM,),
        scratch_shapes=[pltpu.VMEM(shape, f32) for shape in fields]
        + [
            pltpu.VMEM((9, planes, rows, cols), f32),
            pltpu.VMEM((8, cols), f32),
            pltpu.VMEM((136, 16, 128), f32),
            pltpu.VMEM((576, 512), bf16),
            pltpu.VMEM((576, 512), f8),
            pltpu.SemaphoreType.DMA((4,)),
        ],
        compiler_params=pltpu.CompilerParams(vmem_limit_bytes=30 << 20),
        name="field_and_flux",
    )(offsets, packed, e, h, j, kinds, table, dft_e, dft_h, rows_below, cols_left)


GROUP = 8


def slot_row(ref, c):
    return jnp.concatenate([ref[0, pl.ds(GROUP * c + i, 1), :] for i in range(GROUP)], 1)


AREA_SCRATCH = [pltpu.VMEM((384, 512), bf16), pltpu.VMEM((384, 512), f8)]


def split_area(area_ref, head_ref, rest_ref):
    halves = [area_ref[:, :128, :].reshape(384, 256), area_ref[:, 128:, :].reshape(384, 256)]
    return split_scaled(jnp.concatenate(halves, 1), head_ref, rest_ref)


def area_group(patch_ref, head_ref, rest_ref, back, out_ref, c, first):
    patch = slot_row(patch_ref, c + first)
    u, v = lax.shift_right_logical(patch, 8), lax.bitwise_and(patch, 255)
    hot = jnp.concatenate(
        [onehot(256, jnp.where(u < 128, v, 512)), onehot(256, jnp.where(u < 128, 512, v))], 0
    )
    result = jnp.dot(head_ref[...], hot, preferred_element_type=f32)
    result = result + jnp.dot(rest_ref[...], hot.astype(f8), preferred_element_type=f32)
    result = result.reshape(3, 128, GROUP * 128)
    mine = iota((128, GROUP * 128), 0) == lax.bitwise_and(u, 127)
    for q in range(3):
        found = jnp.sum(jnp.where(mine, result[q], 0.0), axis=0, keepdims=True)
        out_ref[c, q : q + 1, :] = found * back


def first_area_kernel(
    count_ref, cell_ref, patch_ref, area_ref, out_ref, packed, offset_ref, head_ref, rest_ref,
    *, groups
):
    back = split_area(area_ref, head_ref, rest_ref)
    lane = iota((1, 128), 1)
    share = 128 // groups

    def chunk(c, carry):
        offset, current = carry
        for i in range(share):
            d = c * share + i
            row, start = lax.shift_right_logical(offset, 7), lax.bitwise_and(offset, 127)
            live = count_ref[0, d]
            offset_ref[0, d] = offset
            rolled = pltpu.roll(cell_ref[0, pl.ds(d, 1), :], start, 1)
            merged = jnp.where(lane >= start, rolled, current)
            packed[pl.ds(row, 1), :] = merged
            current = jnp.where(start + live >= 128, rolled, merged)
            offset = offset + live
        area_group(patch_ref, head_ref, rest_ref, back, out_ref, c, 0)
        return offset, current

    offset, current = lax.fori_loop(
        0, groups, chunk, (jnp.int32(0), jnp.zeros((1, 128), jnp.int32)), unroll=2
    )
    packed[pl.ds(lax.shift_right_logical(offset, 7), 1), :] = current
    offset_ref[0, 128] = offset


def area_kernel(patch_ref, area_ref, out_ref, head_ref, rest_ref, *, first):
    back = split_area(area_ref, head_ref, rest_ref)

    def chunk(c, _):
        area_group(patch_ref, head_ref, rest_ref, back, out_ref, c, first)
        return 0

    lax.fori_loop(0, out_ref.shape[0], chunk, 0, unroll=7)


def area_cost(groups):
    return pl.CostEstimate(
        flops=2 * 768 * 512 * GROUP * 128 * groups, bytes_accessed=2000000, transcendentals=0
    )


def gather_area_and_pack(counts, cells, patch, area, groups):
    return pl.pallas_call(
        functools.partial(first_area_kernel, groups=groups),
        out_shape=(
            jax.ShapeDtypeStruct((groups, 8, GROUP * 128), f32),
            jax.ShapeDtypeStruct((136, 128), jnp.int32),
            jax.ShapeDtypeStruct((1, 136), jnp.int32),
        ),
        in_specs=[SMEM, VMEM, VMEM, VMEM],
        out_specs=(VMEM, VMEM, SMEM),
        scratch_shapes=AREA_SCRATCH,
        compiler_params=pltpu.CompilerParams(vmem_limit_bytes=32 << 20),
        cost_estimate=area_cost(groups),
        name="area_and_pack",
    )(counts, cells, patch, area)


def gather_area(patch, area, first, groups):
    return pl.pallas_call(
        functools.partial(area_kernel, first=first),
        out_shape=jax.ShapeDtypeStruct((groups, 8, GROUP * 128), f32),
        in_specs=[VMEM, VMEM],
        out_specs=VMEM,
        scratch_shapes=AREA_SCRATCH,
        compiler_params=pltpu.CompilerParams(vmem_limit_bytes=32 << 20),
        cost_estimate=area_cost(groups),
        name="gather_area",
    )(patch, area)


EDGE = 104
PIECES = ((0, 2), (2, 1))


def scatter_kernel(
    odd_ref, patch_ref, area_a_ref, area_b_ref, flux_ref, out_ref, first_ref, second_ref, dense,
    *, first
):
    freqs = out_ref.shape[0]
    half, groups = area_a_ref.shape[0], dense.shape[0]
    out_ref[...] = jnp.zeros_like(out_ref)
    top = jnp.zeros((1, GROUP * 128), f32)
    for c in range(groups):
        area = area_a_ref[c] if c < half else area_b_ref[c - half]
        for f in range(freqs):
            density = jnp.zeros((1, GROUP * 128), f32)
            for q in range(3):
                flux = jnp.concatenate(
                    [flux_ref[GROUP * c + i, 3 * (first + f) + q] for i in range(GROUP)], 1
                )
                density = density + area[q : q + 1, :] * flux
            dense[c, f : f + 1, :] = density
            top = jnp.maximum(top, jnp.abs(density))
    top = largest(top)
    scale = TOP / top

    def add_group(c, _):
        patch = slot_row(patch_ref, c)
        u, v = lax.shift_right_logical(patch, 8), lax.bitwise_and(patch, 255)
        hot = onehot(256, v)
        mine = iota((256, GROUP * 128), 0).astype(bf16) == u.astype(bf16)
        heads, rests = [], []
        for f in range(freqs):
            density = dense[c, f : f + 1, :] * scale
            head = density.astype(bf16)
            rest = (density - head.astype(f32)).astype(bf16)
            heads.append(jnp.where(mine, head, jnp.zeros((), bf16)))
            rests.append(jnp.where(mine, rest, jnp.zeros((), bf16)).astype(f8))
        dims = (((1,), (1,)), ((), ()))
        total = lax.dot_general(jnp.concatenate(heads, 0), hot, dims, preferred_element_type=f32)
        total = total + lax.dot_general(
            jnp.concatenate(rests, 0), hot.astype(f8), dims, preferred_element_type=f32
        )
        out_ref[...] += total.reshape(freqs, 256, 256)
        return 0

    lax.fori_loop(0, groups, add_group, 0, unroll=8)
    out_ref[...] = out_ref[...] * (top * (1.0 / TOP)).reshape(1, 1, 1)
    for f in range(freqs):
        head = jnp.transpose(out_ref[f, :, :128])[:EDGE]
        tail = jnp.transpose(out_ref[f, :, 128:])[128 - EDGE :]
        put_edges(is_odd(odd_ref, 0), head, tail, first_ref, second_ref, f)


def block_and_edges(freqs):
    return (
        jax.ShapeDtypeStruct((freqs, 256, 256), f32),
        jax.ShapeDtypeStruct((freqs, EDGE, 256), f32),
        jax.ShapeDtypeStruct((freqs, EDGE, 256), f32),
    )


def scatter_density(odd, patch, area_a, area_b, flux, first, freqs):
    return pl.pallas_call(
        functools.partial(scatter_kernel, first=first),
        out_shape=block_and_edges(freqs),
        in_specs=[VMEM] * 5,
        out_specs=(VMEM,) * 3,
        scratch_shapes=[pltpu.VMEM((128 // GROUP, 8, GROUP * 128), f32)],
        compiler_params=pltpu.CompilerParams(vmem_limit_bytes=36 << 20),
        cost_estimate=pl.CostEstimate(
            flops=2 * freqs * 65536 * 2 * 16384, bytes_accessed=2000000, transcendentals=0
        ),
        name="scatter_density",
    )(odd, patch, area_a, area_b, flux)


def in_window(place):
    return jnp.where((place >= -HALF) & (place < HALF), 1.0, 0.0).astype(bf16)


def two_parts(cells):
    head = cells.astype(bf16)
    return head, (cells - head.astype(f32)).astype(bf16)


def column_kernel(odd_ref, *refs):
    refs, (out_ref, first_ref, second_ref) = refs[:-3], refs[-3:]
    inner = in_window(iota((256, 256), 0) - iota((256, 256), 1))
    place, column = iota((EDGE, 256), 0), iota((EDGE, 256), 1)
    outer = jnp.concatenate(
        [in_window(place - EDGE - column), in_window(place + 256 - column)], 0
    )
    inner = jnp.concatenate([inner, inner], 0)
    outer = jnp.concatenate([outer, outer], 0)
    done = 0
    for block_ref, one_ref, two_ref in zip(refs[0::3], refs[1::3], refs[2::3]):
        for f in range(block_ref.shape[0]):
            total = jnp.dot(
                jnp.concatenate(two_parts(block_ref[f]), 1), inner, preferred_element_type=f32
            )
            edges = jnp.concatenate(got_edges(is_odd(odd_ref, 0), one_ref, two_ref, f), 0)
            total = total + lax.dot_general(
                jnp.concatenate(two_parts(edges), 0),
                outer,
                (((0,), (0,)), ((), ())),
                preferred_element_type=f32,
            )
            out_ref[done] = total
            put_edges(
                is_odd(odd_ref, 1), total[:EDGE], total[256 - EDGE :], first_ref, second_ref, done
            )
            done += 1


def column_sum(odd, *pieces):
    return pl.pallas_call(
        column_kernel,
        out_shape=block_and_edges(3),
        in_specs=[VMEM] * (1 + len(pieces)),
        out_specs=(VMEM,) * 3,
        compiler_params=pltpu.CompilerParams(vmem_limit_bytes=16 << 20),
        name="column_sum",
    )(odd, *pieces)


def row_kernel(odd_ref, block_ref, one_ref, two_ref, out_ref):
    length = 256 + 2 * EDGE
    band = in_window(iota((256, length), 1) - EDGE - iota((256, length), 0))
    band = jnp.concatenate([band, band], 1)
    for f in range(3):
        before, after = got_edges(is_odd(odd_ref, 1), one_ref, two_ref, f)
        cells = jnp.concatenate([before, block_ref[f], after], 0)
        total = jnp.dot(band, jnp.concatenate(two_parts(cells), 0), preferred_element_type=f32)
        out_ref[f] = total * (1.0 / (4.0 * HALF * HALF))


def row_sum(odd, block, first, second):
    return pl.pallas_call(
        row_kernel,
        out_shape=jax.ShapeDtypeStruct((3, 256, 256), f32),
        in_specs=[VMEM] * 4,
        out_specs=VMEM,
        compiler_params=pltpu.CompilerParams(vmem_limit_bytes=16 << 20),
        name="row_sum",
    )(odd, block, first, second)


def shards(
    e_field, h_field, j_field, material, material_table, dft_e, dft_h, skin_cell, counts,
    patch_slot, area,
):
    last_rows, last_cols = field_edges(h_field)
    rows_below = shifted(last_rows, "gy", 1)
    cols_left = shifted(last_cols, "gx", 1)
    odd = jnp.stack([lax.axis_index("gx") % 2, lax.axis_index("gy") % 2])
    odd = jnp.broadcast_to(odd[:, None], (2, 128))
    area_a, packed, offsets = gather_area_and_pack(counts, skin_cell, patch_slot, area, 2)
    rows_below, cols_left, area_a = lax.optimization_barrier((rows_below, cols_left, area_a))
    e_next, j_next, dft_e_next, dft_h_next, rows = field_and_flux(
        offsets, packed, e_field, h_field, j_field, material, material_table, dft_e, dft_h,
        rows_below, cols_left,
    )
    arrived = lax.all_to_all(rows, ("gy", "gx"), split_axis=0, concat_axis=0, tiled=True)
    area_b = gather_area(patch_slot, area, 2, 14)

    blocks, pieces = [], []
    for first, freqs in PIECES:
        block, *edges = scatter_density(odd, patch_slot, area_a, area_b, arrived, first, freqs)
        blocks.append(block)
        pieces += [block, *exchange(*edges, "gx")]
    strip, *edges = column_sum(odd, *pieces)
    edges = exchange(*edges, "gy")
    point_density = jnp.concatenate(blocks, 0)
    avg_density = row_sum(odd, strip, *edges)
    return (e_next, j_next, dft_e_next, dft_h_next, point_density, avg_density)


def solution(mesh):
    placed = (
        P(None, None, "gy", "gx"),
        P(None, None, "gy", "gx"),
        P(None, None, "gy", "gx"),
        P(None, "gy", "gx"),
        P(),
        P(None, None, None, None, "gy", "gx"),
        P(None, None, None, None, "gy", "gx"),
        P(("gy", "gx"), None, None),
        P(("gy", "gx"), None),
        P(("gy", "gx"), None, None),
        P(None, "gy", "gx"),
    )
    return jax.shard_map(
        shards,
        mesh=mesh,
        in_specs=placed,
        out_specs=(
            P(None, None, "gy", "gx"),
            P(None, None, "gy", "gx"),
            P(None, None, None, None, "gy", "gx"),
            P(None, None, None, None, "gy", "gx"),
            P(None, "gy", "gx"),
            P(None, "gy", "gx"),
        ),
        check_vma=False,
    )
```

```python
import functools
import math

import jax
import jax.numpy as jnp
from jax import lax
from jax.experimental import pallas as pl
from jax.experimental.pallas import tpu as pltpu
from jax.sharding import PartitionSpec as P

STEP = 1000
HALF = 100
FREQ_LIST = (28000000000.0, 39000000000.0, 60000000000.0)
TIME_STEP = 1.9e-13

f32 = jnp.float32
bf16 = jnp.bfloat16
f8 = jnp.float8_e4m3fn
TOP = 100000.0
VMEM = pl.BlockSpec(memory_space=pltpu.VMEM)
SMEM = pl.BlockSpec(memory_space=pltpu.SMEM)


def phase_list(offset):
    return [2.0 * math.pi * freq_hz * (STEP + offset) * TIME_STEP for freq_hz in FREQ_LIST]


def iota(shape, dim):
    return lax.broadcasted_iota(jnp.int32, shape, dim)


def shifted(value, axis, steps):
    count = lax.axis_size(axis)
    leading, last = (max(0, -steps), min(count, count - steps))
    return lax.ppermute(value, axis, [(source, source + steps) for source in range(leading, last)])


def exchange(first, second, axis):
    count = lax.axis_size(axis)
    swaps = []
    for start, value in ((1, first), (0, second)):
        lower = range(start, count - 1, 2)
        pairs = [(i, i + 1) for i in lower] + [(i + 1, i) for i in lower]
        swaps.append(lax.ppermute(value, axis, pairs))
    return swaps


def is_odd(odd_ref, axis):
    row = odd_ref[axis : axis + 1, :]
    return jnp.concatenate([row, row], 1) != 0


def put_edges(odd, head, tail, first_ref, second_ref, f):
    first_ref[f] = jnp.where(odd, tail, head)
    second_ref[f] = jnp.where(odd, head, tail)


def got_edges(odd, first_ref, second_ref, f):
    first, second = first_ref[f], second_ref[f]
    return jnp.where(odd, second, first), jnp.where(odd, first, second)


def onehot(count, index):
    places = iota((count, index.shape[1]), 0).astype(bf16)
    return jnp.where(places == index.astype(bf16), jnp.ones((), bf16), jnp.zeros((), bf16))


def largest(values):
    top = jnp.max(jnp.max(jnp.abs(values), axis=0, keepdims=True), axis=1, keepdims=True)
    return jnp.maximum(top, 1e-30)


def split_scaled(values, head_ref, rest_ref):
    top = largest(values)
    values = values * (TOP / top)
    head = values.astype(bf16)
    head_ref[...] = head
    rest_ref[...] = (values - head.astype(f32)).astype(f8)
    return top * (1.0 / TOP)


def edge_kernel(h_ref, row_out, col_out):
    planes, rows, cols = h_ref.shape[1:]
    diagonal = iota((rows, rows), 0) == iota((rows, rows), 1)
    for z in range(planes):
        for part, c in enumerate((1, 2)):
            row_out[part, z : z + 1, :] = h_ref[c, z, rows - 1 : rows, :]
        for part, c in enumerate((0, 2)):
            last = jnp.broadcast_to(h_ref[c, z, :, cols - 1 : cols], (rows, rows))
            col_out[part, z : z + 1, :] = jnp.sum(
                jnp.where(diagonal, last, 0.0), axis=0, keepdims=True
            )


def field_edges(h):
    planes, rows, cols = h.shape[1:]
    return pl.pallas_call(
        edge_kernel,
        out_shape=(
            jax.ShapeDtypeStruct((2, planes, cols), f32),
            jax.ShapeDtypeStruct((2, planes, rows), f32),
        ),
        in_specs=[VMEM],
        out_specs=(VMEM, VMEM),
        compiler_params=pltpu.CompilerParams(vmem_limit_bytes=8 << 20),
        cost_estimate=pl.CostEstimate(flops=3000000000, bytes_accessed=1000000, transcendentals=0),
        name="field_edges",
    )(h)


def field_plane(
    z, e_ref, h_ref, j_ref, kind_ref, wide_ref, dft_e_ref, dft_h_ref, row_ref, col_ref,
    e_out, j_out, dft_e_out, dft_h_out, flux_out,
):
    rows, cols = kind_ref.shape[1:]
    hx, hy, hz = h_ref[0, z], h_ref[1, z], h_ref[2, z]
    first_row = iota((rows, cols), 0) == 0
    first_col = iota((rows, cols), 1) == 0
    diagonal = iota((rows, rows), 0) == iota((rows, rows), 1)

    def below_x(field, part):
        halo = row_ref[part, z : z + 1, :]
        return jnp.where(first_row, halo, pltpu.roll(field, 1, 0))

    def below_y(field, part):
        halo = col_ref[part, z : z + 1, :]
        halo = jnp.sum(jnp.where(diagonal, halo, 0.0), axis=1, keepdims=True)
        return jnp.where(first_col, halo, pltpu.roll(field, 1, 1))

    zero = jnp.zeros((rows, cols), f32)
    below_z = (h_ref[0, z - 1], h_ref[1, z - 1]) if z else (zero, zero)
    curl = (
        (hz - below_y(hz, 1)) - (hy - below_z[1]),
        (hx - below_z[0]) - (hz - below_x(hz, 1)),
        (hy - below_x(hy, 0)) - (hx - below_y(hx, 0)),
    )
    kinds = kind_ref[z]
    coeffs = [
        jnp.take_along_axis(
            jnp.broadcast_to(wide_ref[r : r + 1, :], (rows, cols)), kinds, axis=1
        )
        for r in range(4)
    ]
    e_next = []
    for c in range(3):
        old_e, old_j = e_ref[c, z], j_ref[c, z]
        new_e = coeffs[0] * old_e + coeffs[1] * (curl[c] - old_j)
        e_out[c, z] = new_e
        j_out[c, z] = coeffs[2] * old_j + coeffs[3] * (new_e - old_e)
        e_next.append(new_e)
    field_h = (hx, hy, hz)
    phase_e, phase_h = phase_list(0.0), phase_list(0.5)
    for f in range(3):
        spec_e, spec_h = [], []
        for part in range(2):
            factor_e = math.cos(phase_e[f]) if part == 0 else -math.sin(phase_e[f])
            factor_h = math.cos(phase_h[f]) if part == 0 else -math.sin(phase_h[f])
            now_e = [dft_e_ref[f, part, c, z] + e_next[c] * factor_e for c in range(3)]
            now_h = [dft_h_ref[f, part, c, z] + field_h[c] * factor_h for c in range(3)]
            for c in range(3):
                dft_e_out[f, part, c, z] = now_e[c]
                dft_h_out[f, part, c, z] = now_h[c]
            spec_e.append(now_e)
            spec_h.append(now_h)
        for c in range(3):
            a, b = (c + 1) % 3, (c + 2) % 3
            flux_out[3 * f + c, z] = 0.5 * (
                (spec_e[0][a] * spec_h[0][b] - spec_e[0][b] * spec_h[0][a])
                + (spec_e[1][a] * spec_h[1][b] - spec_e[1][b] * spec_h[1][a])
            )


def lookup_flux(offset_ref, packed, flux_ref, out_ref, found, head_ref, rest_ref):
    planes = [flux_ref[:, z].reshape(576, 128) for z in range(4)]
    back = split_scaled(jnp.concatenate(planes, 1), head_ref, rest_ref)

    def lookup(c):
        cell = jnp.concatenate([packed[pl.ds(2 * c, 1), :], packed[pl.ds(2 * c + 1, 1), :]], 1)
        plane = lax.bitwise_and(lax.shift_right_logical(cell, 13), 3)
        row = lax.bitwise_and(lax.shift_right_logical(cell, 7), 63)
        inner = lax.bitwise_or(lax.shift_left(plane, 7), lax.bitwise_and(cell, 127))
        hot = jnp.concatenate(
            [onehot(256, inner), onehot(256, jnp.where(inner >= 256, inner - 256, 512))], 0
        )
        result = jnp.dot(head_ref[...], hot, preferred_element_type=f32)
        result = result + jnp.dot(rest_ref[...], hot.astype(f8), preferred_element_type=f32)
        result = result.reshape(9, 64, 256)
        mine = iota((64, 256), 0) == row
        for q in range(9):
            value = jnp.sum(jnp.where(mine, result[q], 0.0), axis=0, keepdims=True) * back
            found[2 * c, q : q + 1, :] = value[:, :128]
            found[2 * c + 1, q : q + 1, :] = value[:, 128:]

    def chunk(c, _):
        for part in range(4):
            lookup(4 * c + part)
        return 0

    lax.fori_loop(0, lax.shift_right_logical(offset_ref[0, 128] + 1023, 10), chunk, 0)
    lanes = iota((16, 128), 1)

    def unpack(d, _):
        offset = offset_ref[0, d]
        row, start = lax.shift_right_logical(offset, 7), lax.bitwise_and(offset, 127)
        live = offset_ref[0, d + 1] - offset
        back = lax.bitwise_and(128 - start, 127)
        value = jnp.where(
            lanes < 128 - start, pltpu.roll(found[row], back, 1), pltpu.roll(found[row + 1], back, 1)
        )
        value = jnp.where(lanes < live, value, 0.0)
        for q in range(9):
            out_ref[d, q] = value[q : q + 1, :]
        return 0

    lax.fori_loop(0, 128, unpack, 0, unroll=32)


def field_kernel(
    offset_ref, packed, e_ref, h_ref, j_ref, kind_ref, table_ref, dft_e_ref, dft_h_ref, row_ref,
    col_ref, e_hbm, j_hbm, dft_e_hbm, dft_h_hbm, out_ref, e_new, j_new, dft_e_new, dft_h_new,
    flux_ref, wide_ref, found, head_ref, rest_ref, sems,
):
    wide_ref[...] = jnp.zeros_like(wide_ref)
    wide_ref[0:4, 0:32] = table_ref[...]
    planes = kind_ref.shape[0]
    copies = []
    for z in range(planes):
        field_plane(
            z, e_ref, h_ref, j_ref, kind_ref, wide_ref, dft_e_ref, dft_h_ref, row_ref, col_ref,
            e_new, j_new, dft_e_new, dft_h_new, flux_ref,
        )
    for i, (new, hbm) in enumerate(
        ((dft_e_new, dft_e_hbm), (dft_h_new, dft_h_hbm), (e_new, e_hbm), (j_new, j_hbm))
    ):
        copy = pltpu.make_async_copy(new, hbm, sems.at[i])
        copy.start()
        copies.append(copy)
    lookup_flux(offset_ref, packed, flux_ref, out_ref, found, head_ref, rest_ref)
    for copy in copies:
        copy.wait()


def field_and_flux(offsets, packed, e, h, j, kinds, table, dft_e, dft_h, rows_below, cols_left):
    planes, rows, cols = kinds.shape
    fields = [e.shape, e.shape, dft_e.shape, dft_h.shape]
    return pl.pallas_call(
        field_kernel,
        out_shape=tuple(jax.ShapeDtypeStruct(shape, f32) for shape in fields)
        + (jax.ShapeDtypeStruct((128, 9, 1, 128), f32),),
        in_specs=[SMEM] + [VMEM] * 10,
        out_specs=(pl.BlockSpec(memory_space=pl.ANY),) * 4 + (VMEM,),
        scratch_shapes=[pltpu.VMEM(shape, f32) for shape in fields]
        + [
            pltpu.VMEM((9, planes, rows, cols), f32),
            pltpu.VMEM((8, cols), f32),
            pltpu.VMEM((136, 16, 128), f32),
            pltpu.VMEM((576, 512), bf16),
            pltpu.VMEM((576, 512), f8),
            pltpu.SemaphoreType.DMA((4,)),
        ],
        compiler_params=pltpu.CompilerParams(vmem_limit_bytes=30 << 20),
        name="field_and_flux",
    )(offsets, packed, e, h, j, kinds, table, dft_e, dft_h, rows_below, cols_left)


GROUP = 8


def slot_row(ref, c):
    return jnp.concatenate([ref[0, pl.ds(GROUP * c + i, 1), :] for i in range(GROUP)], 1)


AREA_SCRATCH = [pltpu.VMEM((384, 512), bf16), pltpu.VMEM((384, 512), f8)]


def split_area(area_ref, head_ref, rest_ref):
    halves = [area_ref[:, :128, :].reshape(384, 256), area_ref[:, 128:, :].reshape(384, 256)]
    return split_scaled(jnp.concatenate(halves, 1), head_ref, rest_ref)


def area_group(patch_ref, head_ref, rest_ref, back, out_ref, c, first):
    patch = slot_row(patch_ref, c + first)
    u, v = lax.shift_right_logical(patch, 8), lax.bitwise_and(patch, 255)
    hot = jnp.concatenate(
        [onehot(256, jnp.where(u < 128, v, 512)), onehot(256, jnp.where(u < 128, 512, v))], 0
    )
    result = jnp.dot(head_ref[...], hot, preferred_element_type=f32)
    result = result + jnp.dot(rest_ref[...], hot.astype(f8), preferred_element_type=f32)
    result = result.reshape(3, 128, GROUP * 128)
    mine = iota((128, GROUP * 128), 0) == lax.bitwise_and(u, 127)
    for q in range(3):
        found = jnp.sum(jnp.where(mine, result[q], 0.0), axis=0, keepdims=True)
        out_ref[c, q : q + 1, :] = found * back


def first_area_kernel(
    count_ref, cell_ref, patch_ref, area_ref, out_ref, packed, offset_ref, head_ref, rest_ref,
    *, groups
):
    back = split_area(area_ref, head_ref, rest_ref)
    lane = iota((1, 128), 1)
    share = 128 // groups

    def chunk(c, carry):
        offset, current = carry
        for i in range(share):
            d = c * share + i
            row, start = lax.shift_right_logical(offset, 7), lax.bitwise_and(offset, 127)
            live = count_ref[0, d]
            offset_ref[0, d] = offset
            rolled = pltpu.roll(cell_ref[0, pl.ds(d, 1), :], start, 1)
            merged = jnp.where(lane >= start, rolled, current)
            packed[pl.ds(row, 1), :] = merged
            current = jnp.where(start + live >= 128, rolled, merged)
            offset = offset + live
        area_group(patch_ref, head_ref, rest_ref, back, out_ref, c, 0)
        return offset, current

    offset, current = lax.fori_loop(
        0, groups, chunk, (jnp.int32(0), jnp.zeros((1, 128), jnp.int32)), unroll=2
    )
    packed[pl.ds(lax.shift_right_logical(offset, 7), 1), :] = current
    offset_ref[0, 128] = offset


def area_kernel(patch_ref, area_ref, out_ref, head_ref, rest_ref, *, first):
    back = split_area(area_ref, head_ref, rest_ref)

    def chunk(c, _):
        area_group(patch_ref, head_ref, rest_ref, back, out_ref, c, first)
        return 0

    lax.fori_loop(0, out_ref.shape[0], chunk, 0, unroll=5)


def area_cost(groups):
    return pl.CostEstimate(
        flops=2 * 768 * 512 * GROUP * 128 * groups, bytes_accessed=2000000, transcendentals=0
    )


def gather_area_and_pack(counts, cells, patch, area, groups):
    return pl.pallas_call(
        functools.partial(first_area_kernel, groups=groups),
        out_shape=(
            jax.ShapeDtypeStruct((groups, 8, GROUP * 128), f32),
            jax.ShapeDtypeStruct((136, 128), jnp.int32),
            jax.ShapeDtypeStruct((1, 136), jnp.int32),
        ),
        in_specs=[SMEM, VMEM, VMEM, VMEM],
        out_specs=(VMEM, VMEM, SMEM),
        scratch_shapes=AREA_SCRATCH,
        compiler_params=pltpu.CompilerParams(vmem_limit_bytes=32 << 20),
        cost_estimate=area_cost(groups),
        name="area_and_pack",
    )(counts, cells, patch, area)


def gather_area(patch, area, first, groups):
    return pl.pallas_call(
        functools.partial(area_kernel, first=first),
        out_shape=jax.ShapeDtypeStruct((groups, 8, GROUP * 128), f32),
        in_specs=[VMEM, VMEM],
        out_specs=VMEM,
        scratch_shapes=AREA_SCRATCH,
        compiler_params=pltpu.CompilerParams(vmem_limit_bytes=32 << 20),
        cost_estimate=area_cost(groups),
        name="gather_area",
    )(patch, area)


EDGE = 104
PIECES = ((0, 2), (2, 1))


def scatter_kernel(
    odd_ref, patch_ref, area_a_ref, area_b_ref, flux_ref, out_ref, first_ref, second_ref, dense,
    *, first
):
    freqs = out_ref.shape[0]
    half, groups = area_a_ref.shape[0], dense.shape[0]
    out_ref[...] = jnp.zeros_like(out_ref)
    top = jnp.zeros((1, GROUP * 128), f32)
    for c in range(groups):
        area = area_a_ref[c] if c < half else area_b_ref[c - half]
        for f in range(freqs):
            density = jnp.zeros((1, GROUP * 128), f32)
            for q in range(3):
                flux = jnp.concatenate(
                    [flux_ref[GROUP * c + i, 3 * (first + f) + q] for i in range(GROUP)], 1
                )
                density = density + area[q : q + 1, :] * flux
            dense[c, f : f + 1, :] = density
            top = jnp.maximum(top, jnp.abs(density))
    top = largest(top)
    scale = TOP / top

    def add_group(c, _):
        patch = slot_row(patch_ref, c)
        u, v = lax.shift_right_logical(patch, 8), lax.bitwise_and(patch, 255)
        hot = onehot(256, v)
        mine = iota((256, GROUP * 128), 0).astype(bf16) == u.astype(bf16)
        heads, rests = [], []
        for f in range(freqs):
            density = dense[c, f : f + 1, :] * scale
            head = density.astype(bf16)
            rest = (density - head.astype(f32)).astype(bf16)
            heads.append(jnp.where(mine, head, jnp.zeros((), bf16)))
            rests.append(jnp.where(mine, rest, jnp.zeros((), bf16)).astype(f8))
        dims = (((1,), (1,)), ((), ()))
        total = lax.dot_general(jnp.concatenate(heads, 0), hot, dims, preferred_element_type=f32)
        total = total + lax.dot_general(
            jnp.concatenate(rests, 0), hot.astype(f8), dims, preferred_element_type=f32
        )
        out_ref[...] += total.reshape(freqs, 256, 256)
        return 0

    lax.fori_loop(0, groups, add_group, 0, unroll=8)
    out_ref[...] = out_ref[...] * (top * (1.0 / TOP)).reshape(1, 1, 1)
    for f in range(freqs):
        head = jnp.transpose(out_ref[f, :, :128])[:EDGE]
        tail = jnp.transpose(out_ref[f, :, 128:])[128 - EDGE :]
        put_edges(is_odd(odd_ref, 0), head, tail, first_ref, second_ref, f)


def block_and_edges(freqs):
    return (
        jax.ShapeDtypeStruct((freqs, 256, 256), f32),
        jax.ShapeDtypeStruct((freqs, EDGE, 256), f32),
        jax.ShapeDtypeStruct((freqs, EDGE, 256), f32),
    )


def scatter_density(odd, patch, area_a, area_b, flux, first, freqs):
    return pl.pallas_call(
        functools.partial(scatter_kernel, first=first),
        out_shape=block_and_edges(freqs),
        in_specs=[VMEM] * 5,
        out_specs=(VMEM,) * 3,
        scratch_shapes=[pltpu.VMEM((128 // GROUP, 8, GROUP * 128), f32)],
        compiler_params=pltpu.CompilerParams(vmem_limit_bytes=36 << 20),
        cost_estimate=pl.CostEstimate(
            flops=2 * freqs * 65536 * 2 * 16384, bytes_accessed=2000000, transcendentals=0
        ),
        name="scatter_density",
    )(odd, patch, area_a, area_b, flux)


def in_window(place):
    return jnp.where((place >= -HALF) & (place < HALF), 1.0, 0.0).astype(bf16)


def two_parts(cells):
    head = cells.astype(bf16)
    return head, (cells - head.astype(f32)).astype(bf16)


def column_kernel(odd_ref, *refs):
    refs, (out_ref, first_ref, second_ref) = refs[:-3], refs[-3:]
    inner = in_window(iota((256, 256), 0) - iota((256, 256), 1))
    place, column = iota((EDGE, 256), 0), iota((EDGE, 256), 1)
    outer = jnp.concatenate(
        [in_window(place - EDGE - column), in_window(place + 256 - column)], 0
    )
    inner = jnp.concatenate([inner, inner], 0)
    outer = jnp.concatenate([outer, outer], 0)
    done = 0
    for block_ref, one_ref, two_ref in zip(refs[0::3], refs[1::3], refs[2::3]):
        for f in range(block_ref.shape[0]):
            total = jnp.dot(
                jnp.concatenate(two_parts(block_ref[f]), 1), inner, preferred_element_type=f32
            )
            edges = jnp.concatenate(got_edges(is_odd(odd_ref, 0), one_ref, two_ref, f), 0)
            total = total + lax.dot_general(
                jnp.concatenate(two_parts(edges), 0),
                outer,
                (((0,), (0,)), ((), ())),
                preferred_element_type=f32,
            )
            out_ref[done] = total
            put_edges(
                is_odd(odd_ref, 1), total[:EDGE], total[256 - EDGE :], first_ref, second_ref, done
            )
            done += 1


def column_sum(odd, *pieces):
    return pl.pallas_call(
        column_kernel,
        out_shape=block_and_edges(3),
        in_specs=[VMEM] * (1 + len(pieces)),
        out_specs=(VMEM,) * 3,
        compiler_params=pltpu.CompilerParams(vmem_limit_bytes=16 << 20),
        name="column_sum",
    )(odd, *pieces)


def row_kernel(odd_ref, block_ref, one_ref, two_ref, out_ref):
    length = 256 + 2 * EDGE
    band = in_window(iota((256, length), 1) - EDGE - iota((256, length), 0))
    band = jnp.concatenate([band, band], 1)
    for f in range(3):
        before, after = got_edges(is_odd(odd_ref, 1), one_ref, two_ref, f)
        cells = jnp.concatenate([before, block_ref[f], after], 0)
        total = jnp.dot(band, jnp.concatenate(two_parts(cells), 0), preferred_element_type=f32)
        out_ref[f] = total * (1.0 / (4.0 * HALF * HALF))


def row_sum(odd, block, first, second):
    return pl.pallas_call(
        row_kernel,
        out_shape=jax.ShapeDtypeStruct((3, 256, 256), f32),
        in_specs=[VMEM] * 4,
        out_specs=VMEM,
        compiler_params=pltpu.CompilerParams(vmem_limit_bytes=16 << 20),
        name="row_sum",
    )(odd, block, first, second)


def shards(
    e_field, h_field, j_field, material, material_table, dft_e, dft_h, skin_cell, counts,
    patch_slot, area,
):
    last_rows, last_cols = field_edges(h_field)
    rows_below = shifted(last_rows, "gy", 1)
    cols_left = shifted(last_cols, "gx", 1)
    odd = jnp.stack([lax.axis_index("gx") % 2, lax.axis_index("gy") % 2])
    odd = jnp.broadcast_to(odd[:, None], (2, 128))
    area_a, packed, offsets = gather_area_and_pack(counts, skin_cell, patch_slot, area, 1)
    rows_below, cols_left, area_a = lax.optimization_barrier((rows_below, cols_left, area_a))
    e_next, j_next, dft_e_next, dft_h_next, rows = field_and_flux(
        offsets, packed, e_field, h_field, j_field, material, material_table, dft_e, dft_h,
        rows_below, cols_left,
    )
    arrived = lax.all_to_all(rows, ("gy", "gx"), split_axis=0, concat_axis=0, tiled=True)
    area_b = gather_area(patch_slot, area, 1, 15)

    blocks, pieces = [], []
    for first, freqs in PIECES:
        block, *edges = scatter_density(odd, patch_slot, area_a, area_b, arrived, first, freqs)
        blocks.append(block)
        pieces += [block, *exchange(*edges, "gx")]
    strip, *edges = column_sum(odd, *pieces)
    edges = exchange(*edges, "gy")
    point_density = jnp.concatenate(blocks, 0)
    avg_density = row_sum(odd, strip, *edges)
    return (e_next, j_next, dft_e_next, dft_h_next, point_density, avg_density)


def solution(mesh):
    placed = (
        P(None, None, "gy", "gx"),
        P(None, None, "gy", "gx"),
        P(None, None, "gy", "gx"),
        P(None, "gy", "gx"),
        P(),
        P(None, None, None, None, "gy", "gx"),
        P(None, None, None, None, "gy", "gx"),
        P(("gy", "gx"), None, None),
        P(("gy", "gx"), None),
        P(("gy", "gx"), None, None),
        P(None, "gy", "gx"),
    )
    return jax.shard_map(
        shards,
        mesh=mesh,
        in_specs=placed,
        out_specs=(
            P(None, None, "gy", "gx"),
            P(None, None, "gy", "gx"),
            P(None, None, None, None, "gy", "gx"),
            P(None, None, None, None, "gy", "gx"),
            P(None, "gy", "gx"),
            P(None, "gy", "gx"),
        ),
        check_vma=False,
    )
```

```python
import functools
import math

import jax
import jax.numpy as jnp
from jax import lax
from jax.experimental import pallas as pl
from jax.experimental.pallas import tpu as pltpu
from jax.sharding import PartitionSpec as P

STEP = 1000
HALF = 100
FREQ_LIST = (28000000000.0, 39000000000.0, 60000000000.0)
TIME_STEP = 1.9e-13

f32 = jnp.float32
bf16 = jnp.bfloat16
f8 = jnp.float8_e4m3fn
TOP = 100000.0
VMEM = pl.BlockSpec(memory_space=pltpu.VMEM)
SMEM = pl.BlockSpec(memory_space=pltpu.SMEM)


def phase_list(offset):
    return [2.0 * math.pi * freq_hz * (STEP + offset) * TIME_STEP for freq_hz in FREQ_LIST]


def iota(shape, dim):
    return lax.broadcasted_iota(jnp.int32, shape, dim)


def shifted(value, axis, steps):
    count = lax.axis_size(axis)
    leading, last = (max(0, -steps), min(count, count - steps))
    return lax.ppermute(value, axis, [(source, source + steps) for source in range(leading, last)])


def exchange(first, second, axis):
    count = lax.axis_size(axis)
    swaps = []
    for start, value in ((1, first), (0, second)):
        lower = range(start, count - 1, 2)
        pairs = [(i, i + 1) for i in lower] + [(i + 1, i) for i in lower]
        swaps.append(lax.ppermute(value, axis, pairs))
    return swaps


def is_odd(odd_ref, axis):
    row = odd_ref[axis : axis + 1, :]
    return jnp.concatenate([row, row], 1) != 0


def put_edges(odd, head, tail, first_ref, second_ref, f):
    first_ref[f] = jnp.where(odd, tail, head)
    second_ref[f] = jnp.where(odd, head, tail)


def got_edges(odd, first_ref, second_ref, f):
    first, second = first_ref[f], second_ref[f]
    return jnp.where(odd, second, first), jnp.where(odd, first, second)


def onehot(count, index):
    places = iota((count, index.shape[1]), 0).astype(bf16)
    return jnp.where(places == index.astype(bf16), jnp.ones((), bf16), jnp.zeros((), bf16))


def largest(values):
    top = jnp.max(jnp.max(jnp.abs(values), axis=0, keepdims=True), axis=1, keepdims=True)
    return jnp.maximum(top, 1e-30)


def split_scaled(values, head_ref, rest_ref):
    top = largest(values)
    values = values * (TOP / top)
    head = values.astype(bf16)
    head_ref[...] = head
    rest_ref[...] = (values - head.astype(f32)).astype(f8)
    return top * (1.0 / TOP)


def edge_kernel(h_ref, row_out, col_out):
    planes, rows, cols = h_ref.shape[1:]
    diagonal = iota((rows, rows), 0) == iota((rows, rows), 1)
    for z in range(planes):
        for part, c in enumerate((1, 2)):
            row_out[part, z : z + 1, :] = h_ref[c, z, rows - 1 : rows, :]
        for part, c in enumerate((0, 2)):
            last = jnp.broadcast_to(h_ref[c, z, :, cols - 1 : cols], (rows, rows))
            col_out[part, z : z + 1, :] = jnp.sum(
                jnp.where(diagonal, last, 0.0), axis=0, keepdims=True
            )


def field_edges(h):
    planes, rows, cols = h.shape[1:]
    return pl.pallas_call(
        edge_kernel,
        out_shape=(
            jax.ShapeDtypeStruct((2, planes, cols), f32),
            jax.ShapeDtypeStruct((2, planes, rows), f32),
        ),
        in_specs=[VMEM],
        out_specs=(VMEM, VMEM),
        compiler_params=pltpu.CompilerParams(vmem_limit_bytes=8 << 20),
        cost_estimate=pl.CostEstimate(flops=3000000000, bytes_accessed=1000000, transcendentals=0),
        name="field_edges",
    )(h)


def field_plane(
    z, e_ref, h_ref, j_ref, kind_ref, wide_ref, dft_e_ref, dft_h_ref, row_ref, col_ref,
    e_out, j_out, dft_e_out, dft_h_out, flux_out,
):
    rows, cols = kind_ref.shape[1:]
    hx, hy, hz = h_ref[0, z], h_ref[1, z], h_ref[2, z]
    first_row = iota((rows, cols), 0) == 0
    first_col = iota((rows, cols), 1) == 0
    diagonal = iota((rows, rows), 0) == iota((rows, rows), 1)

    def below_x(field, part):
        halo = row_ref[part, z : z + 1, :]
        return jnp.where(first_row, halo, pltpu.roll(field, 1, 0))

    def below_y(field, part):
        halo = col_ref[part, z : z + 1, :]
        halo = jnp.sum(jnp.where(diagonal, halo, 0.0), axis=1, keepdims=True)
        return jnp.where(first_col, halo, pltpu.roll(field, 1, 1))

    zero = jnp.zeros((rows, cols), f32)
    below_z = (h_ref[0, z - 1], h_ref[1, z - 1]) if z else (zero, zero)
    curl = (
        (hz - below_y(hz, 1)) - (hy - below_z[1]),
        (hx - below_z[0]) - (hz - below_x(hz, 1)),
        (hy - below_x(hy, 0)) - (hx - below_y(hx, 0)),
    )
    kinds = kind_ref[z]
    coeffs = [
        jnp.take_along_axis(
            jnp.broadcast_to(wide_ref[r : r + 1, :], (rows, cols)), kinds, axis=1
        )
        for r in range(4)
    ]
    e_next = []
    for c in range(3):
        old_e, old_j = e_ref[c, z], j_ref[c, z]
        new_e = coeffs[0] * old_e + coeffs[1] * (curl[c] - old_j)
        e_out[c, z] = new_e
        j_out[c, z] = coeffs[2] * old_j + coeffs[3] * (new_e - old_e)
        e_next.append(new_e)
    field_h = (hx, hy, hz)
    phase_e, phase_h = phase_list(0.0), phase_list(0.5)
    for f in range(3):
        spec_e, spec_h = [], []
        for part in range(2):
            factor_e = math.cos(phase_e[f]) if part == 0 else -math.sin(phase_e[f])
            factor_h = math.cos(phase_h[f]) if part == 0 else -math.sin(phase_h[f])
            now_e = [dft_e_ref[f, part, c, z] + e_next[c] * factor_e for c in range(3)]
            now_h = [dft_h_ref[f, part, c, z] + field_h[c] * factor_h for c in range(3)]
            for c in range(3):
                dft_e_out[f, part, c, z] = now_e[c]
                dft_h_out[f, part, c, z] = now_h[c]
            spec_e.append(now_e)
            spec_h.append(now_h)
        for c in range(3):
            a, b = (c + 1) % 3, (c + 2) % 3
            flux_out[3 * f + c, z] = 0.5 * (
                (spec_e[0][a] * spec_h[0][b] - spec_e[0][b] * spec_h[0][a])
                + (spec_e[1][a] * spec_h[1][b] - spec_e[1][b] * spec_h[1][a])
            )


def lookup_flux(offset_ref, packed, flux_ref, out_ref, found, head_ref, rest_ref):
    planes = [flux_ref[:, z].reshape(576, 128) for z in range(4)]
    back = split_scaled(jnp.concatenate(planes, 1), head_ref, rest_ref)

    def lookup(c):
        cell = jnp.concatenate([packed[pl.ds(2 * c, 1), :], packed[pl.ds(2 * c + 1, 1), :]], 1)
        plane = lax.bitwise_and(lax.shift_right_logical(cell, 13), 3)
        row = lax.bitwise_and(lax.shift_right_logical(cell, 7), 63)
        inner = lax.bitwise_or(lax.shift_left(plane, 7), lax.bitwise_and(cell, 127))
        hot = jnp.concatenate(
            [onehot(256, inner), onehot(256, jnp.where(inner >= 256, inner - 256, 512))], 0
        )
        result = jnp.dot(head_ref[...], hot, preferred_element_type=f32)
        result = result + jnp.dot(rest_ref[...], hot.astype(f8), preferred_element_type=f32)
        result = result.reshape(9, 64, 256)
        mine = iota((64, 256), 0) == row
        for q in range(9):
            value = jnp.sum(jnp.where(mine, result[q], 0.0), axis=0, keepdims=True) * back
            found[2 * c, q : q + 1, :] = value[:, :128]
            found[2 * c + 1, q : q + 1, :] = value[:, 128:]

    def chunk(c, _):
        for part in range(4):
            lookup(4 * c + part)
        return 0

    lax.fori_loop(0, lax.shift_right_logical(offset_ref[0, 128] + 1023, 10), chunk, 0)
    lanes = iota((16, 128), 1)

    def unpack(d, _):
        offset = offset_ref[0, d]
        row, start = lax.shift_right_logical(offset, 7), lax.bitwise_and(offset, 127)
        live = offset_ref[0, d + 1] - offset
        back = lax.bitwise_and(128 - start, 127)
        value = jnp.where(
            lanes < 128 - start, pltpu.roll(found[row], back, 1), pltpu.roll(found[row + 1], back, 1)
        )
        value = jnp.where(lanes < live, value, 0.0)
        for q in range(9):
            out_ref[d, q] = value[q : q + 1, :]
        return 0

    lax.fori_loop(0, 128, unpack, 0, unroll=32)


def field_kernel(
    offset_ref, packed, e_ref, h_ref, j_ref, kind_ref, table_ref, dft_e_ref, dft_h_ref, row_ref,
    col_ref, e_hbm, j_hbm, dft_e_hbm, dft_h_hbm, out_ref, e_new, j_new, dft_e_new, dft_h_new,
    flux_ref, wide_ref, found, head_ref, rest_ref, sems,
):
    wide_ref[...] = jnp.zeros_like(wide_ref)
    wide_ref[0:4, 0:32] = table_ref[...]
    planes = kind_ref.shape[0]
    copies = []
    for z in range(planes):
        field_plane(
            z, e_ref, h_ref, j_ref, kind_ref, wide_ref, dft_e_ref, dft_h_ref, row_ref, col_ref,
            e_new, j_new, dft_e_new, dft_h_new, flux_ref,
        )
    for i, (new, hbm) in enumerate(
        ((dft_e_new, dft_e_hbm), (dft_h_new, dft_h_hbm), (e_new, e_hbm), (j_new, j_hbm))
    ):
        copy = pltpu.make_async_copy(new, hbm, sems.at[i])
        copy.start()
        copies.append(copy)
    lookup_flux(offset_ref, packed, flux_ref, out_ref, found, head_ref, rest_ref)
    for copy in copies:
        copy.wait()


def field_and_flux(offsets, packed, e, h, j, kinds, table, dft_e, dft_h, rows_below, cols_left):
    planes, rows, cols = kinds.shape
    fields = [e.shape, e.shape, dft_e.shape, dft_h.shape]
    return pl.pallas_call(
        field_kernel,
        out_shape=tuple(jax.ShapeDtypeStruct(shape, f32) for shape in fields)
        + (jax.ShapeDtypeStruct((128, 9, 1, 128), f32),),
        in_specs=[SMEM] + [VMEM] * 10,
        out_specs=(pl.BlockSpec(memory_space=pl.ANY),) * 4 + (VMEM,),
        scratch_shapes=[pltpu.VMEM(shape, f32) for shape in fields]
        + [
            pltpu.VMEM((9, planes, rows, cols), f32),
            pltpu.VMEM((8, cols), f32),
            pltpu.VMEM((136, 16, 128), f32),
            pltpu.VMEM((576, 512), bf16),
            pltpu.VMEM((576, 512), f8),
            pltpu.SemaphoreType.DMA((4,)),
        ],
        compiler_params=pltpu.CompilerParams(vmem_limit_bytes=30 << 20),
        name="field_and_flux",
    )(offsets, packed, e, h, j, kinds, table, dft_e, dft_h, rows_below, cols_left)


GROUP = 8


def slot_row(ref, c):
    return jnp.concatenate([ref[0, pl.ds(GROUP * c + i, 1), :] for i in range(GROUP)], 1)


AREA_SCRATCH = [pltpu.VMEM((384, 512), bf16), pltpu.VMEM((384, 512), f8)]


def split_area(area_ref, head_ref, rest_ref):
    halves = [area_ref[:, :128, :].reshape(384, 256), area_ref[:, 128:, :].reshape(384, 256)]
    return split_scaled(jnp.concatenate(halves, 1), head_ref, rest_ref)


def area_group(patch_ref, head_ref, rest_ref, back, out_ref, c, first):
    patch = slot_row(patch_ref, c + first)
    u, v = lax.shift_right_logical(patch, 8), lax.bitwise_and(patch, 255)
    hot = jnp.concatenate(
        [onehot(256, jnp.where(u < 128, v, 512)), onehot(256, jnp.where(u < 128, 512, v))], 0
    )
    result = jnp.dot(head_ref[...], hot, preferred_element_type=f32)
    result = result + jnp.dot(rest_ref[...], hot.astype(f8), preferred_element_type=f32)
    result = result.reshape(3, 128, GROUP * 128)
    mine = iota((128, GROUP * 128), 0) == lax.bitwise_and(u, 127)
    for q in range(3):
        found = jnp.sum(jnp.where(mine, result[q], 0.0), axis=0, keepdims=True)
        out_ref[c, q : q + 1, :] = found * back


def first_area_kernel(
    count_ref, cell_ref, patch_ref, area_ref, out_ref, packed, offset_ref, head_ref, rest_ref,
    *, groups
):
    back = split_area(area_ref, head_ref, rest_ref)
    lane = iota((1, 128), 1)
    share = 128 // groups

    def chunk(c, carry):
        offset, current = carry
        for i in range(share):
            d = c * share + i
            row, start = lax.shift_right_logical(offset, 7), lax.bitwise_and(offset, 127)
            live = count_ref[0, d]
            offset_ref[0, d] = offset
            rolled = pltpu.roll(cell_ref[0, pl.ds(d, 1), :], start, 1)
            merged = jnp.where(lane >= start, rolled, current)
            packed[pl.ds(row, 1), :] = merged
            current = jnp.where(start + live >= 128, rolled, merged)
            offset = offset + live
        area_group(patch_ref, head_ref, rest_ref, back, out_ref, c, 0)
        return offset, current

    offset, current = lax.fori_loop(
        0, groups, chunk, (jnp.int32(0), jnp.zeros((1, 128), jnp.int32)), unroll=2
    )
    packed[pl.ds(lax.shift_right_logical(offset, 7), 1), :] = current
    offset_ref[0, 128] = offset


def area_kernel(patch_ref, area_ref, out_ref, head_ref, rest_ref, *, first):
    back = split_area(area_ref, head_ref, rest_ref)

    def chunk(c, _):
        area_group(patch_ref, head_ref, rest_ref, back, out_ref, c, first)
        return 0

    lax.fori_loop(0, out_ref.shape[0], chunk, 0, unroll=5)


def area_cost(groups):
    return pl.CostEstimate(
        flops=2 * 768 * 512 * GROUP * 128 * groups, bytes_accessed=2000000, transcendentals=0
    )


def gather_area_and_pack(counts, cells, patch, area, groups):
    return pl.pallas_call(
        functools.partial(first_area_kernel, groups=groups),
        out_shape=(
            jax.ShapeDtypeStruct((groups, 8, GROUP * 128), f32),
            jax.ShapeDtypeStruct((136, 128), jnp.int32),
            jax.ShapeDtypeStruct((1, 136), jnp.int32),
        ),
        in_specs=[SMEM, VMEM, VMEM, VMEM],
        out_specs=(VMEM, VMEM, SMEM),
        scratch_shapes=AREA_SCRATCH,
        compiler_params=pltpu.CompilerParams(vmem_limit_bytes=32 << 20),
        cost_estimate=area_cost(groups),
        name="area_and_pack",
    )(counts, cells, patch, area)


def gather_area(patch, area, first, groups):
    return pl.pallas_call(
        functools.partial(area_kernel, first=first),
        out_shape=jax.ShapeDtypeStruct((groups, 8, GROUP * 128), f32),
        in_specs=[VMEM, VMEM],
        out_specs=VMEM,
        scratch_shapes=AREA_SCRATCH,
        compiler_params=pltpu.CompilerParams(vmem_limit_bytes=32 << 20),
        cost_estimate=area_cost(groups),
        name="gather_area",
    )(patch, area)


EDGE = 104
PIECES = ((0, 2), (2, 1))


def scatter_kernel(
    odd_ref, patch_ref, area_a_ref, area_b_ref, flux_ref, out_ref, first_ref, second_ref, dense,
    *, first
):
    freqs = out_ref.shape[0]
    half, groups = area_a_ref.shape[0], dense.shape[0]
    out_ref[...] = jnp.zeros_like(out_ref)
    top = jnp.zeros((1, GROUP * 128), f32)
    for c in range(groups):
        area = area_a_ref[c] if c < half else area_b_ref[c - half]
        for f in range(freqs):
            density = jnp.zeros((1, GROUP * 128), f32)
            for q in range(3):
                flux = jnp.concatenate(
                    [flux_ref[GROUP * c + i, 3 * (first + f) + q] for i in range(GROUP)], 1
                )
                density = density + area[q : q + 1, :] * flux
            dense[c, f : f + 1, :] = density
            top = jnp.maximum(top, jnp.abs(density))
    top = largest(top)
    scale = TOP / top

    def add_group(c, _):
        patch = slot_row(patch_ref, c)
        u, v = lax.shift_right_logical(patch, 8), lax.bitwise_and(patch, 255)
        hot = onehot(256, v)
        mine = iota((256, GROUP * 128), 0).astype(bf16) == u.astype(bf16)
        heads, rests = [], []
        for f in range(freqs):
            density = dense[c, f : f + 1, :] * scale
            head = density.astype(bf16)
            rest = (density - head.astype(f32)).astype(bf16)
            heads.append(jnp.where(mine, head, jnp.zeros((), bf16)))
            rests.append(jnp.where(mine, rest, jnp.zeros((), bf16)).astype(f8))
        dims = (((1,), (1,)), ((), ()))
        total = lax.dot_general(jnp.concatenate(heads, 0), hot, dims, preferred_element_type=f32)
        total = total + lax.dot_general(
            jnp.concatenate(rests, 0), hot.astype(f8), dims, preferred_element_type=f32
        )
        out_ref[...] += total.reshape(freqs, 256, 256)
        return 0

    lax.fori_loop(0, groups, add_group, 0, unroll=8)
    out_ref[...] = out_ref[...] * (top * (1.0 / TOP)).reshape(1, 1, 1)
    for f in range(freqs):
        head = jnp.transpose(out_ref[f, :, :128])[:EDGE]
        tail = jnp.transpose(out_ref[f, :, 128:])[128 - EDGE :]
        put_edges(is_odd(odd_ref, 0), head, tail, first_ref, second_ref, f)


def block_and_edges(freqs):
    return (
        jax.ShapeDtypeStruct((freqs, 256, 256), f32),
        jax.ShapeDtypeStruct((freqs, EDGE, 256), f32),
        jax.ShapeDtypeStruct((freqs, EDGE, 256), f32),
    )


def scatter_density(odd, patch, area_a, area_b, flux, first, freqs):
    return pl.pallas_call(
        functools.partial(scatter_kernel, first=first),
        out_shape=block_and_edges(freqs),
        in_specs=[VMEM] * 5,
        out_specs=(VMEM,) * 3,
        scratch_shapes=[pltpu.VMEM((128 // GROUP, 8, GROUP * 128), f32)],
        compiler_params=pltpu.CompilerParams(vmem_limit_bytes=36 << 20),
        cost_estimate=pl.CostEstimate(
            flops=2 * freqs * 65536 * 2 * 16384, bytes_accessed=2000000, transcendentals=0
        ),
        name="scatter_density",
    )(odd, patch, area_a, area_b, flux)


def in_window(place):
    return jnp.where((place >= -HALF) & (place < HALF), 1.0, 0.0).astype(bf16)


def two_parts(cells):
    head = cells.astype(bf16)
    return head, (cells - head.astype(f32)).astype(bf16)


def column_kernel(odd_ref, block_ref, one_ref, two_ref, out_ref, first_ref, second_ref):
    inner = in_window(iota((256, 256), 0) - iota((256, 256), 1))
    place, column = iota((EDGE, 256), 0), iota((EDGE, 256), 1)
    outer = jnp.concatenate(
        [in_window(place - EDGE - column), in_window(place + 256 - column)], 0
    )
    inner = jnp.concatenate([inner, inner], 0)
    outer = jnp.concatenate([outer, outer], 0)
    for f in range(block_ref.shape[0]):
        total = jnp.dot(
            jnp.concatenate(two_parts(block_ref[f]), 1), inner, preferred_element_type=f32
        )
        edges = jnp.concatenate(got_edges(is_odd(odd_ref, 0), one_ref, two_ref, f), 0)
        total = total + lax.dot_general(
            jnp.concatenate(two_parts(edges), 0),
            outer,
            (((0,), (0,)), ((), ())),
            preferred_element_type=f32,
        )
        out_ref[f] = total
        put_edges(is_odd(odd_ref, 1), total[:EDGE], total[256 - EDGE :], first_ref, second_ref, f)


def column_sum(odd, block, first, second):
    return pl.pallas_call(
        column_kernel,
        out_shape=block_and_edges(block.shape[0]),
        in_specs=[VMEM] * 4,
        out_specs=(VMEM,) * 3,
        compiler_params=pltpu.CompilerParams(vmem_limit_bytes=16 << 20),
        name="column_sum",
    )(odd, block, first, second)


def row_kernel(odd_ref, *refs):
    refs, out_ref = refs[:-1], refs[-1]
    length = 256 + 2 * EDGE
    band = in_window(iota((256, length), 1) - EDGE - iota((256, length), 0))
    band = jnp.concatenate([band, band], 1)
    done = 0
    for block_ref, one_ref, two_ref in zip(refs[0::3], refs[1::3], refs[2::3]):
        for f in range(block_ref.shape[0]):
            before, after = got_edges(is_odd(odd_ref, 1), one_ref, two_ref, f)
            cells = jnp.concatenate([before, block_ref[f], after], 0)
            total = jnp.dot(
                band, jnp.concatenate(two_parts(cells), 0), preferred_element_type=f32
            )
            out_ref[done] = total * (1.0 / (4.0 * HALF * HALF))
            done += 1


def row_sum(odd, *pieces):
    return pl.pallas_call(
        row_kernel,
        out_shape=jax.ShapeDtypeStruct((3, 256, 256), f32),
        in_specs=[VMEM] * (1 + len(pieces)),
        out_specs=VMEM,
        compiler_params=pltpu.CompilerParams(vmem_limit_bytes=16 << 20),
        name="row_sum",
    )(odd, *pieces)


def shards(
    e_field, h_field, j_field, material, material_table, dft_e, dft_h, skin_cell, counts,
    patch_slot, area,
):
    last_rows, last_cols = field_edges(h_field)
    rows_below = shifted(last_rows, "gy", 1)
    cols_left = shifted(last_cols, "gx", 1)
    odd = jnp.stack([lax.axis_index("gx") % 2, lax.axis_index("gy") % 2])
    odd = jnp.broadcast_to(odd[:, None], (2, 128))
    area_a, packed, offsets = gather_area_and_pack(counts, skin_cell, patch_slot, area, 1)
    rows_below, cols_left, area_a = lax.optimization_barrier((rows_below, cols_left, area_a))
    e_next, j_next, dft_e_next, dft_h_next, rows = field_and_flux(
        offsets, packed, e_field, h_field, j_field, material, material_table, dft_e, dft_h,
        rows_below, cols_left,
    )
    arrived = lax.all_to_all(rows, ("gy", "gx"), split_axis=0, concat_axis=0, tiled=True)
    area_b = gather_area(patch_slot, area, 1, 15)

    blocks, swaps, pieces = [], [], []
    for first, freqs in PIECES:
        block, *edges = scatter_density(odd, patch_slot, area_a, area_b, arrived, first, freqs)
        blocks.append(block)
        swaps.append(exchange(*edges, "gx"))
    for block, swap in zip(blocks, swaps):
        strip, *edges = column_sum(odd, block, *swap)
        pieces += [strip, *exchange(*edges, "gy")]
    point_density = jnp.concatenate(blocks, 0)
    avg_density = row_sum(odd, *pieces)
    return (e_next, j_next, dft_e_next, dft_h_next, point_density, avg_density)


def solution(mesh):
    placed = (
        P(None, None, "gy", "gx"),
        P(None, None, "gy", "gx"),
        P(None, None, "gy", "gx"),
        P(None, "gy", "gx"),
        P(),
        P(None, None, None, None, "gy", "gx"),
        P(None, None, None, None, "gy", "gx"),
        P(("gy", "gx"), None, None),
        P(("gy", "gx"), None),
        P(("gy", "gx"), None, None),
        P(None, "gy", "gx"),
    )
    return jax.shard_map(
        shards,
        mesh=mesh,
        in_specs=placed,
        out_specs=(
            P(None, None, "gy", "gx"),
            P(None, None, "gy", "gx"),
            P(None, None, None, None, "gy", "gx"),
            P(None, None, None, None, "gy", "gx"),
            P(None, "gy", "gx"),
            P(None, "gy", "gx"),
        ),
        check_vma=False,
    )
```

```python
import functools
import math

import jax
import jax.numpy as jnp
from jax import lax
from jax.experimental import pallas as pl
from jax.experimental.pallas import tpu as pltpu
from jax.sharding import PartitionSpec as P

STEP = 1000
HALF = 100
FREQ_LIST = (28000000000.0, 39000000000.0, 60000000000.0)
TIME_STEP = 1.9e-13

f32 = jnp.float32
bf16 = jnp.bfloat16
f8 = jnp.float8_e4m3fn
TOP = 100000.0
VMEM = pl.BlockSpec(memory_space=pltpu.VMEM)
SMEM = pl.BlockSpec(memory_space=pltpu.SMEM)


def phase_list(offset):
    return [2.0 * math.pi * freq_hz * (STEP + offset) * TIME_STEP for freq_hz in FREQ_LIST]


def iota(shape, dim):
    return lax.broadcasted_iota(jnp.int32, shape, dim)


def shifted(value, axis, steps):
    count = lax.axis_size(axis)
    leading, last = (max(0, -steps), min(count, count - steps))
    return lax.ppermute(value, axis, [(source, source + steps) for source in range(leading, last)])


def exchange(first, second, axis):
    count = lax.axis_size(axis)
    swaps = []
    for start, value in ((1, first), (0, second)):
        lower = range(start, count - 1, 2)
        pairs = [(i, i + 1) for i in lower] + [(i + 1, i) for i in lower]
        swaps.append(lax.ppermute(value, axis, pairs))
    return swaps


def is_odd(odd_ref, axis):
    row = odd_ref[axis : axis + 1, :]
    return jnp.concatenate([row, row], 1) != 0


def put_edges(odd, head, tail, first_ref, second_ref, f):
    first_ref[f] = jnp.where(odd, tail, head)
    second_ref[f] = jnp.where(odd, head, tail)


def got_edges(odd, first_ref, second_ref, f):
    first, second = first_ref[f], second_ref[f]
    return jnp.where(odd, second, first), jnp.where(odd, first, second)


def onehot(count, index):
    places = iota((count, index.shape[1]), 0).astype(bf16)
    return jnp.where(places == index.astype(bf16), jnp.ones((), bf16), jnp.zeros((), bf16))


def largest(values):
    top = jnp.max(jnp.max(jnp.abs(values), axis=0, keepdims=True), axis=1, keepdims=True)
    return jnp.maximum(top, 1e-30)


def split_scaled(values, head_ref, rest_ref):
    top = largest(values)
    values = values * (TOP / top)
    head = values.astype(bf16)
    head_ref[...] = head
    rest_ref[...] = (values - head.astype(f32)).astype(f8)
    return top * (1.0 / TOP)


def edge_kernel(h_ref, col_out, row_out):
    planes, rows, cols = h_ref.shape[1:]
    diagonal = iota((rows, rows), 0) == iota((rows, rows), 1)
    for z in range(planes):
        for part, c in enumerate((1, 2)):
            row_out[part, z : z + 1, :] = h_ref[c, z, rows - 1 : rows, :]
        for part, c in enumerate((0, 2)):
            last = jnp.broadcast_to(h_ref[c, z, :, cols - 1 : cols], (rows, rows))
            col_out[part, z : z + 1, :] = jnp.sum(
                jnp.where(diagonal, last, 0.0), axis=0, keepdims=True
            )


def field_edges(h):
    planes, rows, cols = h.shape[1:]
    return pl.pallas_call(
        edge_kernel,
        out_shape=(
            jax.ShapeDtypeStruct((2, planes, rows), f32),
            jax.ShapeDtypeStruct((2, planes, cols), f32),
        ),
        in_specs=[VMEM],
        out_specs=(VMEM, VMEM),
        compiler_params=pltpu.CompilerParams(vmem_limit_bytes=8 << 20),
        cost_estimate=pl.CostEstimate(flops=3000000000, bytes_accessed=1000000, transcendentals=0),
        name="field_edges",
    )(h)


def field_plane(
    z, e_ref, h_ref, j_ref, kind_ref, wide_ref, dft_e_ref, dft_h_ref, row_ref, col_ref,
    e_out, j_out, dft_e_out, dft_h_out, flux_out,
):
    rows, cols = kind_ref.shape[1:]
    hx, hy, hz = h_ref[0, z], h_ref[1, z], h_ref[2, z]
    first_row = iota((rows, cols), 0) == 0
    first_col = iota((rows, cols), 1) == 0
    diagonal = iota((rows, rows), 0) == iota((rows, rows), 1)

    def below_x(field, part):
        halo = row_ref[part, z : z + 1, :]
        return jnp.where(first_row, halo, pltpu.roll(field, 1, 0))

    def below_y(field, part):
        halo = col_ref[part, z : z + 1, :]
        halo = jnp.sum(jnp.where(diagonal, halo, 0.0), axis=1, keepdims=True)
        return jnp.where(first_col, halo, pltpu.roll(field, 1, 1))

    zero = jnp.zeros((rows, cols), f32)
    below_z = (h_ref[0, z - 1], h_ref[1, z - 1]) if z else (zero, zero)
    curl = (
        (hz - below_y(hz, 1)) - (hy - below_z[1]),
        (hx - below_z[0]) - (hz - below_x(hz, 1)),
        (hy - below_x(hy, 0)) - (hx - below_y(hx, 0)),
    )
    kinds = kind_ref[z]
    coeffs = [
        jnp.take_along_axis(
            jnp.broadcast_to(wide_ref[r : r + 1, :], (rows, cols)), kinds, axis=1
        )
        for r in range(4)
    ]
    e_next = []
    for c in range(3):
        old_e, old_j = e_ref[c, z], j_ref[c, z]
        new_e = coeffs[0] * old_e + coeffs[1] * (curl[c] - old_j)
        e_out[c, z] = new_e
        j_out[c, z] = coeffs[2] * old_j + coeffs[3] * (new_e - old_e)
        e_next.append(new_e)
    field_h = (hx, hy, hz)
    phase_e, phase_h = phase_list(0.0), phase_list(0.5)
    for f in range(3):
        spec_e, spec_h = [], []
        for part in range(2):
            factor_e = math.cos(phase_e[f]) if part == 0 else -math.sin(phase_e[f])
            factor_h = math.cos(phase_h[f]) if part == 0 else -math.sin(phase_h[f])
            now_e = [dft_e_ref[f, part, c, z] + e_next[c] * factor_e for c in range(3)]
            now_h = [dft_h_ref[f, part, c, z] + field_h[c] * factor_h for c in range(3)]
            for c in range(3):
                dft_e_out[f, part, c, z] = now_e[c]
                dft_h_out[f, part, c, z] = now_h[c]
            spec_e.append(now_e)
            spec_h.append(now_h)
        for c in range(3):
            a, b = (c + 1) % 3, (c + 2) % 3
            flux_out[3 * f + c, z] = 0.5 * (
                (spec_e[0][a] * spec_h[0][b] - spec_e[0][b] * spec_h[0][a])
                + (spec_e[1][a] * spec_h[1][b] - spec_e[1][b] * spec_h[1][a])
            )


def lookup_flux(offset_ref, packed, flux_ref, out_ref, found, head_ref, rest_ref):
    planes = [flux_ref[:, z].reshape(576, 128) for z in range(4)]
    back = split_scaled(jnp.concatenate(planes, 1), head_ref, rest_ref)

    def lookup(c):
        cell = jnp.concatenate([packed[pl.ds(2 * c, 1), :], packed[pl.ds(2 * c + 1, 1), :]], 1)
        plane = lax.bitwise_and(lax.shift_right_logical(cell, 13), 3)
        row = lax.bitwise_and(lax.shift_right_logical(cell, 7), 63)
        inner = lax.bitwise_or(lax.shift_left(plane, 7), lax.bitwise_and(cell, 127))
        hot = jnp.concatenate(
            [onehot(256, inner), onehot(256, jnp.where(inner >= 256, inner - 256, 512))], 0
        )
        result = jnp.dot(head_ref[...], hot, preferred_element_type=f32)
        result = result + jnp.dot(rest_ref[...], hot.astype(f8), preferred_element_type=f32)
        result = result.reshape(9, 64, 256)
        mine = iota((64, 256), 0) == row
        for q in range(9):
            value = jnp.sum(jnp.where(mine, result[q], 0.0), axis=0, keepdims=True) * back
            found[2 * c, q : q + 1, :] = value[:, :128]
            found[2 * c + 1, q : q + 1, :] = value[:, 128:]

    def chunk(c, _):
        for part in range(4):
            lookup(4 * c + part)
        return 0

    total = offset_ref[0, 128]
    whole = lax.shift_right_logical(total, 10)
    lax.fori_loop(0, whole, chunk, 0)

    def last(c, _):
        lookup(4 * whole + c)
        return 0

    lax.fori_loop(0, lax.shift_right_logical(lax.bitwise_and(total, 1023) + 255, 8), last, 0)
    lanes = iota((16, 128), 1)

    def unpack(d, _):
        offset = offset_ref[0, d]
        row, start = lax.shift_right_logical(offset, 7), lax.bitwise_and(offset, 127)
        live = offset_ref[0, d + 1] - offset
        back = lax.bitwise_and(128 - start, 127)
        value = jnp.where(
            lanes < 128 - start, pltpu.roll(found[row], back, 1), pltpu.roll(found[row + 1], back, 1)
        )
        value = jnp.where(lanes < live, value, 0.0)
        for q in range(9):
            out_ref[d, q] = value[q : q + 1, :]
        return 0

    lax.fori_loop(0, 128, unpack, 0, unroll=32)


def field_kernel(
    offset_ref, packed, e_ref, h_ref, j_ref, kind_ref, table_ref, dft_e_ref, dft_h_ref, col_ref,
    row_ref, e_hbm, j_hbm, dft_e_hbm, dft_h_hbm, out_ref, e_new, j_new, dft_e_new, dft_h_new,
    flux_ref, wide_ref, found, head_ref, rest_ref, sems,
):
    wide_ref[...] = jnp.zeros_like(wide_ref)
    wide_ref[0:4, 0:32] = table_ref[...]
    planes = kind_ref.shape[0]
    copies = []
    for z in range(planes):
        field_plane(
            z, e_ref, h_ref, j_ref, kind_ref, wide_ref, dft_e_ref, dft_h_ref, row_ref, col_ref,
            e_new, j_new, dft_e_new, dft_h_new, flux_ref,
        )
    for i, (new, hbm) in enumerate(
        ((dft_e_new, dft_e_hbm), (dft_h_new, dft_h_hbm), (e_new, e_hbm), (j_new, j_hbm))
    ):
        copy = pltpu.make_async_copy(new, hbm, sems.at[i])
        copy.start()
        copies.append(copy)
    lookup_flux(offset_ref, packed, flux_ref, out_ref, found, head_ref, rest_ref)
    for copy in copies:
        copy.wait()


def field_and_flux(offsets, packed, e, h, j, kinds, table, dft_e, dft_h, cols_left, rows_below):
    planes, rows, cols = kinds.shape
    fields = [e.shape, e.shape, dft_e.shape, dft_h.shape]
    return pl.pallas_call(
        field_kernel,
        out_shape=tuple(jax.ShapeDtypeStruct(shape, f32) for shape in fields)
        + (jax.ShapeDtypeStruct((128, 9, 1, 128), f32),),
        in_specs=[SMEM] + [VMEM] * 10,
        out_specs=(pl.BlockSpec(memory_space=pl.ANY),) * 4 + (VMEM,),
        scratch_shapes=[pltpu.VMEM(shape, f32) for shape in fields]
        + [
            pltpu.VMEM((9, planes, rows, cols), f32),
            pltpu.VMEM((8, cols), f32),
            pltpu.VMEM((136, 16, 128), f32),
            pltpu.VMEM((576, 512), bf16),
            pltpu.VMEM((576, 512), f8),
            pltpu.SemaphoreType.DMA((4,)),
        ],
        compiler_params=pltpu.CompilerParams(vmem_limit_bytes=30 << 20),
        name="field_and_flux",
    )(offsets, packed, e, h, j, kinds, table, dft_e, dft_h, cols_left, rows_below)


GROUP = 8


def slot_row(ref, c):
    return jnp.concatenate([ref[0, pl.ds(GROUP * c + i, 1), :] for i in range(GROUP)], 1)


AREA_SCRATCH = [pltpu.VMEM((384, 512), bf16), pltpu.VMEM((384, 512), f8)]


def split_area(area_ref, head_ref, rest_ref):
    halves = [area_ref[:, :128, :].reshape(384, 256), area_ref[:, 128:, :].reshape(384, 256)]
    return split_scaled(jnp.concatenate(halves, 1), head_ref, rest_ref)


def area_group(patch_ref, head_ref, rest_ref, back, out_ref, c, first):
    patch = slot_row(patch_ref, c + first)
    u, v = lax.shift_right_logical(patch, 8), lax.bitwise_and(patch, 255)
    hot = jnp.concatenate(
        [onehot(256, jnp.where(u < 128, v, 512)), onehot(256, jnp.where(u < 128, 512, v))], 0
    )
    result = jnp.dot(head_ref[...], hot, preferred_element_type=f32)
    result = result + jnp.dot(rest_ref[...], hot.astype(f8), preferred_element_type=f32)
    result = result.reshape(3, 128, GROUP * 128)
    mine = iota((128, GROUP * 128), 0) == lax.bitwise_and(u, 127)
    for q in range(3):
        found = jnp.sum(jnp.where(mine, result[q], 0.0), axis=0, keepdims=True)
        out_ref[c, q : q + 1, :] = found * back


def first_area_kernel(
    count_ref, cell_ref, patch_ref, area_ref, out_ref, packed, offset_ref, head_ref, rest_ref,
    *, groups
):
    back = split_area(area_ref, head_ref, rest_ref)
    lane = iota((1, 128), 1)
    share = 128 // groups

    def chunk(c, carry):
        offset, current = carry
        for i in range(share):
            d = c * share + i
            row, start = lax.shift_right_logical(offset, 7), lax.bitwise_and(offset, 127)
            live = count_ref[0, d]
            offset_ref[0, d] = offset
            rolled = pltpu.roll(cell_ref[0, pl.ds(d, 1), :], start, 1)
            merged = jnp.where(lane >= start, rolled, current)
            packed[pl.ds(row, 1), :] = merged
            current = jnp.where(start + live >= 128, rolled, merged)
            offset = offset + live
        area_group(patch_ref, head_ref, rest_ref, back, out_ref, c, 0)
        return offset, current

    offset, current = lax.fori_loop(
        0, groups, chunk, (jnp.int32(0), jnp.zeros((1, 128), jnp.int32)), unroll=2
    )
    packed[pl.ds(lax.shift_right_logical(offset, 7), 1), :] = current
    offset_ref[0, 128] = offset


def area_kernel(patch_ref, area_ref, out_ref, head_ref, rest_ref, *, first):
    back = split_area(area_ref, head_ref, rest_ref)

    def chunk(c, _):
        area_group(patch_ref, head_ref, rest_ref, back, out_ref, c, first)
        return 0

    lax.fori_loop(0, out_ref.shape[0], chunk, 0, unroll=5)


def area_cost(groups):
    return pl.CostEstimate(
        flops=2 * 768 * 512 * GROUP * 128 * groups, bytes_accessed=2000000, transcendentals=0
    )


def gather_area_and_pack(counts, cells, patch, area, groups):
    return pl.pallas_call(
        functools.partial(first_area_kernel, groups=groups),
        out_shape=(
            jax.ShapeDtypeStruct((groups, 8, GROUP * 128), f32),
            jax.ShapeDtypeStruct((136, 128), jnp.int32),
            jax.ShapeDtypeStruct((1, 136), jnp.int32),
        ),
        in_specs=[SMEM, VMEM, VMEM, VMEM],
        out_specs=(VMEM, VMEM, SMEM),
        scratch_shapes=AREA_SCRATCH,
        compiler_params=pltpu.CompilerParams(vmem_limit_bytes=32 << 20),
        cost_estimate=area_cost(groups),
        name="area_and_pack",
    )(counts, cells, patch, area)


def gather_area(patch, area, first, groups):
    return pl.pallas_call(
        functools.partial(area_kernel, first=first),
        out_shape=jax.ShapeDtypeStruct((groups, 8, GROUP * 128), f32),
        in_specs=[VMEM, VMEM],
        out_specs=VMEM,
        scratch_shapes=AREA_SCRATCH,
        compiler_params=pltpu.CompilerParams(vmem_limit_bytes=32 << 20),
        cost_estimate=area_cost(groups),
        name="gather_area",
    )(patch, area)


EDGE = 104
PIECES = ((0, 2), (2, 1))


def scatter_kernel(
    odd_ref, patch_ref, area_a_ref, area_b_ref, flux_ref, out_ref, first_ref, second_ref, dense,
    *, first
):
    freqs = out_ref.shape[0]
    half, groups = area_a_ref.shape[0], dense.shape[0]
    out_ref[...] = jnp.zeros_like(out_ref)
    top = jnp.zeros((1, GROUP * 128), f32)
    for c in range(groups):
        area = area_a_ref[c] if c < half else area_b_ref[c - half]
        for f in range(freqs):
            density = jnp.zeros((1, GROUP * 128), f32)
            for q in range(3):
                flux = jnp.concatenate(
                    [flux_ref[GROUP * c + i, 3 * (first + f) + q] for i in range(GROUP)], 1
                )
                density = density + area[q : q + 1, :] * flux
            dense[c, f : f + 1, :] = density
            top = jnp.maximum(top, jnp.abs(density))
    top = largest(top)
    scale = TOP / top

    def add_group(c, _):
        patch = slot_row(patch_ref, c)
        u, v = lax.shift_right_logical(patch, 8), lax.bitwise_and(patch, 255)
        hot = onehot(256, v)
        mine = iota((256, GROUP * 128), 0).astype(bf16) == u.astype(bf16)
        heads, rests = [], []
        for f in range(freqs):
            density = dense[c, f : f + 1, :] * scale
            head = density.astype(bf16)
            rest = (density - head.astype(f32)).astype(bf16)
            heads.append(jnp.where(mine, head, jnp.zeros((), bf16)))
            rests.append(jnp.where(mine, rest, jnp.zeros((), bf16)).astype(f8))
        dims = (((1,), (1,)), ((), ()))
        total = lax.dot_general(jnp.concatenate(heads, 0), hot, dims, preferred_element_type=f32)
        total = total + lax.dot_general(
            jnp.concatenate(rests, 0), hot.astype(f8), dims, preferred_element_type=f32
        )
        out_ref[...] += total.reshape(freqs, 256, 256)
        return 0

    lax.fori_loop(0, groups, add_group, 0, unroll=8)
    out_ref[...] = out_ref[...] * (top * (1.0 / TOP)).reshape(1, 1, 1)
    for f in range(freqs):
        head = jnp.transpose(out_ref[f, :, :128])[:EDGE]
        tail = jnp.transpose(out_ref[f, :, 128:])[128 - EDGE :]
        put_edges(is_odd(odd_ref, 0), head, tail, first_ref, second_ref, f)


def block_and_edges(freqs):
    return (
        jax.ShapeDtypeStruct((freqs, 256, 256), f32),
        jax.ShapeDtypeStruct((freqs, EDGE, 256), f32),
        jax.ShapeDtypeStruct((freqs, EDGE, 256), f32),
    )


def scatter_density(odd, patch, area_a, area_b, flux, first, freqs):
    return pl.pallas_call(
        functools.partial(scatter_kernel, first=first),
        out_shape=block_and_edges(freqs),
        in_specs=[VMEM] * 5,
        out_specs=(VMEM,) * 3,
        scratch_shapes=[pltpu.VMEM((128 // GROUP, 8, GROUP * 128), f32)],
        compiler_params=pltpu.CompilerParams(vmem_limit_bytes=36 << 20),
        cost_estimate=pl.CostEstimate(
            flops=2 * freqs * 65536 * 2 * 16384, bytes_accessed=2000000, transcendentals=0
        ),
        name="scatter_density",
    )(odd, patch, area_a, area_b, flux)


def in_window(place):
    return jnp.where((place >= -HALF) & (place < HALF), 1.0, 0.0).astype(bf16)


def two_parts(cells):
    head = cells.astype(bf16)
    return head, (cells - head.astype(f32)).astype(bf16)


def column_kernel(odd_ref, block_ref, one_ref, two_ref, out_ref, first_ref, second_ref):
    inner = in_window(iota((256, 256), 0) - iota((256, 256), 1))
    place, column = iota((EDGE, 256), 0), iota((EDGE, 256), 1)
    outer = jnp.concatenate(
        [in_window(place - EDGE - column), in_window(place + 256 - column)], 0
    )
    inner = jnp.concatenate([inner, inner], 0)
    outer = jnp.concatenate([outer, outer], 0)
    for f in range(block_ref.shape[0]):
        total = jnp.dot(
            jnp.concatenate(two_parts(block_ref[f]), 1), inner, preferred_element_type=f32
        )
        edges = jnp.concatenate(got_edges(is_odd(odd_ref, 0), one_ref, two_ref, f), 0)
        total = total + lax.dot_general(
            jnp.concatenate(two_parts(edges), 0),
            outer,
            (((0,), (0,)), ((), ())),
            preferred_element_type=f32,
        )
        out_ref[f] = total
        put_edges(is_odd(odd_ref, 1), total[:EDGE], total[256 - EDGE :], first_ref, second_ref, f)


def column_sum(odd, block, first, second):
    return pl.pallas_call(
        column_kernel,
        out_shape=block_and_edges(block.shape[0]),
        in_specs=[VMEM] * 4,
        out_specs=(VMEM,) * 3,
        compiler_params=pltpu.CompilerParams(vmem_limit_bytes=16 << 20),
        name="column_sum",
    )(odd, block, first, second)


def row_kernel(odd_ref, *refs):
    refs, out_ref = refs[:-1], refs[-1]
    length = 256 + 2 * EDGE
    band = in_window(iota((256, length), 1) - EDGE - iota((256, length), 0))
    band = jnp.concatenate([band, band], 1)
    done = 0
    for block_ref, one_ref, two_ref in zip(refs[0::3], refs[1::3], refs[2::3]):
        for f in range(block_ref.shape[0]):
            before, after = got_edges(is_odd(odd_ref, 1), one_ref, two_ref, f)
            cells = jnp.concatenate([before, block_ref[f], after], 0)
            total = jnp.dot(
                band, jnp.concatenate(two_parts(cells), 0), preferred_element_type=f32
            )
            out_ref[done] = total * (1.0 / (4.0 * HALF * HALF))
            done += 1


def row_sum(odd, *pieces):
    return pl.pallas_call(
        row_kernel,
        out_shape=jax.ShapeDtypeStruct((3, 256, 256), f32),
        in_specs=[VMEM] * (1 + len(pieces)),
        out_specs=VMEM,
        compiler_params=pltpu.CompilerParams(vmem_limit_bytes=16 << 20),
        name="row_sum",
    )(odd, *pieces)


def shards(
    e_field, h_field, j_field, material, material_table, dft_e, dft_h, skin_cell, counts,
    patch_slot, area,
):
    last_cols, last_rows = field_edges(h_field)
    cols_left = shifted(last_cols, "gx", 1)
    rows_below = shifted(last_rows, "gy", 1)
    odd = jnp.stack([lax.axis_index("gx") % 2, lax.axis_index("gy") % 2])
    odd = jnp.broadcast_to(odd[:, None], (2, 128))
    area_a, packed, offsets = gather_area_and_pack(counts, skin_cell, patch_slot, area, 1)
    cols_left, rows_below, area_a = lax.optimization_barrier((cols_left, rows_below, area_a))
    e_next, j_next, dft_e_next, dft_h_next, rows = field_and_flux(
        offsets, packed, e_field, h_field, j_field, material, material_table, dft_e, dft_h,
        cols_left, rows_below,
    )
    arrived = lax.all_to_all(rows, ("gy", "gx"), split_axis=0, concat_axis=0, tiled=True)
    area_b = gather_area(patch_slot, area, 1, 15)

    blocks, swaps, pieces = [], [], []
    for first, freqs in PIECES:
        block, *edges = scatter_density(odd, patch_slot, area_a, area_b, arrived, first, freqs)
        blocks.append(block)
        swaps.append(exchange(*edges, "gx"))
    for block, swap in zip(blocks, swaps):
        strip, *edges = column_sum(odd, block, *swap)
        pieces += [strip, *exchange(*edges, "gy")]
    point_density = jnp.concatenate(blocks, 0)
    avg_density = row_sum(odd, *pieces)
    return (e_next, j_next, dft_e_next, dft_h_next, point_density, avg_density)


def solution(mesh):
    placed = (
        P(None, None, "gy", "gx"),
        P(None, None, "gy", "gx"),
        P(None, None, "gy", "gx"),
        P(None, "gy", "gx"),
        P(),
        P(None, None, None, None, "gy", "gx"),
        P(None, None, None, None, "gy", "gx"),
        P(("gy", "gx"), None, None),
        P(("gy", "gx"), None),
        P(("gy", "gx"), None, None),
        P(None, "gy", "gx"),
    )
    return jax.shard_map(
        shards,
        mesh=mesh,
        in_specs=placed,
        out_specs=(
            P(None, None, "gy", "gx"),
            P(None, None, "gy", "gx"),
            P(None, None, None, None, "gy", "gx"),
            P(None, None, None, None, "gy", "gx"),
            P(None, "gy", "gx"),
            P(None, "gy", "gx"),
        ),
        check_vma=False,
    )
```

```python
import functools
import math

import jax
import jax.numpy as jnp
from jax import lax
from jax.experimental import pallas as pl
from jax.experimental.pallas import tpu as pltpu
from jax.sharding import PartitionSpec as P

STEP = 1000
HALF = 100
FREQ_LIST = (28000000000.0, 39000000000.0, 60000000000.0)
TIME_STEP = 1.9e-13

f32 = jnp.float32
bf16 = jnp.bfloat16
f8 = jnp.float8_e4m3fn
TOP = 100000.0
VMEM = pl.BlockSpec(memory_space=pltpu.VMEM)
SMEM = pl.BlockSpec(memory_space=pltpu.SMEM)


def phase_list(offset):
    return [2.0 * math.pi * freq_hz * (STEP + offset) * TIME_STEP for freq_hz in FREQ_LIST]


def iota(shape, dim):
    return lax.broadcasted_iota(jnp.int32, shape, dim)


def shifted(value, axis, steps):
    count = lax.axis_size(axis)
    leading, last = (max(0, -steps), min(count, count - steps))
    return lax.ppermute(value, axis, [(source, source + steps) for source in range(leading, last)])


def exchange(first, second, axis):
    count = lax.axis_size(axis)
    swaps = []
    for start, value in ((1, first), (0, second)):
        lower = range(start, count - 1, 2)
        pairs = [(i, i + 1) for i in lower] + [(i + 1, i) for i in lower]
        swaps.append(lax.ppermute(value, axis, pairs))
    return swaps


def is_odd(odd_ref, axis):
    row = odd_ref[axis : axis + 1, :]
    return jnp.concatenate([row, row], 1) != 0


def put_edges(odd, head, tail, first_ref, second_ref, f):
    first_ref[f] = jnp.where(odd, tail, head)
    second_ref[f] = jnp.where(odd, head, tail)


def got_edges(odd, first_ref, second_ref, f):
    first, second = first_ref[f], second_ref[f]
    return jnp.where(odd, second, first), jnp.where(odd, first, second)


def onehot(count, index):
    places = iota((count, index.shape[1]), 0).astype(bf16)
    return jnp.where(places == index.astype(bf16), jnp.ones((), bf16), jnp.zeros((), bf16))


def largest(values):
    top = jnp.max(jnp.max(jnp.abs(values), axis=0, keepdims=True), axis=1, keepdims=True)
    return jnp.maximum(top, 1e-30)


def split_scaled(values, head_ref, rest_ref):
    top = largest(values)
    values = values * (TOP / top)
    head = values.astype(bf16)
    head_ref[...] = head
    rest_ref[...] = (values - head.astype(f32)).astype(f8)
    return top * (1.0 / TOP)


def edge_kernel(h_ref, col_out, row_out):
    planes, rows, cols = h_ref.shape[1:]
    diagonal = iota((rows, rows), 0) == iota((rows, rows), 1)
    for z in range(planes):
        for part, c in enumerate((1, 2)):
            row_out[part, z : z + 1, :] = h_ref[c, z, rows - 1 : rows, :]
        for part, c in enumerate((0, 2)):
            last = jnp.broadcast_to(h_ref[c, z, :, cols - 1 : cols], (rows, rows))
            col_out[part, z : z + 1, :] = jnp.sum(
                jnp.where(diagonal, last, 0.0), axis=0, keepdims=True
            )


def field_edges(h):
    planes, rows, cols = h.shape[1:]
    return pl.pallas_call(
        edge_kernel,
        out_shape=(
            jax.ShapeDtypeStruct((2, planes, rows), f32),
            jax.ShapeDtypeStruct((2, planes, cols), f32),
        ),
        in_specs=[VMEM],
        out_specs=(VMEM, VMEM),
        compiler_params=pltpu.CompilerParams(vmem_limit_bytes=8 << 20),
        cost_estimate=pl.CostEstimate(flops=3000000000, bytes_accessed=1000000, transcendentals=0),
        name="field_edges",
    )(h)


def field_plane(
    z, e_ref, h_ref, j_ref, kind_ref, wide_ref, dft_e_ref, dft_h_ref, row_ref, col_ref,
    e_out, j_out, dft_e_out, dft_h_out, flux_out,
):
    rows, cols = kind_ref.shape[1:]
    hx, hy, hz = h_ref[0, z], h_ref[1, z], h_ref[2, z]
    first_row = iota((rows, cols), 0) == 0
    first_col = iota((rows, cols), 1) == 0
    diagonal = iota((rows, rows), 0) == iota((rows, rows), 1)

    def below_x(field, part):
        halo = row_ref[part, z : z + 1, :]
        return jnp.where(first_row, halo, pltpu.roll(field, 1, 0))

    def below_y(field, part):
        halo = col_ref[part, z : z + 1, :]
        halo = jnp.sum(jnp.where(diagonal, halo, 0.0), axis=1, keepdims=True)
        return jnp.where(first_col, halo, pltpu.roll(field, 1, 1))

    zero = jnp.zeros((rows, cols), f32)
    below_z = (h_ref[0, z - 1], h_ref[1, z - 1]) if z else (zero, zero)
    curl = (
        (hz - below_y(hz, 1)) - (hy - below_z[1]),
        (hx - below_z[0]) - (hz - below_x(hz, 1)),
        (hy - below_x(hy, 0)) - (hx - below_y(hx, 0)),
    )
    kinds = kind_ref[z]
    coeffs = [
        jnp.take_along_axis(
            jnp.broadcast_to(wide_ref[r : r + 1, :], (rows, cols)), kinds, axis=1
        )
        for r in range(4)
    ]
    e_next = []
    for c in range(3):
        old_e, old_j = e_ref[c, z], j_ref[c, z]
        new_e = coeffs[0] * old_e + coeffs[1] * (curl[c] - old_j)
        e_out[c, z] = new_e
        j_out[c, z] = coeffs[2] * old_j + coeffs[3] * (new_e - old_e)
        e_next.append(new_e)
    field_h = (hx, hy, hz)
    phase_e, phase_h = phase_list(0.0), phase_list(0.5)
    for f in range(3):
        spec_e, spec_h = [], []
        for part in range(2):
            factor_e = math.cos(phase_e[f]) if part == 0 else -math.sin(phase_e[f])
            factor_h = math.cos(phase_h[f]) if part == 0 else -math.sin(phase_h[f])
            now_e = [dft_e_ref[f, part, c, z] + e_next[c] * factor_e for c in range(3)]
            now_h = [dft_h_ref[f, part, c, z] + field_h[c] * factor_h for c in range(3)]
            for c in range(3):
                dft_e_out[f, part, c, z] = now_e[c]
                dft_h_out[f, part, c, z] = now_h[c]
            spec_e.append(now_e)
            spec_h.append(now_h)
        for c in range(3):
            a, b = (c + 1) % 3, (c + 2) % 3
            flux_out[3 * f + c, z] = 0.5 * (
                (spec_e[0][a] * spec_h[0][b] - spec_e[0][b] * spec_h[0][a])
                + (spec_e[1][a] * spec_h[1][b] - spec_e[1][b] * spec_h[1][a])
            )


def lookup_flux(offset_ref, packed, flux_ref, out_ref, found, head_ref, rest_ref):
    planes = [flux_ref[:, z].reshape(576, 128) for z in range(4)]
    back = split_scaled(jnp.concatenate(planes, 1), head_ref, rest_ref)

    def lookup(c):
        cell = jnp.concatenate([packed[pl.ds(2 * c, 1), :], packed[pl.ds(2 * c + 1, 1), :]], 1)
        plane = lax.bitwise_and(lax.shift_right_logical(cell, 13), 3)
        row = lax.bitwise_and(lax.shift_right_logical(cell, 7), 63)
        inner = lax.bitwise_or(lax.shift_left(plane, 7), lax.bitwise_and(cell, 127))
        hot = jnp.concatenate(
            [onehot(256, inner), onehot(256, jnp.where(inner >= 256, inner - 256, 512))], 0
        )
        result = jnp.dot(head_ref[...], hot, preferred_element_type=f32)
        result = result + jnp.dot(rest_ref[...], hot.astype(f8), preferred_element_type=f32)
        result = result.reshape(9, 64, 256)
        mine = iota((64, 256), 0) == row
        for q in range(9):
            value = jnp.sum(jnp.where(mine, result[q], 0.0), axis=0, keepdims=True) * back
            found[2 * c, q : q + 1, :] = value[:, :128]
            found[2 * c + 1, q : q + 1, :] = value[:, 128:]

    def chunk(c, _):
        for part in range(4):
            lookup(4 * c + part)
        return 0

    total = offset_ref[0, 128]
    whole = lax.shift_right_logical(total, 10)
    lax.fori_loop(0, whole, chunk, 0)

    def last(c, _):
        lookup(4 * whole + c)
        return 0

    lax.fori_loop(0, lax.shift_right_logical(lax.bitwise_and(total, 1023) + 255, 8), last, 0)
    lanes = iota((16, 128), 1)

    def unpack(d, _):
        offset = offset_ref[0, d]
        row, start = lax.shift_right_logical(offset, 7), lax.bitwise_and(offset, 127)
        live = offset_ref[0, d + 1] - offset
        back = lax.bitwise_and(128 - start, 127)
        value = jnp.where(
            lanes < 128 - start, pltpu.roll(found[row], back, 1), pltpu.roll(found[row + 1], back, 1)
        )
        value = jnp.where(lanes < live, value, 0.0)
        for q in range(9):
            out_ref[d, q] = value[q : q + 1, :]
        return 0

    lax.fori_loop(0, 128, unpack, 0, unroll=32)


def field_kernel(
    offset_ref, packed, e_ref, h_ref, j_ref, kind_ref, table_ref, dft_e_ref, dft_h_ref, col_ref,
    row_ref, e_hbm, j_hbm, dft_e_hbm, dft_h_hbm, out_ref, e_new, j_new, dft_e_new, dft_h_new,
    flux_ref, wide_ref, found, head_ref, rest_ref, sems,
):
    wide_ref[...] = jnp.zeros_like(wide_ref)
    wide_ref[0:4, 0:32] = table_ref[...]
    planes = kind_ref.shape[0]
    copies = []
    for z in range(planes):
        field_plane(
            z, e_ref, h_ref, j_ref, kind_ref, wide_ref, dft_e_ref, dft_h_ref, row_ref, col_ref,
            e_new, j_new, dft_e_new, dft_h_new, flux_ref,
        )
    for i, (new, hbm) in enumerate(
        ((dft_e_new, dft_e_hbm), (dft_h_new, dft_h_hbm), (e_new, e_hbm), (j_new, j_hbm))
    ):
        copy = pltpu.make_async_copy(new, hbm, sems.at[i])
        copy.start()
        copies.append(copy)
    lookup_flux(offset_ref, packed, flux_ref, out_ref, found, head_ref, rest_ref)
    for copy in copies:
        copy.wait()


def field_and_flux(offsets, packed, e, h, j, kinds, table, dft_e, dft_h, cols_left, rows_below):
    planes, rows, cols = kinds.shape
    fields = [e.shape, e.shape, dft_e.shape, dft_h.shape]
    return pl.pallas_call(
        field_kernel,
        out_shape=tuple(jax.ShapeDtypeStruct(shape, f32) for shape in fields)
        + (jax.ShapeDtypeStruct((128, 9, 1, 128), f32),),
        in_specs=[SMEM] + [VMEM] * 10,
        out_specs=(pl.BlockSpec(memory_space=pl.ANY),) * 4 + (VMEM,),
        scratch_shapes=[pltpu.VMEM(shape, f32) for shape in fields]
        + [
            pltpu.VMEM((9, planes, rows, cols), f32),
            pltpu.VMEM((8, cols), f32),
            pltpu.VMEM((136, 16, 128), f32),
            pltpu.VMEM((576, 512), bf16),
            pltpu.VMEM((576, 512), f8),
            pltpu.SemaphoreType.DMA((4,)),
        ],
        compiler_params=pltpu.CompilerParams(vmem_limit_bytes=30 << 20),
        name="field_and_flux",
    )(offsets, packed, e, h, j, kinds, table, dft_e, dft_h, cols_left, rows_below)


GROUP = 8


def slot_row(ref, c):
    return jnp.concatenate([ref[0, pl.ds(GROUP * c + i, 1), :] for i in range(GROUP)], 1)


AREA_SCRATCH = [pltpu.VMEM((384, 512), bf16), pltpu.VMEM((384, 512), f8)]


def split_area(area_ref, head_ref, rest_ref):
    halves = [area_ref[:, :128, :].reshape(384, 256), area_ref[:, 128:, :].reshape(384, 256)]
    return split_scaled(jnp.concatenate(halves, 1), head_ref, rest_ref)


def area_group(patch_ref, head_ref, rest_ref, back, out_ref, c):
    patch = slot_row(patch_ref, c)
    u, v = lax.shift_right_logical(patch, 8), lax.bitwise_and(patch, 255)
    hot = jnp.concatenate(
        [onehot(256, jnp.where(u < 128, v, 512)), onehot(256, jnp.where(u < 128, 512, v))], 0
    )
    result = jnp.dot(head_ref[...], hot, preferred_element_type=f32)
    result = result + jnp.dot(rest_ref[...], hot.astype(f8), preferred_element_type=f32)
    result = result.reshape(3, 128, GROUP * 128)
    mine = iota((128, GROUP * 128), 0) == lax.bitwise_and(u, 127)
    for q in range(3):
        found = jnp.sum(jnp.where(mine, result[q], 0.0), axis=0, keepdims=True)
        out_ref[c, q : q + 1, :] = found * back


def pack_kernel(count_ref, cell_ref, packed, offset_ref):
    lane = iota((1, 128), 1)

    def pack(d, carry):
        offset, current = carry
        row, start = lax.shift_right_logical(offset, 7), lax.bitwise_and(offset, 127)
        live = count_ref[0, d]
        offset_ref[0, d] = offset
        rolled = pltpu.roll(cell_ref[0, pl.ds(d, 1), :], start, 1)
        merged = jnp.where(lane >= start, rolled, current)
        packed[pl.ds(row, 1), :] = merged
        return offset + live, jnp.where(start + live >= 128, rolled, merged)

    offset, current = lax.fori_loop(
        0, 128, pack, (jnp.int32(0), jnp.zeros((1, 128), jnp.int32)), unroll=64
    )
    packed[pl.ds(lax.shift_right_logical(offset, 7), 1), :] = current
    offset_ref[0, 128] = offset


def area_kernel(patch_ref, area_ref, out_ref, head_ref, rest_ref):
    back = split_area(area_ref, head_ref, rest_ref)

    def chunk(c, _):
        area_group(patch_ref, head_ref, rest_ref, back, out_ref, c)
        return 0

    lax.fori_loop(0, out_ref.shape[0], chunk, 0, unroll=8)


def area_cost(groups):
    return pl.CostEstimate(
        flops=2 * 768 * 512 * GROUP * 128 * groups, bytes_accessed=2000000, transcendentals=0
    )


def pack_slots(counts, cells):
    return pl.pallas_call(
        pack_kernel,
        out_shape=(
            jax.ShapeDtypeStruct((136, 128), jnp.int32),
            jax.ShapeDtypeStruct((1, 136), jnp.int32),
        ),
        in_specs=[SMEM, VMEM],
        out_specs=(VMEM, SMEM),
        compiler_params=pltpu.CompilerParams(vmem_limit_bytes=8 << 20),
        cost_estimate=area_cost(3),
        name="pack_slots",
    )(counts, cells)


def gather_area(patch, area):
    groups = 128 // GROUP
    return pl.pallas_call(
        area_kernel,
        out_shape=jax.ShapeDtypeStruct((groups, 8, GROUP * 128), f32),
        in_specs=[VMEM, VMEM],
        out_specs=VMEM,
        scratch_shapes=AREA_SCRATCH,
        compiler_params=pltpu.CompilerParams(vmem_limit_bytes=32 << 20),
        cost_estimate=area_cost(groups),
        name="gather_area",
    )(patch, area)


EDGE = 104
PIECES = ((0, 2), (2, 1))


def scatter_kernel(
    odd_ref, patch_ref, area_ref, flux_ref, out_ref, first_ref, second_ref, dense,
    *, first
):
    freqs = out_ref.shape[0]
    groups = dense.shape[0]
    out_ref[...] = jnp.zeros_like(out_ref)
    top = jnp.zeros((1, GROUP * 128), f32)
    for c in range(groups):
        area = area_ref[c]
        for f in range(freqs):
            density = jnp.zeros((1, GROUP * 128), f32)
            for q in range(3):
                flux = jnp.concatenate(
                    [flux_ref[GROUP * c + i, 3 * (first + f) + q] for i in range(GROUP)], 1
                )
                density = density + area[q : q + 1, :] * flux
            dense[c, f : f + 1, :] = density
            top = jnp.maximum(top, jnp.abs(density))
    top = largest(top)
    scale = TOP / top

    def add_group(c, _):
        patch = slot_row(patch_ref, c)
        u, v = lax.shift_right_logical(patch, 8), lax.bitwise_and(patch, 255)
        hot = onehot(256, v)
        mine = iota((256, GROUP * 128), 0).astype(bf16) == u.astype(bf16)
        heads, rests = [], []
        for f in range(freqs):
            density = dense[c, f : f + 1, :] * scale
            head = density.astype(bf16)
            rest = (density - head.astype(f32)).astype(bf16)
            heads.append(jnp.where(mine, head, jnp.zeros((), bf16)))
            rests.append(jnp.where(mine, rest, jnp.zeros((), bf16)).astype(f8))
        dims = (((1,), (1,)), ((), ()))
        total = lax.dot_general(jnp.concatenate(heads, 0), hot, dims, preferred_element_type=f32)
        total = total + lax.dot_general(
            jnp.concatenate(rests, 0), hot.astype(f8), dims, preferred_element_type=f32
        )
        out_ref[...] += total.reshape(freqs, 256, 256)
        return 0

    lax.fori_loop(0, groups, add_group, 0, unroll=8)
    out_ref[...] = out_ref[...] * (top * (1.0 / TOP)).reshape(1, 1, 1)
    for f in range(freqs):
        head = jnp.transpose(out_ref[f, :, :128])[:EDGE]
        tail = jnp.transpose(out_ref[f, :, 128:])[128 - EDGE :]
        put_edges(is_odd(odd_ref, 0), head, tail, first_ref, second_ref, f)


def block_and_edges(freqs):
    return (
        jax.ShapeDtypeStruct((freqs, 256, 256), f32),
        jax.ShapeDtypeStruct((freqs, EDGE, 256), f32),
        jax.ShapeDtypeStruct((freqs, EDGE, 256), f32),
    )


def scatter_density(odd, patch, area_rows, flux, first, freqs):
    return pl.pallas_call(
        functools.partial(scatter_kernel, first=first),
        out_shape=block_and_edges(freqs),
        in_specs=[VMEM] * 4,
        out_specs=(VMEM,) * 3,
        scratch_shapes=[pltpu.VMEM((128 // GROUP, 8, GROUP * 128), f32)],
        compiler_params=pltpu.CompilerParams(vmem_limit_bytes=36 << 20),
        cost_estimate=pl.CostEstimate(
            flops=2 * freqs * 65536 * 2 * 16384, bytes_accessed=2000000, transcendentals=0
        ),
        name="scatter_density",
    )(odd, patch, area_rows, flux)


def in_window(place):
    return jnp.where((place >= -HALF) & (place < HALF), 1.0, 0.0).astype(bf16)


def two_parts(cells):
    head = cells.astype(bf16)
    return head, (cells - head.astype(f32)).astype(bf16)


def column_kernel(odd_ref, block_ref, one_ref, two_ref, out_ref, first_ref, second_ref):
    inner = in_window(iota((256, 256), 0) - iota((256, 256), 1))
    place, column = iota((EDGE, 256), 0), iota((EDGE, 256), 1)
    outer = jnp.concatenate(
        [in_window(place - EDGE - column), in_window(place + 256 - column)], 0
    )
    inner = jnp.concatenate([inner, inner], 0)
    outer = jnp.concatenate([outer, outer], 0)
    for f in range(block_ref.shape[0]):
        total = jnp.dot(
            jnp.concatenate(two_parts(block_ref[f]), 1), inner, preferred_element_type=f32
        )
        edges = jnp.concatenate(got_edges(is_odd(odd_ref, 0), one_ref, two_ref, f), 0)
        total = total + lax.dot_general(
            jnp.concatenate(two_parts(edges), 0),
            outer,
            (((0,), (0,)), ((), ())),
            preferred_element_type=f32,
        )
        out_ref[f] = total
        put_edges(is_odd(odd_ref, 1), total[:EDGE], total[256 - EDGE :], first_ref, second_ref, f)


def column_sum(odd, block, first, second):
    return pl.pallas_call(
        column_kernel,
        out_shape=block_and_edges(block.shape[0]),
        in_specs=[VMEM] * 4,
        out_specs=(VMEM,) * 3,
        compiler_params=pltpu.CompilerParams(vmem_limit_bytes=16 << 20),
        name="column_sum",
    )(odd, block, first, second)


def row_kernel(odd_ref, *refs):
    refs, (out_hbm, out_ref, sems) = refs[:-3], refs[-3:]
    copies = []
    length = 256 + 2 * EDGE
    band = in_window(iota((256, length), 1) - EDGE - iota((256, length), 0))
    band = jnp.concatenate([band, band], 1)
    done = 0
    for block_ref, one_ref, two_ref in zip(refs[0::3], refs[1::3], refs[2::3]):
        for f in range(block_ref.shape[0]):
            before, after = got_edges(is_odd(odd_ref, 1), one_ref, two_ref, f)
            cells = jnp.concatenate([before, block_ref[f], after], 0)
            total = jnp.dot(
                band, jnp.concatenate(two_parts(cells), 0), preferred_element_type=f32
            )
            out_ref[done] = total * (1.0 / (4.0 * HALF * HALF))
            copy = pltpu.make_async_copy(out_ref.at[done], out_hbm.at[done], sems.at[done])
            copy.start()
            copies.append(copy)
            done += 1
    for copy in copies:
        copy.wait()


def row_sum(odd, *pieces):
    return pl.pallas_call(
        row_kernel,
        out_shape=jax.ShapeDtypeStruct((3, 256, 256), f32),
        in_specs=[VMEM] * (1 + len(pieces)),
        out_specs=pl.BlockSpec(memory_space=pl.ANY),
        scratch_shapes=[pltpu.VMEM((3, 256, 256), f32), pltpu.SemaphoreType.DMA((3,))],
        compiler_params=pltpu.CompilerParams(vmem_limit_bytes=16 << 20),
        name="row_sum",
    )(odd, *pieces)


def shards(
    e_field, h_field, j_field, material, material_table, dft_e, dft_h, skin_cell, counts,
    patch_slot, area,
):
    last_cols, last_rows = field_edges(h_field)
    cols_left = shifted(last_cols, "gx", 1)
    rows_below = shifted(last_rows, "gy", 1)
    odd = jnp.stack([lax.axis_index("gx") % 2, lax.axis_index("gy") % 2])
    odd = jnp.broadcast_to(odd[:, None], (2, 128))
    packed, offsets = pack_slots(counts, skin_cell)
    cols_left, rows_below, packed = lax.optimization_barrier((cols_left, rows_below, packed))
    e_next, j_next, dft_e_next, dft_h_next, rows = field_and_flux(
        offsets, packed, e_field, h_field, j_field, material, material_table, dft_e, dft_h,
        cols_left, rows_below,
    )
    rows, patch, area_here = lax.optimization_barrier((rows, patch_slot, area))
    arrived = lax.all_to_all(rows, ("gy", "gx"), split_axis=0, concat_axis=0, tiled=True)
    area_rows = gather_area(patch, area_here)

    blocks, swaps, pieces = [], [], []
    for first, freqs in PIECES:
        block, *edges = scatter_density(odd, patch, area_rows, arrived, first, freqs)
        blocks.append(block)
        swaps.append(exchange(*edges, "gx"))
    for block, swap in zip(blocks, swaps):
        strip, *edges = column_sum(odd, block, *swap)
        pieces += [strip, *exchange(*edges, "gy")]
    point_density = jnp.concatenate(blocks, 0)
    avg_density = row_sum(odd, *pieces)
    return (e_next, j_next, dft_e_next, dft_h_next, point_density, avg_density)


def solution(mesh):
    placed = (
        P(None, None, "gy", "gx"),
        P(None, None, "gy", "gx"),
        P(None, None, "gy", "gx"),
        P(None, "gy", "gx"),
        P(),
        P(None, None, None, None, "gy", "gx"),
        P(None, None, None, None, "gy", "gx"),
        P(("gy", "gx"), None, None),
        P(("gy", "gx"), None),
        P(("gy", "gx"), None, None),
        P(None, "gy", "gx"),
    )
    return jax.shard_map(
        shards,
        mesh=mesh,
        in_specs=placed,
        out_specs=(
            P(None, None, "gy", "gx"),
            P(None, None, "gy", "gx"),
            P(None, None, None, None, "gy", "gx"),
            P(None, None, None, None, "gy", "gx"),
            P(None, "gy", "gx"),
            P(None, "gy", "gx"),
        ),
        check_vma=False,
    )
```
